32 devices in a mesh: bucket: 4 (over y, core), dp: 8 (over z, x).
Axes of the slice: x: 2, y: 2, z: 4, core: 2. Of those that a mesh axis runs over, the one named last changes fastest.
Arguments:
- tokens: bfloat16 [32768, 768], P(('bucket', 'dp')), may hold values from -6 to 6
- segment: int32 [32768], P(('bucket', 'dp')), may hold values from 0 to 1023, as said below
- live: int32 [32768], P(('bucket', 'dp')), may hold values from 0 to 1, as said below
- group_patches: int32 [4], replicated, may hold values from 8192 to 65535
- qkv_weight: bfloat16 [768, 2304], replicated, may hold values from -0.21875 to 0.21875
- qkv_bias: float32 [2304], replicated, may hold values from -4 to 4
- out_weight: bfloat16 [768, 768], replicated, may hold values from -0.625 to 0.625
- out_bias: float32 [768], replicated, may hold values from -4 to 4
- fc1_weight: bfloat16 [768, 3072], replicated, may hold values from -0.21875 to 0.21875
- fc1_bias: float32 [3072], replicated, may hold values from -4 to 4
- fc2_weight: bfloat16 [3072, 768], replicated, may hold values from -0.109375 to 0.109375
- fc2_bias: float32 [768], replicated, may hold values from -4 to 4
- norm_gain: float32 [2, 768], replicated, may hold values from 0.1 to 1.9
- norm_shift: float32 [2, 768], replicated, may hold values from -4 to 4
- qk_gain: float32 [2, 64], replicated, may hold values from 0.1 to 1.9
- qk_shift: float32 [2, 64], replicated, may hold values from -4 to 4
- cotangent: bfloat16 [32768, 768], P(('bucket', 'dp')), may hold values from -6 to 6
Outputs:
- out: bfloat16 [32768, 768], P(('bucket', 'dp'))
- tokens_grad: float32 [32768, 768], P(('bucket', 'dp'))
- qkv_weight_grad: float32 [768, 2304], replicated
- qkv_bias_grad: float32 [2304], replicated
- out_weight_grad: float32 [768, 768], replicated
- out_bias_grad: float32 [768], replicated
- fc1_weight_grad: float32 [768, 3072], replicated
- fc1_bias_grad: float32 [3072], replicated
- fc2_weight_grad: float32 [3072, 768], replicated
- fc2_bias_grad: float32 [768], replicated
- norm_gain_grad: float32 [2, 768], replicated
- norm_shift_grad: float32 [2, 768], replicated
- qk_gain_grad: float32 [2, 64], replicated
- qk_shift_grad: float32 [2, 64], replicated
The draws below stay inside these ranges and needn't reach their ends.
Inputs may be any that keep to these rules, and one draw needn't show every extreme that they name: Each row's id is the index, within its device's 1024 rows, of the first row of its segment, so along a device the ids never fall and the first is 0. The rows hold whole sequences of 256 rows on devices in the first half of the bucket axis and of 1024 rows on the others; no segment spans two sequences. The rows with live 0 lie at the tail of their sequence, at most a quarter of it, and form one segment of their own; the last sequence of each device ends with exactly one such row. `live`: 0 only on the tail padding of a sequence.
All inputs are finite; a program needn't handle non-finite values.
Results may differ from the reference program's by a relative error of at most 0.013.
Values sent between devices are 32-bit elements; how exact they have to be, the bound alone decides.
A program may use at most 256 MiB of HBM per device.

```python
import jax
import jax.numpy as jnp
from jax import lax

D = 768
HEADS = 12
HD = 64
FF = 3072
SHORT = 256
LONG = 1024
TOK_DEV = 1024
GROUP_TOK = 8192
TOKENS = 32768
N_BUCKET = 4
N_DP = 8


def packing(key):
    key = jax.random.fold_in(key, 7)
    first_key, second_key, third_key = jax.random.split(key, 3)
    position = jnp.arange(TOKENS, dtype=jnp.int32)
    device = position // TOK_DEV
    device_row = position % TOK_DEV
    group = device // N_DP
    length = jnp.where(group < N_BUCKET // 2, SHORT, LONG).astype(jnp.int32)
    offset = position % length
    sequence_slot = (position - offset) // SHORT
    slot_count = TOKENS // SHORT
    last_sequence = (position - offset + length) % TOK_DEV == 0
    shift_bits = jax.random.randint(first_key, (slot_count,), 4, 10, dtype=jnp.int32)[sequence_slot]
    drawn_pad = jax.random.randint(second_key, (slot_count,), 0, 1 << 20, dtype=jnp.int32)[sequence_slot] % (length // 4 + 1)
    padding = jnp.where(last_sequence, 1, drawn_pad).astype(jnp.int32)
    random_bits = jax.random.randint(third_key, (TOKENS,), 0, 1 << 20, dtype=jnp.int32)
    cut_here = random_bits & jnp.left_shift(jnp.int32(1), shift_bits) - 1 == 0
    alive = offset < length - padding
    starts = (offset == 0) | (offset == length - padding) | cut_here & alive
    marks = jnp.where(starts, device_row, 0).astype(jnp.int32).reshape(TOKENS // TOK_DEV, TOK_DEV)
    ids = lax.cummax(marks, axis=1).reshape(TOKENS)
    return (ids.astype(jnp.int32), alive.astype(jnp.int32))


def draw_segment(key, part):
    return packing(key)[0]


def draw_live(key, part):
    return packing(key)[1]


def place_ends(values, key, low, high):
    longest = values.shape.index(max(values.shape))
    spots = []
    for shift in (0, 1):
        where = [jax.random.randint(jax.random.fold_in(key, axis), (), 0, length) for axis, length in enumerate(values.shape)]
        where[longest] = (where[longest] + shift) % values.shape[longest]
        spots.append(tuple(where))
    return values.at[spots[0]].set(low).at[spots[1]].set(high)


def levels(stream_key, extent, pieces, smallest, high):
    gain, own = 1.0, jax.random.fold_in(stream_key, 6)
    for dim, blocks in pieces:
        heights = jnp.exp(jax.random.uniform(jax.random.fold_in(own, dim), (blocks,), jnp.float32, smallest / len(pieces), high / len(pieces)))
        gain = gain * jnp.repeat(heights, extent[dim] // blocks).reshape([-1 if axis == dim else 1 for axis in range(len(extent))])
    return gain


def noise(stream_key, shape, scale, limit, shards=(), held_as=jnp.bfloat16):
    loudness = levels(stream_key, shape, shards, -0.22, 0.18) if shards else 1.0
    entries = jax.random.normal(stream_key, shape, jnp.float32) * scale * loudness
    return jnp.minimum(jnp.maximum(entries, -limit), limit).astype(held_as)


def setup_inputs(seed: int = 0) -> dict:
    seeds = jax.random.split(jax.random.key(seed), 18)
    tokens = noise(seeds[0], (TOKENS, D), 1.0, 6.0, ((0, 32),))
    segment = draw_segment(jax.random.fold_in(seeds[17], 71), 0)
    live = draw_live(jax.random.fold_in(seeds[17], 71), 0)
    group_patches = place_ends(jax.random.randint(seeds[3], (N_BUCKET,), 8192, 65536), jax.random.fold_in(seeds[3], 1), 8192, 65535).astype(jnp.int32)
    qkv_weight = noise(seeds[4], (D, 3 * D), D ** -0.5, 0.21875)
    qkv_bias = noise(seeds[5], (3 * D,), 0.3, 4.0, (), jnp.float32)
    out_weight = noise(seeds[6], (D, D), (D // 8) ** -0.5, 0.625)
    out_bias = noise(seeds[7], (D,), 0.3, 4.0, (), jnp.float32)
    fc1_weight = noise(seeds[8], (D, FF), D ** -0.5, 0.21875)
    fc1_bias = noise(seeds[9], (FF,), 0.3, 4.0, (), jnp.float32)
    fc2_weight = noise(seeds[10], (FF, D), FF ** -0.5, 0.109375)
    fc2_bias = noise(seeds[11], (D,), 0.3, 4.0, (), jnp.float32)
    norm_gain = jnp.clip(1.0 + 0.18 * jax.random.normal(seeds[12], (2, D), jnp.float32), 0.1, 1.9)
    norm_shift = noise(seeds[13], (2, D), 0.3, 4.0, (), jnp.float32)
    qk_gain = jnp.clip(1.0 + 0.18 * jax.random.normal(seeds[14], (2, HD), jnp.float32), 0.1, 1.9)
    qk_shift = noise(seeds[15], (2, HD), 0.3, 4.0, (), jnp.float32)
    cotangent = noise(seeds[16], (TOKENS, D), 1.0, 6.0, ((0, 32),))
    return dict(tokens=tokens, segment=segment, live=live, group_patches=group_patches, qkv_weight=qkv_weight, qkv_bias=qkv_bias, out_weight=out_weight, out_bias=out_bias, fc1_weight=fc1_weight, fc1_bias=fc1_bias, fc2_weight=fc2_weight, fc2_bias=fc2_bias, norm_gain=norm_gain, norm_shift=norm_shift, qk_gain=qk_gain, qk_shift=qk_shift, cotangent=cotangent)


@jax.custom_vjp
def low(v):
    return lax.optimization_barrier(v.astype(jnp.bfloat16)).astype(jnp.float32)

@jax.custom_vjp
def low_back(v):
    return v

def low_keep(v):
    return (low(v), None)

def low_pass(kept, grad):
    return (grad,)

def back_keep(v):
    return (v, None)

def back_low(kept, grad):
    return (low(grad),)
low.defvjp(low_keep, low_pass)
low_back.defvjp(back_keep, back_low)
EPSILON = 1e-06
HIGHEST = lax.Precision.HIGHEST

def matmul(left, right):
    return jnp.dot(left, right, precision=HIGHEST, preferred_element_type=jnp.float32)

def layer_norm(values, gains, shifts):
    center = values - lax.optimization_barrier(jnp.mean(values, axis=-1, keepdims=True))
    spread = lax.optimization_barrier(jnp.mean(center * center, axis=-1, keepdims=True))
    return center * lax.rsqrt(spread + EPSILON) * gains + shifts

def window(params, inputs, seg_ids, live_ids):
    qkv_w, qkv_b, out_w, out_b, fc1_w, fc1_b, fc2_w, fc2_b, n_gain, n_shift, q_gain, q_shift = params
    row_count = inputs.shape[0]
    a_low = low(layer_norm(inputs, n_gain[0], n_shift[0]))
    qkv = low_back(matmul(a_low, qkv_w) + qkv_b)
    queries = qkv[:, :D].reshape(row_count, HEADS, HD)
    keys_raw = qkv[:, D:2 * D].reshape(row_count, HEADS, HD)
    values_raw = qkv[:, 2 * D:].reshape(row_count, HEADS, HD)
    q_low = low(layer_norm(queries, q_gain[0], q_shift[0]) / jnp.sqrt(jnp.float32(HD)))
    k_low = low(layer_norm(keys_raw, q_gain[1], q_shift[1]))
    v_low = low(values_raw)
    scores = low_back(jnp.einsum('ihd,jhd->hij', q_low, k_low, precision=HIGHEST))
    same_seg = seg_ids[:, None] == seg_ids[None, :]
    scores = jnp.where(same_seg[None], scores, -1e+30)
    p_low = low(jax.nn.softmax(scores, axis=-1))
    attention = jnp.einsum('hij,jhd->ihd', p_low, v_low, precision=HIGHEST).reshape(row_count, D)
    attn_low = low(low_back(attention))
    hidden = inputs + low_back(matmul(attn_low, out_w) + out_b)
    c_low = low(layer_norm(hidden, n_gain[1], n_shift[1]))
    preact = low_back(matmul(c_low, fc1_w) + fc1_b)
    g_low = low(jax.nn.gelu(preact, approximate=False))
    mlp_out = low_back(matmul(g_low, fc2_w) + fc2_b)
    return live_ids[:, None].astype(jnp.float32) * (hidden + mlp_out)

def group_forward(params, inputs, seg_ids, live_ids):
    blocked = jax.checkpoint(window)
    return lax.map(lambda item: blocked(params, item[0], item[1], item[2]), (inputs, seg_ids, live_ids))

def reference(tokens, segment, live, group_patches, qkv_weight, qkv_bias, out_weight, out_bias, fc1_weight, fc1_bias, fc2_weight, fc2_bias, norm_gain, norm_shift, qk_gain, qk_shift, cotangent):
    params = tuple((item.astype(jnp.float32) for item in (qkv_weight, qkv_bias, out_weight, out_bias, fc1_weight, fc1_bias, fc2_weight, fc2_bias, norm_gain, norm_shift, qk_gain, qk_shift)))
    windows = GROUP_TOK // LONG
    inputs = tokens.astype(jnp.float32).reshape(N_BUCKET, windows, LONG, D)
    seg_ids = segment.reshape(N_BUCKET, windows, LONG)
    live_ids = live.reshape(N_BUCKET, windows, LONG)
    cot_all = cotangent.astype(jnp.float32).reshape(N_BUCKET, windows, LONG, D)
    counts = group_patches.astype(jnp.float32)
    rates = counts / (jnp.sum(counts) * jnp.sqrt(jnp.float32(GROUP_TOK)))
    totals = jax.tree.map(jnp.zeros_like, params)
    outputs = []
    grads_in = []
    for group in range(N_BUCKET):

        def forward(prm, values, group=group):
            return group_forward(prm, values, seg_ids[group], live_ids[group])
        result, pull = jax.vjp(forward, params, inputs[group])
        grad_params, grad_inputs = pull(cot_all[group])
        totals = jax.tree.map(lambda acc, term, group=group: acc + rates[group] * term, totals, grad_params)
        outputs.append(result.reshape(GROUP_TOK, D))
        grads_in.append(grad_inputs.reshape(GROUP_TOK, D))
    out = jnp.concatenate(outputs, axis=0).astype(jnp.bfloat16)
    tokens_grad = jnp.concatenate(grads_in, axis=0)
    return (out, tokens_grad, totals[0], totals[1], totals[2], totals[3], totals[4], totals[5], totals[6], totals[7], totals[8], totals[9], totals[10], totals[11])
```

```python
import functools
import heapq
import math

import jax
import jax.numpy as jnp
from jax import lax
from jax.experimental import pallas as pl
from jax.experimental.pallas import tpu as pltpu
from jax.sharding import PartitionSpec as P

MESH = pl.DeviceIdType.MESH

HEADS = 12
HD = 64
LONG = 1024


EPSILON = 1e-06
MASKED = -1e30


def halve(shape):
    rows, cols = shape
    if rows % 16 == 0: return 0
    if cols % 256 == 0: return 1
    return None

def level_orders(nb, nd):
    bk=[("bucket",i) for i in range(int(math.log2(nb)))]
    dp=[("dp",i) for i in range(int(math.log2(nd)))]
    rest_b=bk[1:]
    a=bk[:1]+dp[:2]+rest_b+dp[2:]
    b=bk[:1]+rest_b+dp[1:2]+dp[:1]+dp[2:]
    return a,b

def rate(bit):
    if bit==("bucket",0): return 600e3
    if bit==("dp",2): return 23e3
    return 46e3
def resource(bit):
    if bit==("dp",2): return ("dp",1)
    return bit

class Job: pass

def make_jobs(chunks, nb, nd):
    orders=level_orders(nb,nd)
    jobs=[]
    for ci,(g,r0,rows,cols,ready) in enumerate(chunks):
        for p in range(2):
            if rows%16:
                if p==1: continue
                base,n=r0,rows
            else:
                n=rows//2; base=r0+p*n
            j=Job(); j.g=g; j.base=base; j.shape=(n,cols); j.ready=ready; j.levels=[]
            sh=(n,cols)
            for bit in orders[p]:
                d=halve(sh)
                out=list(sh)
                if d is not None: out[d]//=2
                j.levels.append((bit,d,tuple(sh),tuple(out)))
                sh=tuple(out)
            jobs.append(j)
    return jobs

def simulate(jobs):
    free={}
    ev=[]
    heap=[(j.ready,k,0) for k,j in enumerate(jobs)]
    heapq.heapify(heap)
    order=[]
    while heap:
        t,k,s=heapq.heappop(heap)
        j=jobs[k]; L=len(j.levels)
        lv = s if s<L else 2*L-1-s
        bit,d,before,after=j.levels[lv]
        moved=after if (s<L or d is not None) else None
        size=4*after[0]*after[1] if moved else 0
        if size==0:
            end=t
        else:
            r=resource(bit)
            start=max(t,free.get(r,0.0))
            end=start+size/rate(bit)
            free[r]=end
            end+=2.0
        order.append((end,t,k,s))
        if s+1<2*L: heapq.heappush(heap,(end,k,s+1))
    order.sort()
    return [(k,s) for _,_,k,s in order], max(o[0] for o in order), order

def bit_of(bit):
    axis,i=bit
    return (lax.axis_index(axis)//(1<<i))%2

def partner(bit, names=("bucket","dp")):
    axis,i=bit
    me=lax.axis_index(axis)
    other=me+(1-2*bit_of(bit))*(1<<i)
    return tuple(other if n==axis else lax.axis_index(n) for n in names)

def region(ref, off, shape):
    r,c=off
    if isinstance(c,int) and c==0 and ref.shape[1]==shape[1]:
        return ref.at[pl.ds(r if isinstance(r,int) else pl.multiple_of(r,8),shape[0]),:]
    return ref.at[pl.ds(r if isinstance(r,int) else pl.multiple_of(r,8),shape[0]),pl.ds(c if isinstance(c,int) else pl.multiple_of(c,128),shape[1])]

def add_into(acc, off, recv, shape):
    rows,cols=shape
    rb=8
    while rows%(rb*2)==0 and rb*2*cols<=32*1024: rb*=2
    r,c=off
    def one(i,_):
        a=acc.at[pl.ds(pl.multiple_of(r+i*rb,8),rb), pl.ds(c if isinstance(c,int) else pl.multiple_of(c,128),cols)]
        a[...]=a[...]+recv[pl.ds(pl.multiple_of(i*rb,8),rb),:]
        return 0
    lax.fori_loop(0,rows//rb,one,0)

class Run:
    def __init__(self, j, src, out, acc, recv, ss, rs, ls):
        self.j=j; self.src=src; self.out=out; self.acc=acc; self.recv=recv
        self.ss=ss; self.rs=rs; self.ls=ls
        self.off=(0,0)
        self.sends=[]
        self.cp=None
        self.loc=None
        bit,d,before,after=j.levels[0]
        self.ob=j.base
        self.gofs=(j.base,0)
    def split(self, lv, off):
        bit,d,before,after=self.j.levels[lv]
        b=bit_of(bit)
        keep=list(off); send=list(off)
        keep[d]=off[d]+b*after[d]; send[d]=off[d]+(1-b)*after[d]
        return tuple(keep),tuple(send)
    def start(self, s):
        L=len(self.j.levels)
        if s<L:
            bit,d,before,after=self.j.levels[s]
            if s==0:
                assert d is not None
                keep,send=self.split(0,(self.j.base,0))
                self.gofs=keep
                src=region(self.src,send,after)
                self.loc=pltpu.make_async_copy(region(self.src,keep,after),self.acc,self.ls.at[0])
                self.loc.start()
                self.off=(0,0)
            elif d is None:
                src=region(self.acc,self.off,after)
            else:
                keep,send=self.split(s,self.off)
                src=region(self.acc,send,after)
                self.off=keep
            cp=pltpu.make_async_remote_copy(src_ref=src,dst_ref=self.recv[s],send_sem=self.ss.at[s],recv_sem=self.rs.at[s],device_id=partner(bit),device_id_type=MESH)
            cp.start()
            self.cp=cp
            if d is not None: self.sends.append(cp)
        else:
            lv=2*L-1-s
            bit,d,before,after=self.j.levels[lv]
            if s==L:
                g=self.g()
                self.piece=(g,after)
                self.loc=pltpu.make_async_copy(region(self.acc,self.off,after),region(self.out,g,after),self.ls.at[1])
                self.loc.start()
                self.first=True
            if d is None:
                self.cp=None
                return
            g,shape=self.piece
            assert shape==after,(shape,after)
            if self.first:
                src=region(self.acc,self.off,after)
                self.first=False
            else:
                if self.loc is not None:
                    self.loc.wait(); self.loc=None
                src=region(self.out,g,after)
            cp=pltpu.make_async_remote_copy(src_ref=src,dst_ref=region(self.out,g,after),send_sem=self.ss.at[s],recv_sem=self.rs.at[s],device_id=partner(bit),device_id_type=MESH)
            cp.start(); self.cp=cp; self.sends.append(cp)
    def g(self):
        return (self.gofs[0]+self.off[0], self.gofs[1]+self.off[1])
    def finish(self, s):
        L=len(self.j.levels)
        if s<L:
            bit,d,before,after=self.j.levels[s]
            if s==0:
                self.loc.wait(); self.loc=None
            if d is None: self.cp.wait()
            else: self.cp.wait_recv()
            add_into(self.acc,self.off,self.recv[s],after)
        else:
            lv=2*L-1-s
            bit,d,before,after=self.j.levels[lv]
            if self.cp is not None:
                self.cp.wait_recv()
            if d is not None:
                g,_=self.piece
                up=list(g); up[d]=g[d]-bit_of(bit)*after[d]
                self.piece=(tuple(up),before)
    def close(self):
        if self.loc is not None: self.loc.wait()
        for cp in self.sends: cp.wait_send()

def barrier(bits):
    sem=pltpu.get_barrier_semaphore()
    for bit in bits:
        pl.semaphore_signal(sem,inc=1,device_id=partner(bit),device_id_type=MESH)
    pl.semaphore_wait(sem,len(bits))

def scratch_of(jobs):
    out=[]
    for j in jobs:
        out.append(pltpu.VMEM(j.levels[0][3],jnp.float32))
        for bit,d,before,after in j.levels: out.append(pltpu.VMEM(after,jnp.float32))
        L=len(j.levels)
        out += [pltpu.SemaphoreType.DMA((2*L,)),pltpu.SemaphoreType.DMA((2*L,)),pltpu.SemaphoreType.DMA((2,))]
    return out

def ar_body(jobs, order, nin, bits, *refs):
    ins=refs[:nin]; outs=refs[nin:2*nin]; sc=list(refs[2*nin:])
    runs=[]
    for j in jobs:
        acc=sc.pop(0); recv=[sc.pop(0) for _ in j.levels]; ss,rs,ls=sc.pop(0),sc.pop(0),sc.pop(0)
        runs.append(Run(j,ins[j.g],outs[j.g],acc,recv,ss,rs,ls))
    barrier(bits)
    for r in runs: r.start(0)
    for k,s in order:
        runs[k].finish(s)
        if s+1<2*len(jobs[k].levels): runs[k].start(s+1)
    for r in runs: r.close()

def all_reduce(grads, chunks, nb, nd, cid=7):
    jobs=make_jobs(chunks,nb,nd)
    order,_,_=simulate(jobs)
    bits=level_orders(nb,nd)[0]
    n=len(grads)
    return pl.pallas_call(functools.partial(ar_body,jobs,order,n,bits),
        out_shape=tuple(jax.ShapeDtypeStruct(g.shape,jnp.float32) for g in grads),
        in_specs=[pl.BlockSpec(memory_space=pltpu.HBM)]*n,
        out_specs=tuple([pl.BlockSpec(memory_space=pltpu.HBM)]*n),
        scratch_shapes=scratch_of(jobs),
        compiler_params=pltpu.CompilerParams(collective_id=cid,has_side_effects=True,vmem_limit_bytes=60<<20),name="allreduce")(*grads)


def norm_forward(values, gains, shifts):
    center = values - jnp.mean(values, axis=-1, keepdims=True)
    inverse = lax.rsqrt(jnp.mean(center * center, axis=-1, keepdims=True) + EPSILON)
    unit_vals = center * inverse
    return (unit_vals * gains + shifts, unit_vals, inverse)


def norm_backward(grads, unit_vals, inverse, gains):
    scaled = grads * gains
    inner = (
        scaled
        - jnp.mean(scaled, axis=-1, keepdims=True)
        - unit_vals * jnp.mean(scaled * unit_vals, axis=-1, keepdims=True)
    )
    return inverse * inner


def attend_forward(query_rows, query_segs, key_rows, value_rows, key_segs):
    scores = jnp.einsum("ihd,jhd->hij", query_rows, key_rows, preferred_element_type=jnp.float32)
    same_seg = query_segs[:, None] == key_segs[None, :]
    scores = jnp.where(same_seg[None], scores, MASKED)
    row_max = jnp.max(scores, axis=-1, keepdims=True)
    log_total = row_max + jnp.log(jnp.sum(jnp.exp(scores - row_max), axis=-1, keepdims=True))
    probs_low = jnp.exp(scores - log_total).astype(jnp.bfloat16)
    attention = jnp.einsum(
        "hij,jhd->ihd", probs_low, value_rows, preferred_element_type=jnp.float32
    )
    return (attention, log_total)


def attend_backward(query_rows, query_segs, key_rows, value_rows, key_segs, log_total, out_grad):
    scores = jnp.einsum("ihd,jhd->hij", query_rows, key_rows, preferred_element_type=jnp.float32)
    same_seg = query_segs[:, None] == key_segs[None, :]
    probs = jnp.where(same_seg[None], jnp.exp(scores - log_total), 0.0)
    probs_low = probs.astype(jnp.bfloat16)
    value_part = jnp.einsum("hij,ihd->jhd", probs_low, out_grad, preferred_element_type=jnp.float32)
    prob_grad = jnp.einsum("ihd,jhd->hij", out_grad, value_rows, preferred_element_type=jnp.float32)
    delta_sum = jnp.sum(probs * prob_grad, axis=-1, keepdims=True)
    score_low = (probs * (prob_grad - delta_sum)).astype(jnp.bfloat16)
    query_part = jnp.einsum("hij,jhd->ihd", score_low, key_rows, preferred_element_type=jnp.float32)
    key_part = jnp.einsum("hij,ihd->jhd", score_low, query_rows, preferred_element_type=jnp.float32)
    return (query_part, key_part, value_part)


def add_rows(total, part):
    return total + part


def body(
    tokens,
    segment,
    live,
    group_patches,
    qkv_weight,
    qkv_bias,
    out_weight,
    out_bias,
    fc1_weight,
    fc1_bias,
    fc2_weight,
    fc2_bias,
    norm_gain,
    norm_shift,
    qk_gain,
    qk_shift,
    cotangent,
):
    row_count, features = tokens.shape
    query_block = min(512, LONG)
    block_count = row_count // query_block
    root_head = math.sqrt(HD)
    inputs = tokens.astype(jnp.float32)
    a_val, a_unit, a_inverse = norm_forward(inputs, norm_gain[0], norm_shift[0])
    a_low = a_val.astype(jnp.bfloat16)
    qkv = jnp.dot(a_low, qkv_weight, preferred_element_type=jnp.float32) + qkv_bias
    query_raw = qkv[:, :features].reshape(row_count, HEADS, HD)
    key_raw = qkv[:, features : 2 * features].reshape(row_count, HEADS, HD)
    value_raw = qkv[:, 2 * features :].reshape(row_count, HEADS, HD)
    query_norm, query_unit, query_inverse = norm_forward(query_raw, qk_gain[0], qk_shift[0])
    key_norm, key_unit, key_inverse = norm_forward(key_raw, qk_gain[1], qk_shift[1])
    query_low = (query_norm / root_head).astype(jnp.bfloat16)
    key_low = key_norm.astype(jnp.bfloat16)
    value_low = value_raw.astype(jnp.bfloat16)

    def forward_block(number):
        begin_row = number * query_block
        query_rows = lax.dynamic_slice_in_dim(query_low, begin_row, query_block, 0)
        query_segs = lax.dynamic_slice_in_dim(segment, begin_row, query_block, 0)
        return attend_forward(query_rows, query_segs, key_low, value_low, segment)

    attn_blocks, total_blocks = lax.map(forward_block, jnp.arange(block_count, dtype=jnp.int32))
    attn_low = attn_blocks.reshape(row_count, features).astype(jnp.bfloat16)
    hidden = inputs + jnp.dot(attn_low, out_weight, preferred_element_type=jnp.float32) + out_bias
    c_val, c_unit, c_inverse = norm_forward(hidden, norm_gain[1], norm_shift[1])
    c_low = c_val.astype(jnp.bfloat16)
    preact = jnp.dot(c_low, fc1_weight, preferred_element_type=jnp.float32) + fc1_bias
    g_low = jax.nn.gelu(preact, approximate=False).astype(jnp.bfloat16)
    mlp_out = jnp.dot(g_low, fc2_weight, preferred_element_type=jnp.float32) + fc2_bias
    live_rows = live.astype(jnp.float32)[:, None]
    out = (live_rows * (hidden + mlp_out)).astype(jnp.bfloat16)
    mlp_grad = cotangent.astype(jnp.float32) * live_rows
    mlp_low = mlp_grad.astype(jnp.bfloat16)
    fc2_w_term = jnp.einsum("tf,td->fd", g_low, mlp_low, preferred_element_type=jnp.float32)
    fc2_b_term = jnp.sum(mlp_grad, axis=0)
    gelu_grad = jnp.einsum("td,fd->tf", mlp_low, fc2_weight, preferred_element_type=jnp.float32)
    slope = 0.5 * (1.0 + jax.scipy.special.erf(preact / math.sqrt(2.0))) + preact * jnp.exp(
        -0.5 * preact * preact
    ) / math.sqrt(2.0 * math.pi)
    pre_low = (gelu_grad * slope).astype(jnp.bfloat16)
    fc1_w_term = jnp.einsum("td,tf->df", c_low, pre_low, preferred_element_type=jnp.float32)
    fc1_b_term = jnp.sum(pre_low.astype(jnp.float32), axis=0)
    norm_in_grad = jnp.einsum("tf,df->td", pre_low, fc1_weight, preferred_element_type=jnp.float32)
    gain_second = jnp.sum(norm_in_grad * c_unit, axis=0)
    shift_second = jnp.sum(norm_in_grad, axis=0)
    hidden_grad = mlp_grad + norm_backward(norm_in_grad, c_unit, c_inverse, norm_gain[1])
    branch_low = hidden_grad.astype(jnp.bfloat16)
    out_w_term = jnp.einsum("td,te->de", attn_low, branch_low, preferred_element_type=jnp.float32)
    out_b_term = jnp.sum(branch_low.astype(jnp.float32), axis=0)
    attn_grad_low = jnp.einsum(
        "te,de->td", branch_low, out_weight, preferred_element_type=jnp.float32
    ).astype(jnp.bfloat16)
    attn_grad_heads = attn_grad_low.reshape(row_count, HEADS, HD)

    def backward_block(sums, item):
        number, log_total = item
        begin_row = number * query_block
        query_rows = lax.dynamic_slice_in_dim(query_low, begin_row, query_block, 0)
        query_segs = lax.dynamic_slice_in_dim(segment, begin_row, query_block, 0)
        out_grad = lax.dynamic_slice_in_dim(attn_grad_heads, begin_row, query_block, 0)
        query_part, key_part, value_part = attend_backward(
            query_rows, query_segs, key_low, value_low, segment, log_total, out_grad
        )
        return ((add_rows(sums[0], key_part), add_rows(sums[1], value_part)), query_part)

    empty_heads = jnp.zeros((row_count, HEADS, HD), jnp.float32)
    (key_grad, value_grad), query_blocks = lax.scan(
        backward_block,
        (empty_heads, empty_heads),
        (jnp.arange(block_count, dtype=jnp.int32), total_blocks),
    )
    query_grad = query_blocks.reshape(row_count, HEADS, HD) / root_head
    qgain_term = jnp.sum(query_grad * query_unit, axis=(0, 1))
    kgain_term = jnp.sum(key_grad * key_unit, axis=(0, 1))
    qshift_term = jnp.sum(query_grad, axis=(0, 1))
    kshift_term = jnp.sum(key_grad, axis=(0, 1))
    query_in = norm_backward(query_grad, query_unit, query_inverse, qk_gain[0]).reshape(
        row_count, features
    )
    key_in = norm_backward(key_grad, key_unit, key_inverse, qk_gain[1]).reshape(row_count, features)
    qkv_grad_low = jnp.concatenate(
        [query_in, key_in, value_grad.reshape(row_count, features)], axis=1
    ).astype(jnp.bfloat16)
    qkv_w_term = jnp.einsum("td,te->de", a_low, qkv_grad_low, preferred_element_type=jnp.float32)
    qkv_b_term = jnp.sum(qkv_grad_low.astype(jnp.float32), axis=0)
    first_grad = jnp.einsum(
        "te,de->td", qkv_grad_low, qkv_weight, preferred_element_type=jnp.float32
    )
    gain_first = jnp.sum(first_grad * a_unit, axis=0)
    shift_first = jnp.sum(first_grad, axis=0)
    tokens_grad = hidden_grad + norm_backward(first_grad, a_unit, a_inverse, norm_gain[0])
    small_terms = jnp.concatenate(
        [
            qkv_b_term,
            out_b_term,
            fc1_b_term,
            fc2_b_term,
            gain_first,
            gain_second,
            shift_first,
            shift_second,
            qgain_term,
            kgain_term,
            qshift_term,
            kshift_term,
        ]
    )
    counts = group_patches.astype(jnp.float32)
    own_count = jnp.sum(
        jnp.where(jnp.arange(counts.shape[0]) == lax.axis_index("bucket"), counts, 0.0)
    )
    weighting = own_count / (jnp.sum(counts) * math.sqrt(row_count * lax.axis_size("dp")))
    small_rows = small_terms.size // 128
    small_pad = jnp.pad(small_terms.reshape(small_rows, 128), ((0, 128 - small_rows), (0, 0)))
    terms = [
        weighting * fc2_w_term,
        weighting * fc1_w_term,
        weighting * out_w_term,
        weighting * qkv_w_term,
        weighting * small_pad,
    ]
    wide = features // 4
    chunks = [(0, 4 * wide * i, 4 * wide, features, 0.0) for i in range(4)]
    chunks += [(1, wide * i, wide, 4 * features, 0.0) for i in range(4)]
    chunks += [(2, 0, features, features, 0.0)]
    chunks += [(3, 2 * wide * i, 2 * wide, 3 * features, 0.0) for i in range(2)]
    chunks += [(4, 0, 128, 128, 0.0)]
    finished = all_reduce(terms, chunks, lax.axis_size("bucket"), lax.axis_size("dp"))
    hidden_units = fc1_weight.shape[1]
    small_done = finished[4][:small_rows].reshape(-1)
    offset_one = 3 * features
    offset_two = offset_one + features
    offset_three = offset_two + hidden_units
    offset_four = offset_three + features
    offset_five = offset_four + 2 * features
    offset_six = offset_five + 2 * features
    offset_seven = offset_six + 2 * HD
    return (
        out,
        tokens_grad,
        finished[3],
        small_done[:offset_one],
        finished[2],
        small_done[offset_one:offset_two],
        finished[1],
        small_done[offset_two:offset_three],
        finished[0],
        small_done[offset_three:offset_four],
        small_done[offset_four:offset_five].reshape(2, features),
        small_done[offset_five:offset_six].reshape(2, features),
        small_done[offset_six:offset_seven].reshape(2, HD),
        small_done[offset_seven:].reshape(2, HD),
    )


def solution(mesh):
    return jax.shard_map(
        body,
        mesh=mesh,
        in_specs=(
            P(("bucket", "dp"), None),
            P(("bucket", "dp")),
            P(("bucket", "dp")),
            P(),
            P(),
            P(),
            P(),
            P(),
            P(),
            P(),
            P(),
            P(),
            P(),
            P(),
            P(),
            P(),
            P(("bucket", "dp"), None),
        ),
        out_specs=(
            P(("bucket", "dp"), None),
            P(("bucket", "dp"), None),
            P(),
            P(),
            P(),
            P(),
            P(),
            P(),
            P(),
            P(),
            P(),
            P(),
            P(),
            P(),
        ),
        check_vma=False,
    )
```

```python
import functools
import heapq
import math

import jax
import jax.numpy as jnp
from jax import lax
from jax.experimental import pallas as pl
from jax.experimental.pallas import tpu as pltpu
from jax.sharding import PartitionSpec as P

MESH = pl.DeviceIdType.MESH
F32=jnp.float32; BF=jnp.bfloat16
EPSILON=1e-6
NEG=-1e30
HD=64
VM=58<<20

def mm(a,b,ca=1,cb=0):
    return lax.dot_general(a,b,(((ca,),(cb,)),((),())),preferred_element_type=F32)

def row_norm(x):
    c=x-jnp.mean(x,axis=-1,keepdims=True)
    r=lax.rsqrt(jnp.mean(c*c,axis=-1,keepdims=True)+EPSILON)
    return c*r,r

def head_avg(x,m,twice):
    out=[]
    for i in range(x.shape[1]//256):
        part=x[:,256*i:256*(i+1)]
        hi=part.astype(BF)
        s=mm(hi,m)
        if twice: s=s+mm((part-hi.astype(F32)).astype(BF),m)
        out.append(s)
    return jnp.concatenate(out,axis=1)

def avg_matrix():
    i=lax.broadcasted_iota(jnp.int32,(256,256),0)//HD
    j=lax.broadcasted_iota(jnp.int32,(256,256),1)//HD
    return jnp.where(i==j,1.0/HD,0.0).astype(BF)

def whole(a):
    nd=len(a.shape)
    return pl.BlockSpec(a.shape,lambda *_:(0,)*nd,pipeline_mode=pl.Buffered(1))

def qkv_kernel(x,w,b,ng,ns,qg,qs,a_o,q_o,k_o,v_o,qu_o,ku_o,qr_o,kr_o):
    d=x.shape[1]
    u,_=row_norm(x[...].astype(F32))
    a=(u*ng[0:1,:]+ns[0:1,:]).astype(BF)
    a_o[...]=a
    m=avg_matrix()
    for i,(lo,un,rr) in enumerate(((q_o,qu_o,qr_o),(k_o,ku_o,kr_o))):
        raw=mm(a,w[:,i*d:(i+1)*d])+b[:,i*d:(i+1)*d]
        c=raw-head_avg(raw,m,True)
        r=lax.rsqrt(head_avg(c*c,m,False)+EPSILON)
        unit=c*r
        un[...]=unit.astype(BF)
        rr[...]=r
        n=unit*qg[i:i+1,:]+qs[i:i+1,:]
        if i==0: n=n*(1.0/math.sqrt(HD))
        lo[...]=n.astype(BF)
    v_o[...]=(mm(a,w[:,2*d:])+b[:,2*d:]).astype(BF)

def qkv_forward(x,w,b,ng,ns,qg,qs,rb=256):
    t,d=x.shape
    rows=pl.BlockSpec((rb,d),lambda i:(i,0))
    sh=lambda dt: jax.ShapeDtypeStruct((t,d),dt)
    return pl.pallas_call(qkv_kernel,grid=(t//rb,),
        in_specs=[rows,whole(w),whole(b),whole(ng),whole(ns),whole(qg),whole(qs)],
        out_specs=[rows]*8,
        out_shape=[sh(BF)]*6+[sh(F32)]*2,
        compiler_params=pltpu.CompilerParams(vmem_limit_bytes=VM),name="norm_qkv")(x,w,b,ng,ns,qg,qs)

def attend_kernel(q,k,v,sr,sc,o,lse,ob=256):
    t=q.shape[0]
    vt=v[...].T
    kk=k[...]
    lane=lax.broadcasted_iota(jnp.int32,(1,2*HD),1)//HD
    for i in range(t//ob):
        same=sc[...]==sr[:,i*ob:(i+1)*ob]
        parts=[]
        for h in range(2):
            qm=jnp.where(lane==h,q[i*ob:(i+1)*ob,:],0)
            s=jnp.where(same,mm(kk,qm,1,1),NEG)
            m=jnp.max(s,axis=0,keepdims=True)
            p=jnp.exp(s-m)
            l=jnp.sum(p,axis=0,keepdims=True)
            lse[0,h:h+1,i*ob:(i+1)*ob]=m+jnp.log(l)
            acc=mm(vt[h*HD:(h+1)*HD,:],p.astype(BF))
            parts.append(acc*(1.0/l))
        o[i*ob:(i+1)*ob,:]=jnp.concatenate(parts,axis=0).T.astype(BF)

def attend_forward(q,k,v,sr,sc):
    t,d=q.shape
    hp=d//(2*HD)
    col=pl.BlockSpec((t,2*HD),lambda h:(0,h))
    return pl.pallas_call(attend_kernel,grid=(hp,),
        in_specs=[col,col,col,whole(sr),whole(sc)],
        out_specs=[col,pl.BlockSpec((1,2,t),lambda h:(h,0,0))],
        out_shape=[jax.ShapeDtypeStruct((t,d),BF),jax.ShapeDtypeStruct((hp,2,t),F32)],
        compiler_params=pltpu.CompilerParams(vmem_limit_bytes=VM),name="attend")(q,k,v,sr,sc)

def mlp_kernel(nr,nw,wt,x,cot,live,attn,wo,bo,w1,b1,w2,b2,ng,ns,
               out_o,dhid_o,dattn_o,small_o,sf_o,dw2_o,dw1_o,dwo_o,
               g_s,du_s,dm_s,c_s,db_s):
    i=pl.program_id(0)
    rb,d=x.shape
    ff=w1.shape[1]
    fb=ff//nw
    @pl.when(i<nr)
    def _():
        rows=pl.ds(pl.multiple_of(i*rb,rb),rb)
        hid=x[...].astype(F32)+mm(attn[rows,:],wo[...])+bo[...]
        unit,r=row_norm(hid)
        c=(unit*ng[1:2,:]+ns[1:2,:]).astype(BF)
        c_s[rows,:]=c
        lv=live[...].astype(F32)
        dm=cot[...].astype(F32)*lv
        dml=dm.astype(BF)
        dm_s[rows,:]=dml
        mlp=jnp.zeros((rb,d),F32); dc=jnp.zeros((rb,d),F32)
        for f in range(nw):
            cols=slice(f*fb,(f+1)*fb)
            pre=mm(c,w1[:,cols])+b1[:,cols]
            dg=mm(dml,w2[cols,:],1,1)
            phi=0.5*(1.0+lax.erf(pre*(1.0/math.sqrt(2.0))))
            g=(pre*phi).astype(BF)
            slope=phi+pre*jnp.exp(-0.5*pre*pre)*(1.0/math.sqrt(2.0*math.pi))
            du=(dg*slope).astype(BF)
            g_s[rows,cols]=g
            du_s[rows,cols]=du
            mlp=mlp+mm(g,w2[cols,:])
            dc=dc+mm(du,w1[:,cols],1,1)
            part=jnp.sum(du.astype(F32),axis=0,keepdims=True)
            @pl.when(i==0)
            def _(): sf_o[0:1,cols]=part
            @pl.when(i>0)
            def _(): sf_o[0:1,cols]+=part
        out_o[...]=(lv*(hid+mlp+b2[...])).astype(BF)
        e=dc*ng[1:2,:]
        dh=dm+r*(e-jnp.mean(e,axis=-1,keepdims=True)-unit*jnp.mean(e*unit,axis=-1,keepdims=True))
        dhid_o[...]=dh
        db=dh.astype(BF)
        db_s[rows,:]=db
        dattn_o[...]=mm(db,wo[...],1,1).astype(BF)
        sums=jnp.concatenate([jnp.sum(dm,axis=0,keepdims=True),jnp.sum(db.astype(F32),axis=0,keepdims=True),
            jnp.sum(dc*unit,axis=0,keepdims=True),jnp.sum(dc,axis=0,keepdims=True)],axis=0)
        @pl.when(i==0)
        def _(): small_o[...]=sums
        @pl.when(i>0)
        def _(): small_o[...]+=sums
    scale=wt[0]
    for f in range(nw):
        @pl.when(i==nr+f)
        def _():
            cols=slice(f*fb,(f+1)*fb)
            dw2_o[...]=scale*mm(g_s[:,cols],dm_s[...],0,0)
            dw1_o[...]=scale*mm(c_s[...],du_s[:,cols],0,0)
            if f==nw-1:
                dwo_o[...]=scale*mm(attn[...],db_s[...],0,0)

def mlp(wt,x,cot,live,attn,wo,bo,w1,b1,w2,b2,ng,ns,rb=256,nw=4):
    t,d=x.shape; ff=w1.shape[1]
    nr=t//rb; fb=ff//nw
    rows=pl.BlockSpec((rb,d),lambda i:(jnp.minimum(i,nr-1),0))
    const=lambda s: pl.BlockSpec(s,lambda i:(0,)*len(s))
    return pl.pallas_call(functools.partial(mlp_kernel,nr,nw),grid=(nr+nw,),
        in_specs=[pl.BlockSpec(memory_space=pltpu.SMEM),rows,rows,pl.BlockSpec((rb,1),lambda i:(jnp.minimum(i,nr-1),0))]+[whole(a) for a in (attn,wo,bo,w1,b1,w2,b2,ng,ns)],
        out_specs=[rows,rows,rows,const((4,d)),const((1,ff)),pl.BlockSpec((fb,d),lambda i:(jnp.maximum(i-nr,0),0)),
                   pl.BlockSpec((d,fb),lambda i:(0,jnp.maximum(i-nr,0))),const((d,d))],
        out_shape=[jax.ShapeDtypeStruct((t,d),BF),jax.ShapeDtypeStruct((t,d),F32),jax.ShapeDtypeStruct((t,d),BF),
                   jax.ShapeDtypeStruct((4,d),F32),jax.ShapeDtypeStruct((1,ff),F32),jax.ShapeDtypeStruct((ff,d),F32),
                   jax.ShapeDtypeStruct((d,ff),F32),jax.ShapeDtypeStruct((d,d),F32)],
        scratch_shapes=[pltpu.VMEM((t,ff),BF),pltpu.VMEM((t,ff),BF),pltpu.VMEM((t,d),BF),pltpu.VMEM((t,d),BF),pltpu.VMEM((t,d),BF)],
        compiler_params=pltpu.CompilerParams(vmem_limit_bytes=VM),name="mlp")(wt,x,cot,live,attn,wo,bo,w1,b1,w2,b2,ng,ns)

def attend_back_kernel(q,k,v,do,at,lse,sr,sc,qu,ku,qr,kr,qg,dq_o,dk_o,dv_o,small_o,dq_s,dk_s,dv_s,ob=256):
    t=q.shape[0]
    kk=k[...]; vv=v[...]
    kt=kk.T
    lane=lax.broadcasted_iota(jnp.int32,(1,2*HD),1)//HD
    half=lax.broadcasted_iota(jnp.int32,(8,2*HD),1)//HD
    pick=jnp.where(half==lax.broadcasted_iota(jnp.int32,(8,2*HD),0),1.0,0.0).astype(BF)
    for i in range(t//ob):
        rows=slice(i*ob,(i+1)*ob)
        same=sc[...]==sr[:,rows]
        dd=do[rows,:].astype(F32)*at[rows,:].astype(F32)
        hi=dd.astype(BF); rest=dd-hi.astype(F32); mid=rest.astype(BF); low=(rest-mid.astype(F32)).astype(BF)
        delta=mm(pick,hi,1,1)+(mm(pick,mid,1,1)+mm(pick,low,1,1))
        dqs=[]
        for h in range(2):
            qm=jnp.where(lane==h,q[rows,:],0)
            dm=jnp.where(lane==h,do[rows,:],0)
            s=mm(kk,qm,1,1)
            p=jnp.where(same,jnp.exp(s-lse[0,h:h+1,rows]),0.0)
            dp=mm(vv,dm,1,1)
            ds=(p*(dp-delta[h:h+1,:])).astype(BF)
            dvp=mm(p.astype(BF),dm)
            dkp=mm(ds,qm)
            if i==0 and h==0:
                dv_s[...]=dvp; dk_s[...]=dkp
            else:
                dv_s[...]+=dvp; dk_s[...]+=dkp
            dqs.append(mm(kt[h*HD:(h+1)*HD,:],ds))
        dq_s[rows,:]=jnp.concatenate(dqs,axis=0).T*(1.0/math.sqrt(HD))
    dv_o[...]=dv_s[...].astype(BF)
    m=avg_matrix()[:2*HD,:2*HD]
    def avg(x):
        hi=x.astype(BF)
        return mm(hi,m)+mm((x-hi.astype(F32)).astype(BF),m)
    sums=[]
    for n,(g,un,rr,o) in enumerate(((dq_s,qu,qr,dq_o),(dk_s,ku,kr,dk_o))):
        gg=g[...]; u=un[...].astype(F32)
        e=gg*qg[n:n+1,:]
        back=rr[...]*(e-avg(e)-u*avg(e*u))
        o[...]=back.astype(BF)
        sums+= [jnp.sum(gg*u,axis=0,keepdims=True),jnp.sum(gg,axis=0,keepdims=True),jnp.sum(o[...].astype(F32),axis=0,keepdims=True)]
    sums.append(jnp.sum(dv_o[...].astype(F32),axis=0,keepdims=True))
    small_o[...]=jnp.concatenate(sums+[jnp.zeros((1,2*HD),F32)],axis=0)

def attend_backward(q,k,v,do,at,lse,sr,sc,qu,ku,qr,kr,qg):
    t,d=q.shape
    hp=d//(2*HD)
    col=pl.BlockSpec((t,2*HD),lambda h:(0,h))
    return pl.pallas_call(attend_back_kernel,grid=(hp,),
        in_specs=[col]*5+[pl.BlockSpec((1,2,t),lambda h:(h,0,0)),whole(sr),whole(sc)]+[col]*4+[pl.BlockSpec((2,2*HD),lambda h:(0,0))],
        out_specs=[col]*3+[pl.BlockSpec((8,2*HD),lambda h:(0,h))],
        out_shape=[jax.ShapeDtypeStruct((t,d),BF)]*3+[jax.ShapeDtypeStruct((8,d),F32)],
        scratch_shapes=[pltpu.VMEM((t,2*HD),F32)]*3,
        compiler_params=pltpu.CompilerParams(vmem_limit_bytes=VM),name="attend_back")(q,k,v,do,at,lse,sr,sc,qu,ku,qr,kr,qg)

def input_kernel(nr,nw,wt,x,dh,dq,dk,dv,a,w,ng,tg_o,small_o,dw_o):
    i=pl.program_id(0)
    rb,d=x.shape
    @pl.when(i<nr)
    def _():
        rows=pl.ds(pl.multiple_of(i*rb,rb),rb)
        da=mm(dq[rows,:],w[:,:d],1,1)+mm(dk[rows,:],w[:,d:2*d],1,1)+mm(dv[rows,:],w[:,2*d:],1,1)
        unit,r=row_norm(x[...].astype(F32))
        e=da*ng[0:1,:]
        tg_o[...]=dh[...]+r*(e-jnp.mean(e,axis=-1,keepdims=True)-unit*jnp.mean(e*unit,axis=-1,keepdims=True))
        sums=jnp.concatenate([jnp.sum(da*unit,axis=0,keepdims=True),jnp.sum(da,axis=0,keepdims=True)],axis=0)
        @pl.when(i==0)
        def _(): small_o[...]=sums
        @pl.when(i>0)
        def _(): small_o[...]+=sums
    scale=wt[0]
    for f,src in enumerate((dq,dk,dv)):
        @pl.when(i==nr+f)
        def _():
            dw_o[...]=scale*mm(a[...],src[...],0,0)

def input_backward(wt,x,dh,dq,dk,dv,a,w,ng,rb=256):
    t,d=x.shape
    nr=t//rb; nw=3
    rows=pl.BlockSpec((rb,d),lambda i:(jnp.minimum(i,nr-1),0))
    return pl.pallas_call(functools.partial(input_kernel,nr,nw),grid=(nr+nw,),
        in_specs=[pl.BlockSpec(memory_space=pltpu.SMEM),rows,rows]+[whole(z) for z in (dq,dk,dv,a,w,ng)],
        out_specs=[rows,pl.BlockSpec((2,d),lambda i:(0,0)),pl.BlockSpec((d,d),lambda i:(0,jnp.maximum(i-nr,0)))],
        out_shape=[jax.ShapeDtypeStruct((t,d),F32),jax.ShapeDtypeStruct((2,d),F32),jax.ShapeDtypeStruct((d,3*d),F32)],
        compiler_params=pltpu.CompilerParams(vmem_limit_bytes=VM),name="input_back")(wt,x,dh,dq,dk,dv,a,w,ng)


def halve(shape):
    rows, cols = shape
    if rows % 16 == 0: return 0
    if cols % 256 == 0: return 1
    return None

def level_orders(nb, nd):
    bk=[("bucket",i) for i in range(int(math.log2(nb)))]
    dp=[("dp",i) for i in range(int(math.log2(nd)))]
    rest_b=bk[1:]
    a=bk[:1]+dp[:2]+rest_b+dp[2:]
    b=bk[:1]+rest_b+dp[1:2]+dp[:1]+dp[2:]
    return a,b

def rate(bit):
    if bit==("bucket",0): return 600e3
    if bit==("dp",2): return 23e3
    return 46e3
def resource(bit):
    if bit==("dp",2): return ("dp",1)
    return bit

class Job: pass

def make_jobs(chunks, nb, nd):
    orders=level_orders(nb,nd)
    jobs=[]
    for ci,(g,r0,rows,cols,ready) in enumerate(chunks):
        for p in range(2):
            if rows%16:
                if p==1: continue
                base,n=r0,rows
            else:
                n=rows//2; base=r0+p*n
            j=Job(); j.g=g; j.base=base; j.shape=(n,cols); j.ready=ready; j.levels=[]
            sh=(n,cols)
            for bit in orders[p]:
                d=halve(sh)
                out=list(sh)
                if d is not None: out[d]//=2
                j.levels.append((bit,d,tuple(sh),tuple(out)))
                sh=tuple(out)
            jobs.append(j)
    return jobs

def simulate(jobs):
    free={}
    ev=[]
    heap=[(j.ready,k,0) for k,j in enumerate(jobs)]
    heapq.heapify(heap)
    order=[]
    while heap:
        t,k,s=heapq.heappop(heap)
        j=jobs[k]; L=len(j.levels)
        lv = s if s<L else 2*L-1-s
        bit,d,before,after=j.levels[lv]
        moved=after if (s<L or d is not None) else None
        size=4*after[0]*after[1] if moved else 0
        if size==0:
            end=t
        else:
            r=resource(bit)
            start=max(t,free.get(r,0.0))
            end=start+size/rate(bit)
            free[r]=end
            end+=2.0
        order.append((end,t,k,s))
        if s+1<2*L: heapq.heappush(heap,(end,k,s+1))
    order.sort()
    return [(k,s) for _,_,k,s in order], max(o[0] for o in order), order

def bit_of(bit):
    axis,i=bit
    return (lax.axis_index(axis)//(1<<i))%2

def partner(bit, names=("bucket","dp")):
    axis,i=bit
    me=lax.axis_index(axis)
    other=me+(1-2*bit_of(bit))*(1<<i)
    return tuple(other if n==axis else lax.axis_index(n) for n in names)

def region(ref, off, shape):
    r,c=off
    if isinstance(c,int) and c==0 and ref.shape[1]==shape[1]:
        return ref.at[pl.ds(r if isinstance(r,int) else pl.multiple_of(r,8),shape[0]),:]
    return ref.at[pl.ds(r if isinstance(r,int) else pl.multiple_of(r,8),shape[0]),pl.ds(c if isinstance(c,int) else pl.multiple_of(c,128),shape[1])]

def add_into(acc, off, recv, shape):
    rows,cols=shape
    rb=8
    while rows%(rb*2)==0 and rb*2*cols<=32*1024: rb*=2
    r,c=off
    def one(i,_):
        a=acc.at[pl.ds(pl.multiple_of(r+i*rb,8),rb), pl.ds(c if isinstance(c,int) else pl.multiple_of(c,128),cols)]
        a[...]=a[...]+recv[pl.ds(pl.multiple_of(i*rb,8),rb),:]
        return 0
    lax.fori_loop(0,rows//rb,one,0)

class Run:
    def __init__(self, j, src, out, acc, recv, ss, rs, ls):
        self.j=j; self.src=src; self.out=out; self.acc=acc; self.recv=recv
        self.ss=ss; self.rs=rs; self.ls=ls
        self.off=(0,0)
        self.sends=[]
        self.cp=None
        self.loc=None
        bit,d,before,after=j.levels[0]
        self.ob=j.base
        self.gofs=(j.base,0)
    def split(self, lv, off):
        bit,d,before,after=self.j.levels[lv]
        b=bit_of(bit)
        keep=list(off); send=list(off)
        keep[d]=off[d]+b*after[d]; send[d]=off[d]+(1-b)*after[d]
        return tuple(keep),tuple(send)
    def start(self, s):
        L=len(self.j.levels)
        if s<L:
            bit,d,before,after=self.j.levels[s]
            if s==0:
                assert d is not None
                keep,send=self.split(0,(self.j.base,0))
                self.gofs=keep
                src=region(self.src,send,after)
                self.loc=pltpu.make_async_copy(region(self.src,keep,after),self.acc,self.ls.at[0])
                self.loc.start()
                self.off=(0,0)
            elif d is None:
                src=region(self.acc,self.off,after)
            else:
                keep,send=self.split(s,self.off)
                src=region(self.acc,send,after)
                self.off=keep
            cp=pltpu.make_async_remote_copy(src_ref=src,dst_ref=self.recv[s],send_sem=self.ss.at[s],recv_sem=self.rs.at[s],device_id=partner(bit),device_id_type=MESH)
            cp.start()
            self.cp=cp
            if d is not None: self.sends.append(cp)
        else:
            lv=2*L-1-s
            bit,d,before,after=self.j.levels[lv]
            if s==L:
                g=self.g()
                self.piece=(g,after)
                self.loc=pltpu.make_async_copy(region(self.acc,self.off,after),region(self.out,g,after),self.ls.at[1])
                self.loc.start()
                self.first=True
            if d is None:
                self.cp=None
                return
            g,shape=self.piece
            assert shape==after,(shape,after)
            if self.first:
                src=region(self.acc,self.off,after)
                self.first=False
            else:
                if self.loc is not None:
                    self.loc.wait(); self.loc=None
                src=region(self.out,g,after)
            cp=pltpu.make_async_remote_copy(src_ref=src,dst_ref=region(self.out,g,after),send_sem=self.ss.at[s],recv_sem=self.rs.at[s],device_id=partner(bit),device_id_type=MESH)
            cp.start(); self.cp=cp; self.sends.append(cp)
    def g(self):
        return (self.gofs[0]+self.off[0], self.gofs[1]+self.off[1])
    def finish(self, s):
        L=len(self.j.levels)
        if s<L:
            bit,d,before,after=self.j.levels[s]
            if s==0:
                self.loc.wait(); self.loc=None
            if d is None: self.cp.wait()
            else: self.cp.wait_recv()
            add_into(self.acc,self.off,self.recv[s],after)
        else:
            lv=2*L-1-s
            bit,d,before,after=self.j.levels[lv]
            if self.cp is not None:
                self.cp.wait_recv()
            if d is not None:
                g,_=self.piece
                up=list(g); up[d]=g[d]-bit_of(bit)*after[d]
                self.piece=(tuple(up),before)
    def close(self):
        if self.loc is not None: self.loc.wait()
        for cp in self.sends: cp.wait_send()

def barrier(bits):
    sem=pltpu.get_barrier_semaphore()
    for bit in bits:
        pl.semaphore_signal(sem,inc=1,device_id=partner(bit),device_id_type=MESH)
    pl.semaphore_wait(sem,len(bits))

def scratch_of(jobs):
    out=[]
    for j in jobs:
        out.append(pltpu.VMEM(j.levels[0][3],jnp.float32))
        for bit,d,before,after in j.levels: out.append(pltpu.VMEM(after,jnp.float32))
        L=len(j.levels)
        out += [pltpu.SemaphoreType.DMA((2*L,)),pltpu.SemaphoreType.DMA((2*L,)),pltpu.SemaphoreType.DMA((2,))]
    return out

def ar_body(jobs, order, nin, bits, *refs):
    ins=refs[:nin]; outs=refs[nin:2*nin]; sc=list(refs[2*nin:])
    runs=[]
    for j in jobs:
        acc=sc.pop(0); recv=[sc.pop(0) for _ in j.levels]; ss,rs,ls=sc.pop(0),sc.pop(0),sc.pop(0)
        runs.append(Run(j,ins[j.g],outs[j.g],acc,recv,ss,rs,ls))
    barrier(bits)
    for r in runs: r.start(0)
    for k,s in order:
        runs[k].finish(s)
        if s+1<2*len(jobs[k].levels): runs[k].start(s+1)
    for r in runs: r.close()

def all_reduce(grads, chunks, nb, nd, cid=7):
    jobs=make_jobs(chunks,nb,nd)
    order,_,_=simulate(jobs)
    bits=level_orders(nb,nd)[0]
    n=len(grads)
    return pl.pallas_call(functools.partial(ar_body,jobs,order,n,bits),
        out_shape=tuple(jax.ShapeDtypeStruct(g.shape,jnp.float32) for g in grads),
        in_specs=[pl.BlockSpec(memory_space=pltpu.HBM)]*n,
        out_specs=tuple([pl.BlockSpec(memory_space=pltpu.HBM)]*n),
        scratch_shapes=scratch_of(jobs),
        compiler_params=pltpu.CompilerParams(collective_id=cid,has_side_effects=True,vmem_limit_bytes=60<<20),name="allreduce")(*grads)


def body(
    tokens,
    segment,
    live,
    group_patches,
    qkv_weight,
    qkv_bias,
    out_weight,
    out_bias,
    fc1_weight,
    fc1_bias,
    fc2_weight,
    fc2_bias,
    norm_gain,
    norm_shift,
    qk_gain,
    qk_shift,
    cotangent,
):
    row_count, features = tokens.shape
    heads = features // HD
    counts = group_patches.astype(jnp.float32)
    own_count = jnp.sum(
        jnp.where(jnp.arange(counts.shape[0]) == lax.axis_index("bucket"), counts, 0.0)
    )
    weighting = own_count / (jnp.sum(counts) * math.sqrt(row_count * lax.axis_size("dp")))
    wt = weighting.reshape(1)
    seg_row, seg_col = segment[None, :], segment[:, None]
    gains = jnp.tile(qk_gain, (1, heads))
    shifts = jnp.tile(qk_shift, (1, heads))
    a_low, q_low, k_low, v_low, q_unit, k_unit, q_inv, k_inv = qkv_forward(
        tokens, qkv_weight, qkv_bias[None], norm_gain, norm_shift, gains, shifts
    )
    attn_low, lse = attend_forward(q_low, k_low, v_low, seg_row, seg_col)
    out, dhid, dattn, mid_sums, fc1_b_sum, fc2_w_term, fc1_w_term, out_w_term = mlp(
        wt,
        tokens,
        cotangent,
        live[:, None],
        attn_low,
        out_weight,
        out_bias[None],
        fc1_weight,
        fc1_bias[None],
        fc2_weight,
        fc2_bias[None],
        norm_gain,
        norm_shift,
    )
    dq_low, dk_low, dv_low, head_sums = attend_backward(
        q_low, k_low, v_low, dattn, attn_low, lse, seg_row, seg_col, q_unit, k_unit, q_inv, k_inv, gains
    )
    tokens_grad, in_sums, qkv_w_term = input_backward(
        wt, tokens, dhid, dq_low, dk_low, dv_low, a_low, qkv_weight, norm_gain
    )
    per_head = head_sums.reshape(8, heads, HD).sum(axis=1)
    small_terms = weighting * jnp.concatenate(
        [
            head_sums[2],
            head_sums[5],
            head_sums[6],
            mid_sums[1],
            fc1_b_sum[0],
            mid_sums[0],
            in_sums[0],
            mid_sums[2],
            in_sums[1],
            mid_sums[3],
            per_head[0],
            per_head[3],
            per_head[1],
            per_head[4],
        ]
    )
    small_rows = small_terms.size // 128
    small_pad = jnp.pad(small_terms.reshape(small_rows, 128), ((0, 128 - small_rows), (0, 0)))
    terms = [fc2_w_term, fc1_w_term, out_w_term, qkv_w_term, small_pad]
    wide = features // 4
    chunks = [(0, 4 * wide * i, 4 * wide, features, 0.0) for i in range(4)]
    chunks += [(1, wide * i, wide, 4 * features, 0.0) for i in range(4)]
    chunks += [(2, 0, features, features, 0.0)]
    chunks += [(3, 2 * wide * i, 2 * wide, 3 * features, 0.0) for i in range(2)]
    chunks += [(4, 0, 128, 128, 0.0)]
    finished = all_reduce(terms, chunks, lax.axis_size("bucket"), lax.axis_size("dp"))
    hidden_units = fc1_weight.shape[1]
    small_done = finished[4][:small_rows].reshape(-1)
    offset_one = 3 * features
    offset_two = offset_one + features
    offset_three = offset_two + hidden_units
    offset_four = offset_three + features
    offset_five = offset_four + 2 * features
    offset_six = offset_five + 2 * features
    offset_seven = offset_six + 2 * HD
    return (
        out,
        tokens_grad,
        finished[3],
        small_done[:offset_one],
        finished[2],
        small_done[offset_one:offset_two],
        finished[1],
        small_done[offset_two:offset_three],
        finished[0],
        small_done[offset_three:offset_four],
        small_done[offset_four:offset_five].reshape(2, features),
        small_done[offset_five:offset_six].reshape(2, features),
        small_done[offset_six:offset_seven].reshape(2, HD),
        small_done[offset_seven:].reshape(2, HD),
    )


def solution(mesh):
    return jax.shard_map(
        body,
        mesh=mesh,
        in_specs=(
            P(("bucket", "dp"), None),
            P(("bucket", "dp")),
            P(("bucket", "dp")),
            *((P(),) * 13),
            P(("bucket", "dp"), None),
        ),
        out_specs=(P(("bucket", "dp"), None), P(("bucket", "dp"), None), *((P(),) * 12)),
        check_vma=False,
    )
```

```python
import functools
import heapq
import math

import jax
import jax.numpy as jnp
from jax import lax
from jax.experimental import pallas as pl
from jax.experimental.pallas import tpu as pltpu
from jax.sharding import PartitionSpec as P

F32=jnp.float32; BF=jnp.bfloat16
EPSILON=1e-6
NEG=-1e30
HD=64
VM=58<<20

def mm(a,b,ca=1,cb=0):
    return lax.dot_general(a,b,(((ca,),(cb,)),((),())),preferred_element_type=F32)

def row_norm(x):
    c=x-jnp.mean(x,axis=-1,keepdims=True)
    r=lax.rsqrt(jnp.mean(c*c,axis=-1,keepdims=True)+EPSILON)
    return c*r,r

def head_avg(x,m,twice):
    out=[]
    for i in range(x.shape[1]//256):
        part=x[:,256*i:256*(i+1)]
        hi=part.astype(BF)
        s=mm(hi,m)
        if twice: s=s+mm((part-hi.astype(F32)).astype(BF),m)
        out.append(s)
    return jnp.concatenate(out,axis=1)

def avg_matrix():
    i=lax.broadcasted_iota(jnp.int32,(256,256),0)//HD
    j=lax.broadcasted_iota(jnp.int32,(256,256),1)//HD
    return jnp.where(i==j,1.0/HD,0.0).astype(BF)

def whole(a):
    nd=len(a.shape)
    return pl.BlockSpec(a.shape,lambda *_:(0,)*nd,pipeline_mode=pl.Buffered(1))

def qkv_kernel(x,w,b,ng,ns,qg,qs,a_o,q_o,k_o,v_o,qu_o,ku_o,qr_o,kr_o):
    d=x.shape[1]
    u,_=row_norm(x[...].astype(F32))
    a=(u*ng[0:1,:]+ns[0:1,:]).astype(BF)
    a_o[...]=a
    m=avg_matrix()
    for i,(lo,un,rr) in enumerate(((q_o,qu_o,qr_o),(k_o,ku_o,kr_o))):
        raw=mm(a,w[:,i*d:(i+1)*d])+b[:,i*d:(i+1)*d]
        c=raw-head_avg(raw,m,True)
        r=lax.rsqrt(head_avg(c*c,m,False)+EPSILON)
        unit=c*r
        un[...]=unit.astype(BF)
        rr[...]=r
        n=unit*qg[i:i+1,:]+qs[i:i+1,:]
        if i==0: n=n*(1.0/math.sqrt(HD))
        lo[...]=n.astype(BF)
    v_o[...]=(mm(a,w[:,2*d:])+b[:,2*d:]).astype(BF)

def qkv_forward(x,w,b,ng,ns,qg,qs,rb=256):
    t,d=x.shape
    rows=pl.BlockSpec((rb,d),lambda i:(i,0))
    sh=lambda dt: jax.ShapeDtypeStruct((t,d),dt)
    return pl.pallas_call(qkv_kernel,grid=(t//rb,),
        in_specs=[rows,whole(w),whole(b),whole(ng),whole(ns),whole(qg),whole(qs)],
        out_specs=[rows]*8,
        out_shape=[sh(BF)]*6+[sh(F32)]*2,
        compiler_params=pltpu.CompilerParams(vmem_limit_bytes=VM),name="norm_qkv")(x,w,b,ng,ns,qg,qs)

def attend_kernel(q,k,v,sr,sc,o,lse,ob=256):
    t=q.shape[0]
    vt=v[...].T
    kk=k[...]
    lane=lax.broadcasted_iota(jnp.int32,(1,2*HD),1)//HD
    for i in range(t//ob):
        same=sc[...]==sr[:,i*ob:(i+1)*ob]
        parts=[]
        for h in range(2):
            qm=jnp.where(lane==h,q[i*ob:(i+1)*ob,:],0)
            s=jnp.where(same,mm(kk,qm,1,1),NEG)
            m=jnp.max(s,axis=0,keepdims=True)
            p=jnp.exp(s-m)
            l=jnp.sum(p,axis=0,keepdims=True)
            lse[0,h:h+1,i*ob:(i+1)*ob]=m+jnp.log(l)
            acc=mm(vt[h*HD:(h+1)*HD,:],p.astype(BF))
            parts.append(acc*(1.0/l))
        o[i*ob:(i+1)*ob,:]=jnp.concatenate(parts,axis=0).T.astype(BF)

def attend_forward(q,k,v,sr,sc):
    t,d=q.shape
    hp=d//(2*HD)
    col=pl.BlockSpec((t,2*HD),lambda h:(0,h))
    return pl.pallas_call(attend_kernel,grid=(hp,),
        in_specs=[col,col,col,whole(sr),whole(sc)],
        out_specs=[col,pl.BlockSpec((1,2,t),lambda h:(h,0,0))],
        out_shape=[jax.ShapeDtypeStruct((t,d),BF),jax.ShapeDtypeStruct((hp,2,t),F32)],
        compiler_params=pltpu.CompilerParams(vmem_limit_bytes=VM),name="attend")(q,k,v,sr,sc)

def mlp_kernel(nf,x,cot,live,attn,wo,bo,w1,b1,w2,b2,ng,ns,
               out_o,dhid_o,dattn_o,g_o,du_o,dm_o,c_o,db_o,small_o):
    i=pl.program_id(0)
    rb,d=x.shape
    hid=x[...].astype(F32)+mm(attn[...],wo[...])+bo[...]
    unit,r=row_norm(hid)
    c=(unit*ng[1:2,:]+ns[1:2,:]).astype(BF)
    c_o[...]=c
    lv=live[...].astype(F32)
    dm=cot[...].astype(F32)*lv
    dml=dm.astype(BF)
    dm_o[...]=dml
    out=jnp.zeros((rb,d),F32); dc=jnp.zeros((rb,d),F32)
    sums=[]
    for f in range(nf):
        cols=slice(f*d,(f+1)*d)
        pre=mm(c,w1[:,cols])+b1[:,cols]
        dg=mm(dml,w2[cols,:],1,1)
        phi=0.5*(1.0+lax.erf(pre*(1.0/math.sqrt(2.0))))
        g=(pre*phi).astype(BF)
        slope=phi+pre*jnp.exp(-0.5*pre*pre)*(1.0/math.sqrt(2.0*math.pi))
        du=(dg*slope).astype(BF)
        g_o[:,cols]=g
        du_o[:,cols]=du
        out=out+mm(g,w2[cols,:])
        dc=dc+mm(du,w1[:,cols],1,1)
        sums.append(jnp.sum(du.astype(F32),axis=0,keepdims=True))
    out_o[...]=(lv*(hid+out+b2[...])).astype(BF)
    e=dc*ng[1:2,:]
    dh=dm+r*(e-jnp.mean(e,axis=-1,keepdims=True)-unit*jnp.mean(e*unit,axis=-1,keepdims=True))
    dhid_o[...]=dh
    db=dh.astype(BF)
    db_o[...]=db
    dattn_o[...]=mm(db,wo[...],1,1).astype(BF)
    total=jnp.concatenate([jnp.sum(db.astype(F32),axis=0,keepdims=True)]+sums+[jnp.sum(dm,axis=0,keepdims=True),
        jnp.sum(dc*unit,axis=0,keepdims=True),jnp.sum(dc,axis=0,keepdims=True)],axis=0)
    @pl.when(i==0)
    def _(): small_o[...]=total
    @pl.when(i>0)
    def _(): small_o[...]+=total

def mlp(x,cot,live,attn,wo,bo,w1,b1,w2,b2,ng,ns,rb=256):
    t,d=x.shape; ff=w1.shape[1]; nf=ff//d
    rows=pl.BlockSpec((rb,d),lambda i:(i,0))
    wide=pl.BlockSpec((rb,ff),lambda i:(i,0))
    low=jax.ShapeDtypeStruct((t,d),BF)
    big=jax.ShapeDtypeStruct((t,ff),BF)
    return pl.pallas_call(functools.partial(mlp_kernel,nf),grid=(t//rb,),
        in_specs=[rows,rows,pl.BlockSpec((rb,1),lambda i:(i,0)),rows]+[whole(a) for a in (wo,bo,w1,b1,w2,b2,ng,ns)],
        out_specs=[rows,rows,rows,wide,wide,rows,rows,rows,pl.BlockSpec((nf+4,d),lambda i:(0,0))],
        out_shape=[low,jax.ShapeDtypeStruct((t,d),F32),low,big,big,low,low,low,jax.ShapeDtypeStruct((nf+4,d),F32)],
        compiler_params=pltpu.CompilerParams(vmem_limit_bytes=VM),name="mlp")(x,cot,live,attn,wo,bo,w1,b1,w2,b2,ng,ns)

MESH = pl.DeviceIdType.MESH
LATENCY=2.0
TICK=0.7

def halve(shape):
    rows, cols = shape
    if rows % 16 == 0: return 0
    if cols % 256 == 0: return 1
    return None

def bits_of(nb, nd):
    return ([("bucket",i) for i in range(int(math.log2(nb)))]
            + [("dp",i) for i in range(int(math.log2(nd)))])

def level_orders(nb, nd):
    bk=[("bucket",i) for i in range(int(math.log2(nb)))]
    dp=[("dp",i) for i in range(int(math.log2(nd)))]
    a=bk[:1]+dp[:2]+bk[1:]+dp[2:]
    b=bk[:1]+bk[1:]+dp[1:2]+dp[:1]+dp[2:]
    return a,b

class Job:
    def __init__(self, chunk, part, out, place, local, shape, order):
        self.chunk=chunk; self.part=part; self.out=out; self.place=place; self.local=local
        self.levels=[]
        for bit in order:
            d=halve(shape)
            after=list(shape)
            if d is not None: after[d]//=2
            self.levels.append((bit,d,tuple(shape),tuple(after)))
            shape=tuple(after)

def make_jobs(chunks, nb, nd):
    orders=level_orders(nb,nd)
    jobs=[]
    for c,(out,r,k,rows,cols) in enumerate(chunks):
        for p in range(2):
            local=p*(rows//2)
            jobs.append(Job(c,p,out,(r+local,k),local,(rows//2,cols),orders[p]))
    return jobs

class Links:
    def __init__(self): self.free={}
    def end(self, bit, size, t):
        if bit==("dp",2):
            mid,low=self.free.get(bit,0.0),self.free.get(("dp",1),0.0)
            start=max(t,mid,low)
            self.free[("dp",1)]=max(t,low)+size/46e3
            self.free[bit]=start+size/23e3
            return start+size/23e3+LATENCY
        rate=600e3 if bit==("bucket",0) else 46e3
        start=max(t,self.free.get(bit,0.0))
        self.free[bit]=start+size/rate
        return self.free[bit]+LATENCY

def schedule(jobs, steps, ring, shares):
    links=Links(); heap=[]; items=[]; done=set(); now=0.0
    of_chunk={}
    for k,j in enumerate(jobs): of_chunk.setdefault(j.chunk,[]).append(k)
    def issue(k,s,t):
        L=len(jobs[k].levels)
        bit,d,before,after=jobs[k].levels[s if s<L else 2*L-1-s]
        end=t if (s>=L and d is None) else links.end(bit,4*after[0]*after[1],t)
        heapq.heappush(heap,(end,k,s))
    def one(t):
        end,k,s=heapq.heappop(heap)
        t=max(t,end)+TICK
        items.append(("end",k,s)); done.add((k,s))
        if s+1<2*len(jobs[k].levels): issue(k,s+1,t)
        return t
    for i,(chunk,us) in enumerate(steps):
        while heap and heap[0][0]<=now: now=one(now)
        if chunk is not None:
            need=[(k,0) for k in of_chunk.get(chunk-ring,[])] if us>0 and chunk+1<len(of_chunk) else []
            if chunk in shares:
                need+=[(k,2*len(jobs[k].levels)-1) for k in of_chunk[shares[chunk]]]
            while not all(n in done for n in need): now=one(now)
        items.append(("step",i)); now+=us
        if chunk is not None:
            for k in of_chunk[chunk]: issue(k,0,now)
    while heap: now=one(now)
    return items,now

def bit_of(bit):
    axis,i=bit
    return (lax.axis_index(axis)//(1<<i))%2

def partner(bit):
    axis,i=bit
    me=lax.axis_index(axis)
    other=me+(1-2*bit_of(bit))*(1<<i)
    return tuple(other if n==axis else lax.axis_index(n) for n in ("bucket","dp"))

def span(start,size,by):
    return pl.ds(start if isinstance(start,int) else pl.multiple_of(start,by),size)

def region(ref, off, shape):
    return ref.at[span(off[0],shape[0],8),span(off[1],shape[1],128)]

def add_rows(dst, a, b, shape):
    rows,cols=shape
    rb=8
    while rows%(rb*2)==0 and rb*2*cols<=32*1024: rb*=2
    def one(i,_):
        at=pl.ds(pl.multiple_of(i*rb,8),rb)
        dst[at,:]=a[at,:]+b[at,:]
        return 0
    lax.fori_loop(0,rows//rb,one,0)

class Run:
    def __init__(self, job, src, out, acc, recv, ss, rs, ls, credit=None, give=False, take=False):
        self.j=job; self.src=src; self.out=out; self.acc=acc; self.recv=recv
        self.ss=ss; self.rs=rs; self.ls=ls
        self.credit=credit; self.give=give; self.take=take
        self.n=len(job.levels)
        self.unsent={s for s in range(2*self.n) if self.level(s)[1] is not None}
        self.stored=False
    def level(self, s):
        return self.j.levels[s if s<self.n else 2*self.n-1-s]
    def offset(self, first, last):
        off=[0,0]
        for bit,d,before,after in self.j.levels[first:last+1]:
            if d is not None: off[d]=off[d]+bit_of(bit)*after[d]
        return off
    def given(self, s, off):
        bit,d,before,after=self.j.levels[s]
        off=list(off); off[d]=off[d]+(1-bit_of(bit))*after[d]
        return off
    def piece(self, lv):
        off=self.offset(0,lv)
        return [self.j.place[0]+off[0],self.j.place[1]+off[1]]
    def local(self):
        after=self.level(self.n)[3]
        return pltpu.make_async_copy(region(self.acc,self.offset(1,self.n-1),after),
                                     region(self.out,self.piece(self.n-1),after),self.ls.at[0])
    def remote(self, s):
        bit,d,before,after=self.level(s)
        if s==0:
            src,dst=region(self.src,self.given(0,[self.j.local,0]),after),self.recv[0]
        elif s<self.n:
            off=self.offset(1,s-1)
            src,dst=region(self.acc,off if d is None else self.given(s,off),after),self.recv[s]
        else:
            dst=region(self.out,self.piece(2*self.n-1-s),after)
            first=all(self.level(i)[1] is None for i in range(self.n,s))
            src=region(self.acc,self.offset(1,self.n-1),after) if first else dst
        return pltpu.make_async_remote_copy(src_ref=src,dst_ref=dst,send_sem=self.ss.at[s],recv_sem=self.rs.at[s],
                                            device_id=partner(bit),device_id_type=MESH)
    def start(self, s):
        bit,d,before,after=self.level(s)
        if s==self.n: self.local().start()
        if s>=self.n and d is None: return
        if s>self.n and not self.stored and any(self.level(i)[1] is not None for i in range(self.n,s)):
            self.local().wait(); self.stored=True
        if s==0 and self.take: pl.semaphore_wait(self.credit,1)
        self.remote(s).start()
    def finish(self, s):
        bit,d,before,after=self.level(s)
        if s>=self.n:
            if d is not None: self.remote(s).wait_recv()
        else:
            if d is None: self.remote(s).wait()
            else: self.remote(s).wait_recv()
            to=region(self.acc,self.offset(1,s),after)
            own=region(self.src,[self.j.local+self.offset(0,0)[0],0],after) if s==0 else to
            add_rows(to,own,self.recv[s],after)
            if s==0 and self.give:
                pl.semaphore_signal(self.credit,inc=1,device_id=partner(bit),device_id_type=MESH)
        if s+1<2*self.n: self.start(s+1)
    def sent(self):
        if 0 in self.unsent: self.remote(0).wait_send(); self.unsent.discard(0)
    def close(self):
        if not self.stored: self.local().wait(); self.stored=True
        for s in sorted(self.unsent): self.remote(s).wait_send()
        self.unsent=set()

RING=2

def back_kernel(plan,*refs):
    (jobs,items,nchunk,nf,nhead,nblk,nrow,shares,bits)=plan
    refs=list(refs)
    def take(n):
        out=refs[:n]; del refs[:n]; return out
    (wt,g,du,dm,c,at_h,db,a,w)=take(9)
    (q,k,v,do,at,lse,qu,ku,qr,kr)=take(10)
    (sr,sc,qg,mid,x,dh,ng)=take(7)
    outs=take(5)
    (tg_o,)=take(1)
    (pool,stage,l0,dqkv,dq_s,dk_s,dv_s,kt_s,small)=take(9)
    (pool_sem,credit)=take(2)
    t,d=at_h.shape
    ob=t//nblk
    own=nchunk-len(shares)-1
    bufs=[]
    for n in range(own+1):
        pair=[]
        for p in range(2):
            L=len(jobs[2*(n if n<own else nchunk-1)+p].levels)
            pair.append((take(1)[0],take(L-1 if n<own else L)))
        bufs.append(pair)
    runs=[]
    for n,j in enumerate(jobs):
        ss,rs,ls=take(3)
        if j.chunk==nchunk-1:
            acc,recv=bufs[own][j.part]
            runs.append(Run(j,small,outs[j.out],acc,recv,ss,rs,ls))
        else:
            acc,recv=bufs[shares.get(j.chunk,j.chunk)][j.part]
            runs.append(Run(j,stage.at[j.chunk%RING],outs[j.out],acc,[l0.at[2*(j.chunk%RING)+j.part]]+list(recv),ss,rs,ls,
                            credit.at[j.part],give=j.chunk+RING<nchunk-1,take=j.chunk>=RING))
    pid=pl.program_id(0)
    def col(ref,f): return ref.at[:,pl.ds(f*d,d)]
    names={"g":g,"du":du,"dm":dm,"c":c,"at":at_h,"db":db,"a":a,"w":w}
    plan_l=[]
    for f in range(nf): plan_l.append((("g",f),0 if f%2==0 else 2,1,True))
    for f in range(nf): plan_l.append((("du",f),0 if (nf+f)%2==0 else 2,3,False))
    load={i:[] for i in range(-1,2*nf+2)}
    load[-1]+= [(("dm",0),1),(("c",0),3)]
    for i,(what,s,other,_) in enumerate(plan_l):
        load[max(i-2,-1)].append((what,s))
    n0=2*nf+1
    s_at=0 if (2*nf)%2==0 else 2
    load[2*nf-2].append((("at",0),s_at))
    load[nf].append((("db",0),1))
    load[2*nf-1].append((("a",0),3))
    load[2*nf]+= [(("w",0),0),(("w",1),1),(("w",2),2)]
    def copy_of(what,s):
        name,f=what
        if name=="w": return pltpu.make_async_copy(col(w,f),pool.at[s,pl.ds(0,d),:],pool_sem.at[s])
        if name in ("g","du"): return pltpu.make_async_copy(col(names[name],f),pool.at[s],pool_sem.at[s])
        return pltpu.make_async_copy(names[name],pool.at[s],pool_sem.at[s])
    waiting={}
    def fetch_after(i):
        for what,s in load.get(i,[]):
            copy_of(what,s).start(); waiting[s]=what
    def ready(s):
        if s in waiting: copy_of(waiting.pop(s),s).wait()
    scale=wt[0]
    steps=[]
    for i,(what,s,other,first) in enumerate(plan_l): steps.append(("w",i,s,other) if first else ("w",i,other,s))
    steps.append(("w",2*nf,s_at,1))
    for h in range(nhead*nblk): steps.append(("h",h))
    for n in range(3): steps.append(("x",n))
    for r in range(nrow): steps.append(("r",r))
    n_h=n0; n_x=n0+nhead*nblk; n_r=n_x+3; n_end=n_r+nrow

    def weight_step(chunk,lhs,rhs):
        if chunk>=RING:
            for p in range(2): runs[2*(chunk-RING)+p].sent()
        if chunk in shares:
            for p in range(2): runs[2*shares[chunk]+p].close()
        stage[chunk%RING]=scale*mm(lhs,rhs,0,0)
        for p in range(2): runs[2*chunk+p].start(0)

    def before(i):
        for it in segments[i]: runs[it[1]].finish(it[2])
    segments=[[]]
    for it in items:
        if it[0]=="step": segments.append([])
        else: segments[-1].append(it)
    for i,st in enumerate(steps+[("end",)]):
        kind=st[0]
        need = segments[i] or kind in ("w","x","end") or i==0 or i==n_r
        if not need: continue
        @pl.when(pid==i)
        def _(i=i,st=st,kind=kind):
            if i==0:
                sem=pltpu.get_barrier_semaphore()
                for bit in bits:
                    pl.semaphore_signal(sem,inc=1,device_id=partner(bit),device_id_type=MESH)
                pl.semaphore_wait(sem,len(bits))
                fetch_after(-1)
                small[...]=jnp.zeros_like(small)
                small[3:3+nf+2,:]=scale*mid[0:nf+2,:]
                small[nf+6:nf+7,:]=scale*mid[nf+2:nf+3,:]
                small[nf+8:nf+9,:]=scale*mid[nf+3:nf+4,:]
            before(i)
            if kind=="w":
                _,n,ls_,rs_=st
                ready(ls_); ready(rs_)
                weight_step(n,pool[ls_],pool[rs_])
                fetch_after(n)
            elif kind=="x":
                n=st[1]
                if n==0:
                    for s in range(4): ready(s)
                weight_step(n0+n,pool[3],dqkv[:,n*d:(n+1)*d])
            elif kind=="end":
                for r in runs: r.close()
    @pl.when((pid>=n_h)&(pid<n_x))
    def _():
        ib=lax.rem(pid-n_h,nblk); hp=(pid-n_h)//nblk
        rows=pl.ds(pl.multiple_of(ib*ob,ob),ob)
        lanes=pl.ds(pl.multiple_of(hp*2*HD,2*HD),2*HD)
        @pl.when(ib==0)
        def _():
            kt_s[...]=k[...].T
            dk_s[...]=jnp.zeros_like(dk_s); dv_s[...]=jnp.zeros_like(dv_s)
        lane=lax.broadcasted_iota(jnp.int32,(1,2*HD),1)//HD
        half=lax.broadcasted_iota(jnp.int32,(8,2*HD),1)//HD
        pick=jnp.where(half==lax.broadcasted_iota(jnp.int32,(8,2*HD),0),1.0,0.0).astype(BF)
        same=sc[...]==sr[:,rows]
        dd=do[rows,:].astype(F32)*at[rows,:].astype(F32)
        hi=dd.astype(BF); rest=dd-hi.astype(F32); mid_=rest.astype(BF); low=(rest-mid_.astype(F32)).astype(BF)
        delta=mm(pick,hi,1,1)+(mm(pick,mid_,1,1)+mm(pick,low,1,1))
        dqs=[]
        for h in range(2):
            qm=jnp.where(lane==h,q[rows,:],0)
            dom=jnp.where(lane==h,do[rows,:],0)
            s=mm(k[...],qm,1,1)
            p=jnp.where(same,jnp.exp(s-lse[0,h:h+1,rows]),0.0)
            dp=mm(v[...],dom,1,1)
            ds=(p*(dp-delta[h:h+1,:])).astype(BF)
            dv_s[...]+=mm(p.astype(BF),dom)
            dk_s[...]+=mm(ds,qm)
            dqs.append(mm(kt_s[h*HD:(h+1)*HD,:],ds))
        dq_s[rows,:]=jnp.concatenate(dqs,axis=0).T*(1.0/math.sqrt(HD))
        @pl.when(ib==nblk-1)
        def _():
            m=avg_matrix()[:2*HD,:2*HD]
            def avg(y):
                yh=y.astype(BF)
                return mm(yh,m)+mm((y-yh.astype(F32)).astype(BF),m)
            for n,(gr,un,rr) in enumerate(((dq_s,qu,qr),(dk_s,ku,kr))):
                gg=gr[...]; u=un[...].astype(F32)
                e=gg*qg[n:n+1,:]
                back=(rr[...]*(e-avg(e)-u*avg(e*u))).astype(BF)
                dqkv[:,pl.ds(pl.multiple_of(n*d+hp*2*HD,2*HD),2*HD)]=back
                small[n:n+1,lanes]=scale*jnp.sum(back.astype(F32),axis=0,keepdims=True)
                small[nf+9+n:nf+10+n,lanes]=scale*jnp.sum(gg*u,axis=0,keepdims=True)
                small[nf+11+n:nf+12+n,lanes]=scale*jnp.sum(gg,axis=0,keepdims=True)
            back=dv_s[...].astype(BF)
            dqkv[:,pl.ds(pl.multiple_of(2*d+hp*2*HD,2*HD),2*HD)]=back
            small[2:3,lanes]=scale*jnp.sum(back.astype(F32),axis=0,keepdims=True)
    @pl.when((pid>=n_r)&(pid<n_end))
    def _():
        rb=x.shape[0]
        rows=pl.ds(pl.multiple_of((pid-n_r)*rb,rb),rb)
        da=mm(dqkv[rows,0:d],pool[0,:d,:],1,1)+mm(dqkv[rows,d:2*d],pool[1,:d,:],1,1)+mm(dqkv[rows,2*d:],pool[2,:d,:],1,1)
        unit,r=row_norm(x[...].astype(F32))
        e=da*ng[0:1,:]
        tg_o[...]=dh[...]+r*(e-jnp.mean(e,axis=-1,keepdims=True)-unit*jnp.mean(e*unit,axis=-1,keepdims=True))
        small[nf+5:nf+6,:]+=scale*jnp.sum(da*unit,axis=0,keepdims=True)
        small[nf+7:nf+8,:]+=scale*jnp.sum(da,axis=0,keepdims=True)
        @pl.when(pid==n_end-1)
        def _():
            for p in range(2): runs[2*(nchunk-1)+p].start(0)

def backward(wt,g,du,dm,c,at,db,a,w,q,k,v,do,lse,qu,ku,qr,kr,sr,sc,qg,mid,x,dh,ng,nb,nd,ob=256,rb=256):
    t,d=x.shape; ff=g.shape[1]; nf=ff//d
    nhead=d//(2*HD); nblk=t//ob; nrow=t//rb
    n0=2*nf+1
    chunks=[(0,f*d,0,d,d) for f in range(nf)]+[(1,0,f*d,d,d) for f in range(nf)]+[(2,0,0,d,d)]
    chunks+=[(3,0,n*d,d,d) for n in range(3)]+[(4,0,0,32,d)]
    nchunk=len(chunks)
    shares={n0+n:n for n in range(3)}
    jobs=make_jobs(chunks,nb,nd)
    steps=[(n,1.9) for n in range(n0)]+[(None,1.8)]*(nhead*nblk)+[(n0+n,1.9) for n in range(3)]+[(None,2.0)]*(nrow-1)+[(nchunk-1,2.0)]
    items,_=schedule(jobs,steps,RING,shares)
    bits=bits_of(nb,nd)
    n_h=n0; n_x=n0+nhead*nblk; n_r=n_x+3; n_end=n_r+nrow
    def head(i): return jnp.clip((i-n_h)//nblk,0,nhead-1)
    def row(i): return jnp.clip(i-n_r,0,nrow-1)
    any_=pl.BlockSpec(memory_space=pltpu.HBM)
    colspec=pl.BlockSpec((t,2*HD),lambda i:(0,head(i)))
    rows=pl.BlockSpec((rb,d),lambda i:(row(i),0))
    in_specs=[pl.BlockSpec(memory_space=pltpu.SMEM)]+[any_]*8+[colspec]*5+[pl.BlockSpec((1,2,t),lambda i:(head(i),0,0))]+[colspec]*4
    in_specs+=[whole(sr),whole(sc),pl.BlockSpec((2,2*HD),lambda i:(0,0)),whole(mid),rows,rows,whole(ng)]
    out_specs=[any_]*5+[rows]
    S=jax.ShapeDtypeStruct
    out_shape=[S((ff,d),F32),S((d,ff),F32),S((d,d),F32),S((d,3*d),F32),S((32,d),F32),S((t,d),F32)]
    half=(d//2)//2
    scratch=[pltpu.VMEM((4,t,d),BF),pltpu.VMEM((RING,d,d),F32),pltpu.VMEM((2*RING,half,d),F32),pltpu.VMEM((t,3*d),BF)]
    scratch+=[pltpu.VMEM((t,2*HD),F32)]*3+[pltpu.VMEM((2*HD,t),BF),pltpu.VMEM((32,d),F32),pltpu.SemaphoreType.DMA((4,)),pltpu.SemaphoreType.REGULAR((2,))]
    own=nchunk-len(shares)-1
    for n in range(own+1):
        small=n==own
        for p in range(2):
            j=jobs[2*(nchunk-1 if small else n)+p]
            scratch.append(pltpu.VMEM(j.levels[0][3],F32))
            for lv in j.levels[0 if small else 1:]: scratch.append(pltpu.VMEM(lv[3],F32))
    for j in jobs:
        L=len(j.levels)
        scratch+=[pltpu.SemaphoreType.DMA((2*L,)),pltpu.SemaphoreType.DMA((2*L,)),pltpu.SemaphoreType.DMA((1,))]
    plan=(jobs,items,nchunk,nf,nhead,nblk,nrow,shares,bits)
    return pl.pallas_call(functools.partial(back_kernel,plan),grid=(n_end+1,),in_specs=in_specs,out_specs=out_specs,out_shape=out_shape,
        scratch_shapes=scratch,
        compiler_params=pltpu.CompilerParams(collective_id=7,has_side_effects=True,vmem_limit_bytes=63<<20),name="backward")(
        wt,g,du,dm,c,at,db,a,w,q,k,v,do,at,lse,qu,ku,qr,kr,sr,sc,qg,mid,x,dh,ng)


def body(
    tokens,
    segment,
    live,
    group_patches,
    qkv_weight,
    qkv_bias,
    out_weight,
    out_bias,
    fc1_weight,
    fc1_bias,
    fc2_weight,
    fc2_bias,
    norm_gain,
    norm_shift,
    qk_gain,
    qk_shift,
    cotangent,
):
    row_count, features = tokens.shape
    heads = features // HD
    counts = group_patches.astype(jnp.float32)
    own_count = jnp.sum(
        jnp.where(jnp.arange(counts.shape[0]) == lax.axis_index("bucket"), counts, 0.0)
    )
    weighting = own_count / (jnp.sum(counts) * math.sqrt(row_count * lax.axis_size("dp")))
    wt = weighting.reshape(1)
    seg_row, seg_col = segment[None, :], segment[:, None]
    gains = jnp.tile(qk_gain, (1, heads))
    shifts = jnp.tile(qk_shift, (1, heads))
    a_low, q_low, k_low, v_low, q_unit, k_unit, q_inv, k_inv = qkv_forward(
        tokens, qkv_weight, qkv_bias[None], norm_gain, norm_shift, gains, shifts
    )
    attn_low, lse = attend_forward(q_low, k_low, v_low, seg_row, seg_col)
    out, dhid, dattn, g_low, du_low, dm_low, c_low, db_low, mid_sums = mlp(
        tokens,
        cotangent,
        live[:, None],
        attn_low,
        out_weight,
        out_bias[None],
        fc1_weight,
        fc1_bias[None],
        fc2_weight,
        fc2_bias[None],
        norm_gain,
        norm_shift,
    )
    fc2_grad, fc1_grad, out_grad, qkv_grad, small, tokens_grad = backward(
        wt, g_low, du_low, dm_low, c_low, attn_low, db_low, a_low, qkv_weight,
        q_low, k_low, v_low, dattn, lse, q_unit, k_unit, q_inv, k_inv,
        seg_row, seg_col, gains, mid_sums, tokens, dhid, norm_gain,
        lax.axis_size("bucket"), lax.axis_size("dp"),
    )
    wide = fc1_weight.shape[1] // features
    per_head = small[wide + 9 : wide + 13].reshape(4, heads, HD).sum(axis=1)
    return (
        out,
        tokens_grad,
        qkv_grad,
        small[:3].reshape(-1),
        out_grad,
        small[3],
        fc1_grad,
        small[4 : wide + 4].reshape(-1),
        fc2_grad,
        small[wide + 4],
        small[wide + 5 : wide + 7],
        small[wide + 7 : wide + 9],
        per_head[:2],
        per_head[2:],
    )


def solution(mesh):
    return jax.shard_map(
        body,
        mesh=mesh,
        in_specs=(
            P(("bucket", "dp"), None),
            P(("bucket", "dp")),
            P(("bucket", "dp")),
            *((P(),) * 13),
            P(("bucket", "dp"), None),
        ),
        out_specs=(P(("bucket", "dp"), None), P(("bucket", "dp"), None), *((P(),) * 12)),
        check_vma=False,
    )
```

```python
import functools
import heapq
import math

import jax
import jax.numpy as jnp
from jax import lax
from jax.experimental import pallas as pl
from jax.experimental.pallas import tpu as pltpu
from jax.sharding import PartitionSpec as P

F32=jnp.float32; BF=jnp.bfloat16
EPSILON=1e-6
NEG=-1e30
HD=64
VM=58<<20

def mm(a,b,ca=1,cb=0):
    return lax.dot_general(a,b,(((ca,),(cb,)),((),())),preferred_element_type=F32)

def row_norm(x):
    c=x-jnp.mean(x,axis=-1,keepdims=True)
    r=lax.rsqrt(jnp.mean(c*c,axis=-1,keepdims=True)+EPSILON)
    return c*r,r

def head_avg(x,m,twice):
    out=[]
    for i in range(x.shape[1]//256):
        part=x[:,256*i:256*(i+1)]
        hi=part.astype(BF)
        s=mm(hi,m)
        if twice: s=s+mm((part-hi.astype(F32)).astype(BF),m)
        out.append(s)
    return jnp.concatenate(out,axis=1)

def avg_matrix():
    i=lax.broadcasted_iota(jnp.int32,(256,256),0)//HD
    j=lax.broadcasted_iota(jnp.int32,(256,256),1)//HD
    return jnp.where(i==j,1.0/HD,0.0).astype(BF)

def row(ref):
    return ref[...][None,:]

def column(values, lanes):
    return jnp.broadcast_to(values,(lanes,values.shape[1])).T

def per_head(ref, times):
    return jnp.concatenate([ref[...]]*times,axis=1)

def whole(a):
    nd=len(a.shape)
    return pl.BlockSpec(a.shape,lambda *_:(0,)*nd,pipeline_mode=pl.Buffered(1))

def qkv_kernel(x,w,b,ng,ns,qg,qs,a_o,q_o,k_o,v_o,qu_o,ku_o,qr_o,kr_o):
    d=x.shape[1]
    gains=per_head(qg,d//HD); shifts=per_head(qs,d//HD)
    bias=row(b)
    u,_=row_norm(x[...].astype(F32))
    a=(u*ng[0:1,:]+ns[0:1,:]).astype(BF)
    a_o[...]=a
    m=avg_matrix()
    for i,(lo,un,rr) in enumerate(((q_o,qu_o,qr_o),(k_o,ku_o,kr_o))):
        raw=mm(a,w[:,i*d:(i+1)*d])+bias[:,i*d:(i+1)*d]
        c=raw-head_avg(raw,m,True)
        r=lax.rsqrt(head_avg(c*c,m,False)+EPSILON)
        unit=c*r
        un[...]=unit.astype(BF)
        rr[...]=r
        n=unit*gains[i:i+1,:]+shifts[i:i+1,:]
        if i==0: n=n*(1.0/math.sqrt(HD))
        lo[...]=n.astype(BF)
    v_o[...]=(mm(a,w[:,2*d:])+bias[:,2*d:]).astype(BF)

def qkv_forward(x,w,b,ng,ns,qg,qs,rb=256):
    t,d=x.shape
    rows=pl.BlockSpec((rb,d),lambda i:(i,0))
    sh=lambda dt: jax.ShapeDtypeStruct((t,d),dt)
    return pl.pallas_call(qkv_kernel,grid=(t//rb,),
        in_specs=[rows,whole(w),whole(b),whole(ng),whole(ns),whole(qg),whole(qs)],
        out_specs=[rows]*8,
        out_shape=[sh(BF)]*6+[sh(F32)]*2,
        compiler_params=pltpu.CompilerParams(vmem_limit_bytes=VM),name="norm_qkv")(x,w,b,ng,ns,qg,qs)

BIG=384.0

def segment_codes(col, count):
    bits=(count-1).bit_length()
    at=lax.rem(lax.broadcasted_iota(jnp.int32,col.shape,1),HD)
    bit=lax.shift_right_logical(col.astype(jnp.int32),jnp.minimum(at,bits))&1
    sign=jnp.where(at<bits,(2*bit-1).astype(F32),0.0)
    key=jnp.where(at==bits,1.0,sign)
    query=jnp.where(at==bits,-BIG*bits,BIG*sign)
    return key.astype(BF),query.astype(BF)

def attend_kernel(q,k,v,seg,o,lse,kc,qc,s_s,p_s,ob=256,tb=64):
    t=q.shape[0]
    @pl.when(pl.program_id(0)==0)
    def _(): kc[...],qc[...]=segment_codes(column(row(seg).astype(F32),2*HD),t)
    vt=v[...].T
    lane=lax.broadcasted_iota(jnp.int32,(1,2*HD),1)//HD
    keys=[jnp.where(lane==h,k[...],kc[...]) for h in range(2)]
    for i in range(t//ob):
        rows=slice(i*ob,(i+1)*ob)
        parts=[]
        for h in range(2):
            s_s[h]=mm(keys[h],jnp.where(lane==h,q[rows,:],qc[rows,:]),1,1)
        for h in range(2):
            top=s_s[h,:tb,:]
            for n in range(1,t//tb): top=jnp.maximum(top,s_s[h,n*tb:(n+1)*tb,:])
            m=jnp.max(top,axis=0,keepdims=True)
            total=jnp.zeros((tb,ob),F32)
            for n in range(t//tb):
                p=jnp.exp(s_s[h,n*tb:(n+1)*tb,:]-m)
                total=total+p
                p_s[h,n*tb:(n+1)*tb,:]=p.astype(BF)
            l=jnp.sum(total,axis=0,keepdims=True)
            lse[0,h:h+1,rows]=m+jnp.log(l)
            parts.append(mm(vt[h*HD:(h+1)*HD,:],p_s[h])*(1.0/l))
        o[rows,:]=jnp.concatenate(parts,axis=0).T.astype(BF)

def attend_forward(q,k,v,seg):
    t,d=q.shape
    hp=d//(2*HD)
    col=pl.BlockSpec((t,2*HD),lambda h:(0,h))
    return pl.pallas_call(attend_kernel,grid=(hp,),
        in_specs=[col,col,col,whole(seg)],
        out_specs=[col,pl.BlockSpec((1,2,t),lambda h:(h,0,0))],
        out_shape=[jax.ShapeDtypeStruct((t,d),BF),jax.ShapeDtypeStruct((hp,2,t),F32)],
        scratch_shapes=[pltpu.VMEM((t,2*HD),BF)]*2+[pltpu.VMEM((2,t,256),F32),pltpu.VMEM((2,t,256),BF)],
        compiler_params=pltpu.CompilerParams(vmem_limit_bytes=VM),name="attend")(q,k,v,seg)

def mlp_kernel(nf,x,cot,live,attn,wo,bo,w1,b1,w2,b2,ng,ns,
               out_o,dhid_o,dattn_o,g_o,du_o,dm_o,c_o,db_o,small_o,pre_s,dg_s,tb=16):
    i=pl.program_id(0)
    rb,d=x.shape
    hid=x[...].astype(F32)+mm(attn[...],wo[...])+row(bo)
    unit,r=row_norm(hid)
    c=(unit*ng[1:2,:]+ns[1:2,:]).astype(BF)
    c_o[...]=c
    lv=column(live[:,pl.ds(pl.multiple_of(i*rb,rb),rb)].astype(F32),8)[:,:1]
    fc1_bias=row(b1)
    dm=cot[...].astype(F32)*lv
    dml=dm.astype(BF)
    dm_o[...]=dml
    out=jnp.zeros((rb,d),F32); dc=jnp.zeros((rb,d),F32)
    sums=[]
    for f in range(nf):
        cols=slice(f*d,(f+1)*d)
        pre_s[...]=mm(c,w1[:,cols])
        dg_s[...]=mm(dml,w2[cols,:],1,1)
        total=jnp.zeros((tb,d),F32)
        for n in range(rb//tb):
            at=slice(n*tb,(n+1)*tb)
            pre=pre_s[at,:]+fc1_bias[:,cols]
            phi=0.5*(1.0+lax.erf(pre*(1.0/math.sqrt(2.0))))
            slope=phi+pre*jnp.exp(-0.5*pre*pre)*(1.0/math.sqrt(2.0*math.pi))
            du=(dg_s[at,:]*slope).astype(BF)
            g_o[at,cols]=(pre*phi).astype(BF)
            du_o[at,cols]=du
            total=total+du.astype(F32)
        g,du=g_o[:,cols],du_o[:,cols]
        out=out+mm(g,w2[cols,:])
        dc=dc+mm(du,w1[:,cols],1,1)
        sums.append(jnp.sum(total,axis=0,keepdims=True))
    out_o[...]=(lv*(hid+out+row(b2))).astype(BF)
    e=dc*ng[1:2,:]
    dh=dm+r*(e-jnp.mean(e,axis=-1,keepdims=True)-unit*jnp.mean(e*unit,axis=-1,keepdims=True))
    dhid_o[...]=dh
    db=dh.astype(BF)
    db_o[...]=db
    dattn_o[...]=mm(db,wo[...],1,1).astype(BF)
    total=jnp.concatenate([jnp.sum(db.astype(F32),axis=0,keepdims=True)]+sums+[jnp.sum(dm,axis=0,keepdims=True),
        jnp.sum(dc*unit,axis=0,keepdims=True),jnp.sum(dc,axis=0,keepdims=True)],axis=0)
    @pl.when(i==0)
    def _(): small_o[...]=total
    @pl.when(i>0)
    def _(): small_o[...]+=total

def mlp(x,cot,live,attn,wo,bo,w1,b1,w2,b2,ng,ns,rb=256):
    t,d=x.shape; ff=w1.shape[1]; nf=ff//d
    rows=pl.BlockSpec((rb,d),lambda i:(i,0))
    wide=pl.BlockSpec((rb,ff),lambda i:(i,0))
    low=jax.ShapeDtypeStruct((t,d),BF)
    big=jax.ShapeDtypeStruct((t,ff),BF)
    return pl.pallas_call(functools.partial(mlp_kernel,nf),grid=(t//rb,),
        in_specs=[rows,rows,whole(live),rows]+[whole(a) for a in (wo,bo,w1,b1,w2,b2,ng,ns)],
        out_specs=[rows,rows,rows,wide,wide,rows,rows,rows,pl.BlockSpec((nf+4,d),lambda i:(0,0))],
        out_shape=[low,jax.ShapeDtypeStruct((t,d),F32),low,big,big,low,low,low,jax.ShapeDtypeStruct((nf+4,d),F32)],
        scratch_shapes=[pltpu.VMEM((rb,d),F32)]*2,
        compiler_params=pltpu.CompilerParams(vmem_limit_bytes=VM),name="mlp")(x,cot,live,attn,wo,bo,w1,b1,w2,b2,ng,ns)

MESH = pl.DeviceIdType.MESH
RATE=45e3
LATENCY=1.6
ENDS=(0.45,0.3)
CAP=99
ORDERS=(
    'cxyab', 'cyaxb', 'cayxb', 'cyxab', 'cxayb', 'caxyb', 'cxayb', 'cyabx',
    'cxayb', 'cyaxb', 'cxayb', 'cyaxb', 'cyaxb', 'cxyab', 'cxyab', 'cyxab',
    'cxyab', 'cyxab', 'cxayb', 'cxayb', 'cxyab', 'cyxab', 'cayxb', 'cyabx',
    'cxayb', 'cyaxb',
)

def halve(shape):
    rows, cols = shape
    if rows % 16 == 0: return 0
    if cols % 256 == 0: return 1
    return None

def bits_of(nb, nd):
    return ([("bucket",i) for i in range(int(math.log2(nb)))]
            + [("dp",i) for i in range(int(math.log2(nd)))])

def level_orders(nb, nd):
    bk=[("bucket",i) for i in range(int(math.log2(nb)))]
    dp=[("dp",i) for i in range(int(math.log2(nd)))]
    a=bk[:1]+dp[:2]+bk[1:]+dp[2:]
    b=bk[:1]+bk[1:]+dp[1:2]+dp[:1]+dp[2:]
    return a,b

class Job:
    def __init__(self, chunk, part, out, place, local, shape, order):
        self.chunk=chunk; self.part=part; self.out=out; self.place=place; self.local=local
        self.levels=[]
        for bit in order:
            d=halve(shape)
            after=list(shape)
            if d is not None: after[d]//=2
            self.levels.append((bit,d,tuple(shape),tuple(after)))
            shape=tuple(after)

def make_jobs(chunks, nb, nd):
    orders=level_orders(nb,nd)
    named=dict(c=("bucket",0),y=("bucket",1),x=("dp",0),a=("dp",1),b=("dp",2))
    chosen=[[named[n] for n in word] for word in ORDERS] if (nb,nd)==(4,8) else []
    jobs=[]
    for c,(out,r,k,rows,cols) in enumerate(chunks):
        for p in range(2):
            local=p*(rows//2)
            jobs.append(Job(c,p,out,(r+local,k),local,(rows//2,cols),chosen[2*c+p] if chosen else orders[p]))
    return jobs

class Links:
    def __init__(self): self.free={}
    def end(self, bit, size, t):
        if bit==("dp",2):
            mid,low=self.free.get(bit,0.0),self.free.get(("dp",1),0.0)
            start=max(t,mid,low)
            self.free[("dp",1)]=max(t,low)+size/RATE
            self.free[bit]=start+size/RATE*2
            return start+size/RATE*2+LATENCY
        rate=600e3 if bit==("bucket",0) else RATE
        start=max(t,self.free.get(bit,0.0))
        self.free[bit]=start+size/rate
        return self.free[bit]+LATENCY

def schedule(jobs, steps, ring, shares):
    links=Links(); heap=[]; items=[]; done=set(); now=0.0
    of_chunk={}
    for k,j in enumerate(jobs): of_chunk.setdefault(j.chunk,[]).append(k)
    def issue(k,s,t):
        L=len(jobs[k].levels)
        bit,d,before,after=jobs[k].levels[s if s<L else 2*L-1-s]
        end=t if (s>=L and d is None) else links.end(bit,4*after[0]*after[1],t)
        heapq.heappush(heap,(end,k,s))
    def one(t):
        end,k,s=heapq.heappop(heap)
        t=max(t,end)+ENDS[s>=len(jobs[k].levels)]
        items.append(("end",k,s)); done.add((k,s))
        if s+1<2*len(jobs[k].levels): issue(k,s+1,t)
        return t
    for i,(chunk,us) in enumerate(steps):
        n=0
        while heap and heap[0][0]<=now and n<CAP: now=one(now); n+=1
        if chunk is not None:
            need=[(k,0) for k in of_chunk.get(chunk-ring,[])] if us>0 and chunk+1<len(of_chunk) else []
            if chunk in shares:
                need+=[(k,2*len(jobs[k].levels)-1) for k in of_chunk[shares[chunk]]]
            while not all(n in done for n in need): now=one(now)
        items.append(("step",i)); now+=us
        if chunk is not None:
            for k in of_chunk[chunk]: issue(k,0,now)
    while heap: now=one(now)
    return items,now

class Place:
    def __init__(self, bits):
        me={n: lax.axis_index(n) for n in ("bucket","dp")}
        self.bit={(n,i): lax.rem(lax.div(me[n],1<<i),2) for n,i in bits}
        self.partner={(n,i): tuple(me[m]+(1-2*self.bit[n,i])*(1<<i) if m==n else me[m] for m in me) for n,i in bits}

def span(start,size,by):
    return pl.ds(start if isinstance(start,int) else pl.multiple_of(start,by),size)

def region(ref, off, shape):
    return ref.at[span(off[0],shape[0],8),span(off[1],shape[1],128)]

def add_rows(dst, a, b, shape):
    rows,cols=shape
    rb=8
    while rows%(rb*2)==0 and rb*2*cols<=32*1024: rb*=2
    def one(i,_):
        at=pl.ds(pl.multiple_of(i*rb,8),rb)
        dst[at,:]=a[at,:]+b[at,:]
        return 0
    lax.fori_loop(0,rows//rb,one,0)

class Run:
    def __init__(self, place, job, src, out, acc, recv, ss, rs, ls, credit=None, give=False, take=False):
        self.at=place; self.j=job; self.src=src; self.out=out; self.acc=acc; self.recv=recv
        self.ss=ss; self.rs=rs; self.ls=ls
        self.credit=credit; self.give=give; self.take=take
        self.n=len(job.levels)
        split=[s for s in range(2*self.n) if self.level(s)[1] is not None]
        self.store_at=min(s for s in split if s>=self.n)+1
        self.out_rows=sum(self.level(s)[3][0]*self.level(s)[3][1] for s in split[1:])//job.levels[0][2][1]
    def level(self, s):
        return self.j.levels[s if s<self.n else 2*self.n-1-s]
    def slot(self, s):
        return s if s==0 or self.level(s)[1] is None else 2*self.n-1
    def offset(self, first, last):
        off=[0,0]
        for bit,d,before,after in self.j.levels[first:last+1]:
            if d is not None: off[d]=off[d]+self.at.bit[bit]*after[d]
        return off
    def given(self, s, off):
        bit,d,before,after=self.j.levels[s]
        off=list(off); off[d]=off[d]+(1-self.at.bit[bit])*after[d]
        return off
    def piece(self, lv):
        off=self.offset(0,lv)
        return [self.j.place[0]+off[0],self.j.place[1]+off[1]]
    def local(self):
        after=self.level(self.n)[3]
        return pltpu.make_async_copy(region(self.acc,self.offset(1,self.n-1),after),
                                     region(self.out,self.piece(self.n-1),after),self.ls.at[0])
    def remote(self, s):
        bit,d,before,after=self.level(s)
        if s==0:
            src,dst=region(self.src,self.given(0,[self.j.local,0]),after),self.recv[0]
        elif s<self.n:
            off=self.offset(1,s-1)
            src,dst=region(self.acc,off if d is None else self.given(s,off),after),self.recv[s]
        else:
            dst=region(self.out,self.piece(2*self.n-1-s),after)
            first=all(self.level(i)[1] is None for i in range(self.n,s))
            src=region(self.acc,self.offset(1,self.n-1),after) if first else dst
        return pltpu.make_async_remote_copy(src_ref=src,dst_ref=dst,send_sem=self.ss.at[self.slot(s)],recv_sem=self.rs.at[s],
                                            device_id=self.at.partner[bit],device_id_type=MESH)
    def start(self, s):
        bit,d,before,after=self.level(s)
        if s==self.n: self.local().start()
        if s>=self.n and d is None: return
        if s==self.store_at: self.local().wait()
        if s==0 and self.take: pl.semaphore_wait(self.credit,1)
        self.remote(s).start()
    def finish(self, s):
        bit,d,before,after=self.level(s)
        if s>=self.n:
            if d is not None: self.remote(s).wait_recv()
        else:
            if d is None: self.remote(s).wait()
            else: self.remote(s).wait_recv()
            to=region(self.acc,self.offset(1,s),after)
            own=region(self.src,[self.j.local+self.offset(0,0)[0],0],after) if s==0 else to
            add_rows(to,own,self.recv[s],after)
            if s==0 and self.give:
                pl.semaphore_signal(self.credit,inc=1,device_id=self.at.partner[bit],device_id_type=MESH)
        if s+1<2*self.n: self.start(s+1)
        else: self.close()
    def sent(self):
        self.remote(0).wait_send()
    def close(self):
        if self.store_at==2*self.n: self.local().wait()
        if not self.give: self.sent()
        sent=region(self.out,(0,0),(self.out_rows,self.j.levels[0][2][1]))
        pltpu.make_async_remote_copy(src_ref=sent,dst_ref=sent,send_sem=self.ss.at[2*self.n-1],recv_sem=self.rs.at[0],
                                     device_id=self.at.partner[self.j.levels[0][0]],device_id_type=MESH).wait_send()

RING=2

def back_kernel(plan,*refs):
    (jobs,items,nchunk,nf,nhead,nblk,nrow,shares,bits,norm)=plan
    refs=list(refs)
    def take(n):
        out=refs[:n]; del refs[:n]; return out
    (wt,g,du,dm,c,at_h,db,a,w)=take(9)
    (q,k,v,do,at,lse,qu,ku,qr,kr)=take(10)
    (seg,qg,mid,x,dh,ng)=take(6)
    outs=take(5)
    (tg_o,)=take(1)
    (pool,stage,l0,dqkv,dq_s,dk_s,dv_s,kt_s,small,kc,qc,s_s,dp_s,p_s,ds_s)=take(15)
    (pool_sem,credit)=take(2)
    t,d=at_h.shape
    ob=t//nblk; tb=64
    own=nchunk-len(shares)-1
    bufs=[]
    for n in range(own+1):
        pair=[]
        for p in range(2):
            L=len(jobs[2*(n if n<own else nchunk-1)+p].levels)
            pair.append((take(1)[0],take(L-1 if n<own else L)))
        bufs.append(pair)
    place=Place(bits)
    runs=[]
    for n,j in enumerate(jobs):
        ss,rs,ls=take(3)
        if j.chunk==nchunk-1:
            acc,recv=bufs[own][j.part]
            runs.append(Run(place,j,small,outs[j.out],acc,recv,ss,rs,ls))
        else:
            acc,recv=bufs[shares.get(j.chunk,j.chunk)][j.part]
            runs.append(Run(place,j,stage.at[j.chunk%RING],outs[j.out],acc,[l0.at[2*(j.chunk%RING)+j.part]]+list(recv),ss,rs,ls,
                            credit.at[j.part],give=j.chunk+RING<nchunk-1,take=j.chunk>=RING))
    pid=pl.program_id(0)
    def col(ref,f): return ref.at[:,pl.ds(f*d,d)]
    names={"g":g,"du":du,"dm":dm,"c":c,"at":at_h,"db":db,"a":a,"w":w}
    plan_l=[]
    for f in range(nf): plan_l.append((("g",f),0 if f%2==0 else 2,1,True))
    for f in range(nf): plan_l.append((("du",f),0 if (nf+f)%2==0 else 2,3,False))
    load={i:[] for i in range(-1,2*nf+2)}
    load[-1]+= [(("dm",0),1),(("c",0),3)]
    for i,(what,s,other,_) in enumerate(plan_l):
        load[max(i-2,-1)].append((what,s))
    n0=2*nf+1
    s_at=0 if (2*nf)%2==0 else 2
    load[2*nf-2].append((("at",0),s_at))
    load[nf].append((("db",0),1))
    load[2*nf-1].append((("a",0),3))
    load[2*nf]+= [(("w",0),0),(("w",1),1),(("w",2),2)]
    def copy_of(what,s):
        name,f=what
        if name=="w": return pltpu.make_async_copy(col(w,f),pool.at[s,pl.ds(0,d),:],pool_sem.at[s])
        if name in ("g","du"): return pltpu.make_async_copy(col(names[name],f),pool.at[s],pool_sem.at[s])
        return pltpu.make_async_copy(names[name],pool.at[s],pool_sem.at[s])
    waiting={}
    def fetch_after(i):
        for what,s in load.get(i,[]):
            copy_of(what,s).start(); waiting[s]=what
    def ready(s):
        if s in waiting: copy_of(waiting.pop(s),s).wait()
    total=wt[0]
    for n in range(1,wt.shape[0]): total=total+wt[n]
    scale=wt[lax.axis_index("bucket")].astype(F32)/(total.astype(F32)*norm)
    steps=[]
    for i,(what,s,other,first) in enumerate(plan_l): steps.append(("w",i,s,other) if first else ("w",i,other,s))
    steps.append(("w",2*nf,s_at,1))
    for h in range(nhead): steps.append(("h",h))
    for n in range(3): steps.append(("x",n))
    for r in range(nrow): steps.append(("r",r))
    n_h=n0; n_x=n0+nhead; n_r=n_x+3; n_end=n_r+nrow

    def weight_step(chunk,lhs,rhs):
        if chunk>=RING:
            for p in range(2): runs[2*(chunk-RING)+p].sent()
        stage[chunk%RING]=scale*mm(lhs,rhs,0,0)
        for p in range(2): runs[2*chunk+p].start(0)

    def before(i):
        for it in segments[i]: runs[it[1]].finish(it[2])
    segments=[[]]
    for it in items:
        if it[0]=="step": segments.append([])
        else: segments[-1].append(it)
    inner={h: segments[n_h+h*nblk:n_h+(h+1)*nblk] for h in range(nhead)}
    segments=segments[:n_h]+[inner[h][0] for h in range(nhead)]+segments[n_h+nhead*nblk:]
    for i,st in enumerate(steps+[("end",)]):
        kind=st[0]
        need = segments[i] or kind in ("w","x","end") or i==0 or i==n_r
        if not need: continue
        @pl.when(pid==i)
        def _(i=i,st=st,kind=kind):
            if i==0:
                sem=pltpu.get_barrier_semaphore()
                for bit in bits:
                    pl.semaphore_signal(sem,inc=1,device_id=place.partner[bit],device_id_type=MESH)
                pl.semaphore_wait(sem,len(bits))
                fetch_after(-1)
                kc[...],qc[...]=segment_codes(column(seg[...].astype(F32),2*HD),t)
                small[...]=jnp.zeros_like(small)
                small[3:3+nf+2,:]=scale*mid[0:nf+2,:]
                small[nf+6:nf+7,:]=scale*mid[nf+2:nf+3,:]
                small[nf+8:nf+9,:]=scale*mid[nf+3:nf+4,:]
            before(i)
            if kind=="w":
                _,n,ls_,rs_=st
                ready(ls_); ready(rs_)
                weight_step(n,pool[ls_],pool[rs_])
                fetch_after(n)
            elif kind=="x":
                n=st[1]
                if n==0:
                    for s in range(4): ready(s)
                weight_step(n0+n,pool[3],dqkv[:,n*d:(n+1)*d])
            elif kind=="end":
                pass
    @pl.when((pid>=n_h)&(pid<n_x))
    def _():
        hp=pid-n_h
        lanes=pl.ds(pl.multiple_of(hp*2*HD,2*HD),2*HD)
        kt_s[...]=k[...].T
        lane=lax.broadcasted_iota(jnp.int32,(1,2*HD),1)//HD
        half=lax.broadcasted_iota(jnp.int32,(8,2*HD),1)//HD
        pick=jnp.where(half==lax.broadcasted_iota(jnp.int32,(8,2*HD),0),1.0,0.0).astype(BF)
        for ib in range(nblk):
            for h in range(nhead):
                if ib>0 and inner[h][ib]:
                    @pl.when(hp==h)
                    def _(h=h):
                        for it in inner[h][ib]: runs[it[1]].finish(it[2])
            rows=slice(ib*ob,(ib+1)*ob)
            dd=do[rows,:].astype(F32)*at[rows,:].astype(F32)
            hi=dd.astype(BF); rest=dd-hi.astype(F32); mid_=rest.astype(BF); low=(rest-mid_.astype(F32)).astype(BF)
            delta=mm(pick,hi,1,1)+(mm(pick,mid_,1,1)+mm(pick,low,1,1))
            dqs=[]
            for h in range(2):
                s_s[h]=mm(jnp.where(lane==h,k[...],kc[...]),jnp.where(lane==h,q[rows,:],qc[rows,:]),1,1)
                dp_s[h]=mm(v[...],jnp.where(lane==h,do[rows,:],0),1,1)
            for h in range(2):
                top,dl=lse[0,h:h+1,rows],delta[h:h+1,:]
                for n in range(t//tb):
                    at_n=slice(n*tb,(n+1)*tb)
                    p=jnp.exp(s_s[h,at_n,:]-top)
                    p_s[h,at_n,:]=p.astype(BF)
                    ds_s[h,at_n,:]=(p*(dp_s[h,at_n,:]-dl)).astype(BF)
                dvp=mm(p_s[h],jnp.where(lane==h,do[rows,:],0))
                dkp=mm(ds_s[h],jnp.where(lane==h,q[rows,:],0))
                if ib==0 and h==0: dv_s[...]=dvp; dk_s[...]=dkp
                else: dv_s[...]+=dvp; dk_s[...]+=dkp
                dqs.append(mm(kt_s[h*HD:(h+1)*HD,:],ds_s[h]))
            dq_s[rows,:]=jnp.concatenate(dqs,axis=0).T*(1.0/math.sqrt(HD))
        m=avg_matrix()[:2*HD,:2*HD]
        def avg(y):
            yh=y.astype(BF)
            return mm(yh,m)+mm((y-yh.astype(F32)).astype(BF),m)
        gains=per_head(qg,2)
        for n,(gr,un,rr) in enumerate(((dq_s,qu,qr),(dk_s,ku,kr))):
            gg=gr[...]; u=un[...].astype(F32)
            e=gg*gains[n:n+1,:]
            back=(rr[...]*(e-avg(e)-u*avg(e*u))).astype(BF)
            dqkv[:,pl.ds(pl.multiple_of(n*d+hp*2*HD,2*HD),2*HD)]=back
            small[n:n+1,lanes]=scale*jnp.sum(back.astype(F32),axis=0,keepdims=True)
            small[nf+9+n:nf+10+n,lanes]=scale*jnp.sum(gg*u,axis=0,keepdims=True)
            small[nf+11+n:nf+12+n,lanes]=scale*jnp.sum(gg,axis=0,keepdims=True)
        back=dv_s[...].astype(BF)
        dqkv[:,pl.ds(pl.multiple_of(2*d+hp*2*HD,2*HD),2*HD)]=back
        small[2:3,lanes]=scale*jnp.sum(back.astype(F32),axis=0,keepdims=True)
    @pl.when((pid>=n_r)&(pid<n_end))
    def _():
        rb=x.shape[0]
        rows=pl.ds(pl.multiple_of((pid-n_r)*rb,rb),rb)
        da=mm(dqkv[rows,0:d],pool[0,:d,:],1,1)+mm(dqkv[rows,d:2*d],pool[1,:d,:],1,1)+mm(dqkv[rows,2*d:],pool[2,:d,:],1,1)
        unit,r=row_norm(x[...].astype(F32))
        e=da*ng[0:1,:]
        tg_o[...]=dh[...]+r*(e-jnp.mean(e,axis=-1,keepdims=True)-unit*jnp.mean(e*unit,axis=-1,keepdims=True))
        small[nf+5:nf+6,:]+=scale*jnp.sum(da*unit,axis=0,keepdims=True)
        small[nf+7:nf+8,:]+=scale*jnp.sum(da,axis=0,keepdims=True)
        @pl.when(pid==n_end-1)
        def _():
            for p in range(2): runs[2*(nchunk-1)+p].start(0)

def backward(wt,g,du,dm,c,at,db,a,w,q,k,v,do,lse,qu,ku,qr,kr,seg,qg,mid,x,dh,ng,nb,nd,ob=256,rb=256):
    t,d=x.shape; ff=g.shape[1]; nf=ff//d
    nhead=d//(2*HD); nblk=t//ob; nrow=t//rb
    n0=2*nf+1
    chunks=[(0,f*d,0,d,d) for f in range(nf)]+[(1,0,f*d,d,d) for f in range(nf)]+[(2,0,0,d,d)]
    chunks+=[(3,0,n*d,d,d) for n in range(3)]+[(4,0,0,32,d)]
    nchunk=len(chunks)
    shares={} if (nb,nd)==(4,8) else {n0+n:n for n in range(3)}
    jobs=make_jobs(chunks,nb,nd)
    steps=[(n,2.2) for n in range(n0)]+[(None,2.1)]*(nhead*nblk)+[(n0+n,2.2) for n in range(3)]+[(None,2.6)]*(nrow-1)+[(nchunk-1,2.6)]
    items,_=schedule(jobs,steps,RING,shares)
    bits=bits_of(nb,nd)
    n_h=n0; n_x=n0+nhead; n_r=n_x+3; n_end=n_r+nrow
    def head(i): return jnp.clip(i-n_h,0,nhead-1)
    def block(i): return jnp.clip(i-n_r,0,nrow-1)
    any_=pl.BlockSpec(memory_space=pltpu.HBM)
    colspec=pl.BlockSpec((t,2*HD),lambda i:(0,head(i)))
    rows=pl.BlockSpec((rb,d),lambda i:(block(i),0))
    in_specs=[pl.BlockSpec(memory_space=pltpu.SMEM)]+[any_]*8+[colspec]*5+[pl.BlockSpec((1,2,t),lambda i:(head(i),0,0))]+[colspec]*4
    in_specs+=[whole(seg),whole(qg),whole(mid),rows,rows,whole(ng)]
    out_specs=[any_]*5+[rows]
    S=jax.ShapeDtypeStruct
    out_shape=[S((ff,d),F32),S((d,ff),F32),S((d,d),F32),S((d,3*d),F32),S((32,d),F32),S((t,d),F32)]
    half=(d//2)//2
    scratch=[pltpu.VMEM((4,t,d),BF),pltpu.VMEM((RING,d,d),F32),pltpu.VMEM((2*RING,half,d),F32),pltpu.VMEM((t,3*d),BF)]
    scratch+=[pltpu.VMEM((t,2*HD),F32)]*3+[pltpu.VMEM((2*HD,t),BF),pltpu.VMEM((32,d),F32),pltpu.VMEM((t,2*HD),BF),pltpu.VMEM((t,2*HD),BF),pltpu.VMEM((2,t,ob),F32),pltpu.VMEM((2,t,ob),F32),pltpu.VMEM((2,t,ob),BF),pltpu.VMEM((2,t,ob),BF),pltpu.SemaphoreType.DMA((4,)),pltpu.SemaphoreType.REGULAR((2,))]
    own=nchunk-len(shares)-1
    for n in range(own+1):
        small=n==own
        for p in range(2):
            j=jobs[2*(nchunk-1 if small else n)+p]
            scratch.append(pltpu.VMEM(j.levels[0][3],F32))
            for lv in j.levels[0 if small else 1:]: scratch.append(pltpu.VMEM(lv[3],F32))
    for j in jobs:
        L=len(j.levels)
        scratch+=[pltpu.SemaphoreType.DMA((2*L,)),pltpu.SemaphoreType.DMA((2*L,)),pltpu.SemaphoreType.DMA((1,))]
    plan=(jobs,items,nchunk,nf,nhead,nblk,nrow,shares,bits,math.sqrt(t*nd))
    return pl.pallas_call(functools.partial(back_kernel,plan),grid=(n_end+1,),in_specs=in_specs,out_specs=out_specs,out_shape=out_shape,
        scratch_shapes=scratch,
        compiler_params=pltpu.CompilerParams(collective_id=7,has_side_effects=True,vmem_limit_bytes=63<<20),name="backward")(
        wt,g,du,dm,c,at,db,a,w,q,k,v,do,at,lse,qu,ku,qr,kr,seg,qg,mid,x,dh,ng)

def finish_kernel(nf,f2,f1,fo,fq,tg,small,f2_o,f1_o,fo_o,fq_o,tg_o,bq_o,bo_o,b1_o,b2_o,gain_o,shift_o,hg_o,hs_o):
    for src,dst in ((f2,f2_o),(f1,f1_o),(fo,fo_o),(fq,fq_o),(tg,tg_o)): dst[...]=src[...]
    d=small.shape[1]
    @pl.when(pl.program_id(0)==0)
    def _():
        for i in range(3): bq_o[i*d:(i+1)*d]=small[i,:]
        bo_o[...]=small[3,:]
        for i in range(nf): b1_o[i*d:(i+1)*d]=small[4+i,:]
        b2_o[...]=small[4+nf,:]
        gain_o[...]=small[5+nf:7+nf,:]
        shift_o[...]=small[7+nf:9+nf,:]
        for n,o in enumerate((hg_o,hs_o)):
            wide=small[9+nf+2*n:11+nf+2*n,:]
            pair=wide[:,:2*HD]
            for i in range(1,d//(2*HD)): pair=pair+wide[:,2*HD*i:2*HD*(i+1)]
            o[...]=pair[:,:HD]+pair[:,HD:]

def finish(f2,f1,fo,fq,tg,small,n=4):
    ff,d=f2.shape; nf=ff//d
    S=jax.ShapeDtypeStruct
    wide=[pl.BlockSpec((a.shape[0]//n,a.shape[1]),lambda i:(i,0)) for a in (f2,f1,fo,fq,tg)]
    big=[S(a.shape,F32) for a in (f2,f1,fo,fq,tg)]
    rest=[S((3*d,),F32),S((d,),F32),S((ff,),F32),S((d,),F32),S((2,d),F32),S((2,d),F32),S((2,HD),F32),S((2,HD),F32)]
    return pl.pallas_call(functools.partial(finish_kernel,nf),grid=(n,),
        in_specs=wide+[whole(small)],
        out_specs=wide+[whole(a) for a in rest],
        out_shape=big+rest,compiler_params=pltpu.CompilerParams(vmem_limit_bytes=VM),name="finish")(f2,f1,fo,fq,tg,small)


def body(
    tokens,
    segment,
    live,
    group_patches,
    qkv_weight,
    qkv_bias,
    out_weight,
    out_bias,
    fc1_weight,
    fc1_bias,
    fc2_weight,
    fc2_bias,
    norm_gain,
    norm_shift,
    qk_gain,
    qk_shift,
    cotangent,
):
    a_low, q_low, k_low, v_low, q_unit, k_unit, q_inv, k_inv = qkv_forward(
        tokens, qkv_weight, qkv_bias, norm_gain, norm_shift, qk_gain, qk_shift
    )
    attn_low, lse = attend_forward(q_low, k_low, v_low, segment)
    out, dhid, dattn, g_low, du_low, dm_low, c_low, db_low, mid_sums = mlp(
        tokens,
        cotangent,
        live[None],
        attn_low,
        out_weight,
        out_bias,
        fc1_weight,
        fc1_bias,
        fc2_weight,
        fc2_bias,
        norm_gain,
        norm_shift,
    )
    fc2_grad, fc1_grad, out_grad, qkv_grad, small, tokens_grad = backward(
        group_patches, g_low, du_low, dm_low, c_low, attn_low, db_low, a_low, qkv_weight,
        q_low, k_low, v_low, dattn, lse, q_unit, k_unit, q_inv, k_inv,
        segment[None], qk_gain, mid_sums, tokens, dhid, norm_gain,
        lax.axis_size("bucket"), lax.axis_size("dp"),
    )
    (fc2_grad, fc1_grad, out_grad, qkv_grad, tokens_grad, qkv_b, out_b, fc1_b, fc2_b, n_gain, n_shift, h_gain, h_shift) = finish(
        fc2_grad, fc1_grad, out_grad, qkv_grad, tokens_grad, small
    )
    return (
        out, tokens_grad, qkv_grad, qkv_b, out_grad, out_b, fc1_grad, fc1_b, fc2_grad, fc2_b,
        n_gain, n_shift, h_gain, h_shift,
    )


def solution(mesh):
    return jax.shard_map(
        body,
        mesh=mesh,
        in_specs=(
            P(("bucket", "dp"), None),
            P(("bucket", "dp")),
            P(("bucket", "dp")),
            *((P(),) * 13),
            P(("bucket", "dp"), None),
        ),
        out_specs=(P(("bucket", "dp"), None), P(("bucket", "dp"), None), *((P(),) * 12)),
        check_vma=False,
    )
```

```python
import functools
import heapq
import math

import jax
import jax.numpy as jnp
from jax import lax
from jax.experimental import pallas as pl
from jax.experimental.pallas import tpu as pltpu
from jax.sharding import PartitionSpec as P

F32=jnp.float32; BF=jnp.bfloat16
EPSILON=1e-6
NEG=-1e30
HD=64
VM=58<<20

def mm(a,b,ca=1,cb=0):
    return lax.dot_general(a,b,(((ca,),(cb,)),((),())),preferred_element_type=F32)

def row_norm(x):
    c=x-jnp.mean(x,axis=-1,keepdims=True)
    r=lax.rsqrt(jnp.mean(c*c,axis=-1,keepdims=True)+EPSILON)
    return c*r,r

def head_avg(x,m,twice):
    out=[]
    for i in range(x.shape[1]//256):
        part=x[:,256*i:256*(i+1)]
        hi=part.astype(BF)
        s=mm(hi,m)
        if twice: s=s+mm((part-hi.astype(F32)).astype(BF),m)
        out.append(s)
    return jnp.concatenate(out,axis=1)

def avg_matrix():
    i=lax.broadcasted_iota(jnp.int32,(256,256),0)//HD
    j=lax.broadcasted_iota(jnp.int32,(256,256),1)//HD
    return jnp.where(i==j,1.0/HD,0.0).astype(BF)

def row(ref):
    return ref[...][None,:]

def column(values, lanes):
    return jnp.broadcast_to(values,(lanes,values.shape[1])).T

def per_head(ref, times):
    return jnp.concatenate([ref[...]]*times,axis=1)

def whole(a):
    nd=len(a.shape)
    return pl.BlockSpec(a.shape,lambda *_:(0,)*nd,pipeline_mode=pl.Buffered(1))

def qkv_kernel(x,w,b,ng,ns,qg,qs,a_o,q_o,k_o,v_o,qu_o,ku_o,qr_o,kr_o):
    d=x.shape[1]
    gains=per_head(qg,d//HD); shifts=per_head(qs,d//HD)
    bias=row(b)
    u,_=row_norm(x[...].astype(F32))
    a=(u*ng[0:1,:]+ns[0:1,:]).astype(BF)
    a_o[...]=a
    m=avg_matrix()
    for i,(lo,un,rr) in enumerate(((q_o,qu_o,qr_o),(k_o,ku_o,kr_o))):
        raw=mm(a,w[:,i*d:(i+1)*d])+bias[:,i*d:(i+1)*d]
        c=raw-head_avg(raw,m,True)
        r=lax.rsqrt(head_avg(c*c,m,False)+EPSILON)
        unit=c*r
        un[...]=unit.astype(BF)
        rr[...]=r
        n=unit*gains[i:i+1,:]+shifts[i:i+1,:]
        if i==0: n=n*(1.0/math.sqrt(HD))
        lo[...]=n.astype(BF)
    v_o[...]=(mm(a,w[:,2*d:])+bias[:,2*d:]).astype(BF)

def qkv_forward(x,w,b,ng,ns,qg,qs,rb=256):
    t,d=x.shape
    rows=pl.BlockSpec((rb,d),lambda i:(i,0))
    sh=lambda dt: jax.ShapeDtypeStruct((t,d),dt)
    return pl.pallas_call(qkv_kernel,grid=(t//rb,),
        in_specs=[rows,whole(w),whole(b),whole(ng),whole(ns),whole(qg),whole(qs)],
        out_specs=[rows]*8,
        out_shape=[sh(BF)]*6+[sh(F32)]*2,
        compiler_params=pltpu.CompilerParams(vmem_limit_bytes=VM),name="norm_qkv")(x,w,b,ng,ns,qg,qs)

BIG=384.0

def segment_codes(col, count):
    bits=(count-1).bit_length()
    at=lax.rem(lax.broadcasted_iota(jnp.int32,col.shape,1),HD)
    bit=lax.shift_right_logical(col.astype(jnp.int32),jnp.minimum(at,bits))&1
    sign=jnp.where(at<bits,(2*bit-1).astype(F32),0.0)
    key=jnp.where(at==bits,1.0,sign)
    query=jnp.where(at==bits,-BIG*bits,BIG*sign)
    return key.astype(BF),query.astype(BF)

def attend_kernel(q,k,v,seg,o,lse,kc,qc,s_s,p_s,ob=512,tb=32):
    t=q.shape[0]
    @pl.when(pl.program_id(0)==0)
    def _(): kc[...],qc[...]=segment_codes(column(row(seg).astype(F32),2*HD),t)
    vt=v[...].T
    lane=lax.broadcasted_iota(jnp.int32,(1,2*HD),1)//HD
    keys=[jnp.where(lane==h,k[...],kc[...]) for h in range(2)]
    for i in range(t//ob):
        rows=slice(i*ob,(i+1)*ob)
        parts=[]
        for h in range(2):
            s_s[h]=mm(keys[h],jnp.where(lane==h,q[rows,:],qc[rows,:]),1,1)
        for h in range(2):
            top=s_s[h,:tb,:]
            for n in range(1,t//tb): top=jnp.maximum(top,s_s[h,n*tb:(n+1)*tb,:])
            m=jnp.max(top,axis=0,keepdims=True)
            total=jnp.zeros((tb,ob),F32)
            for n in range(t//tb):
                p=jnp.exp(s_s[h,n*tb:(n+1)*tb,:]-m)
                total=total+p
                p_s[h,n*tb:(n+1)*tb,:]=p.astype(BF)
            l=jnp.sum(total,axis=0,keepdims=True)
            lse[0,h:h+1,rows]=m+jnp.log(l)
            parts.append(mm(vt[h*HD:(h+1)*HD,:],p_s[h])*(1.0/l))
        o[rows,:]=jnp.concatenate(parts,axis=0).T.astype(BF)

def attend_forward(q,k,v,seg):
    t,d=q.shape
    hp=d//(2*HD)
    col=pl.BlockSpec((t,2*HD),lambda h:(0,h))
    return pl.pallas_call(attend_kernel,grid=(hp,),
        in_specs=[col,col,col,whole(seg)],
        out_specs=[col,pl.BlockSpec((1,2,t),lambda h:(h,0,0))],
        out_shape=[jax.ShapeDtypeStruct((t,d),BF),jax.ShapeDtypeStruct((hp,2,t),F32)],
        scratch_shapes=[pltpu.VMEM((t,2*HD),BF)]*2+[pltpu.VMEM((2,t,512),F32),pltpu.VMEM((2,t,512),BF)],
        compiler_params=pltpu.CompilerParams(vmem_limit_bytes=VM),name="attend")(q,k,v,seg)

def mlp_kernel(nf,x,cot,live,attn,wo,bo,w1,b1,w2,b2,ng,ns,
               out_o,dhid_o,dattn_o,g_o,du_o,dm_o,c_o,db_o,small_o,pre_s,dg_s,tb=16):
    i=pl.program_id(0)
    rb,d=x.shape
    hid=x[...].astype(F32)+mm(attn[...],wo[...])+row(bo)
    unit,r=row_norm(hid)
    c=(unit*ng[1:2,:]+ns[1:2,:]).astype(BF)
    c_o[...]=c
    lv=column(live[:,pl.ds(pl.multiple_of(i*rb,rb),rb)].astype(F32),8)[:,:1]
    fc1_bias=row(b1)
    dm=cot[...].astype(F32)*lv
    dml=dm.astype(BF)
    dm_o[...]=dml
    out=jnp.zeros((rb,d),F32); dc=jnp.zeros((rb,d),F32)
    sums=[]
    for f in range(nf):
        cols=slice(f*d,(f+1)*d)
        pre_s[...]=mm(c,w1[:,cols])
        dg_s[...]=mm(dml,w2[cols,:],1,1)
        total=jnp.zeros((tb,d),F32)
        for n in range(rb//tb):
            at=slice(n*tb,(n+1)*tb)
            pre=pre_s[at,:]+fc1_bias[:,cols]
            phi=0.5*(1.0+lax.erf(pre*(1.0/math.sqrt(2.0))))
            slope=phi+pre*jnp.exp(-0.5*pre*pre)*(1.0/math.sqrt(2.0*math.pi))
            du=(dg_s[at,:]*slope).astype(BF)
            g_o[at,cols]=(pre*phi).astype(BF)
            du_o[at,cols]=du
            total=total+du.astype(F32)
        g,du=g_o[:,cols],du_o[:,cols]
        out=out+mm(g,w2[cols,:])
        dc=dc+mm(du,w1[:,cols],1,1)
        sums.append(jnp.sum(total,axis=0,keepdims=True))
    out_o[...]=(lv*(hid+out+row(b2))).astype(BF)
    e=dc*ng[1:2,:]
    dh=dm+r*(e-jnp.mean(e,axis=-1,keepdims=True)-unit*jnp.mean(e*unit,axis=-1,keepdims=True))
    dhid_o[...]=dh
    db=dh.astype(BF)
    db_o[...]=db
    dattn_o[...]=mm(db,wo[...],1,1).astype(BF)
    total=jnp.concatenate([jnp.sum(db.astype(F32),axis=0,keepdims=True)]+sums+[jnp.sum(dm,axis=0,keepdims=True),
        jnp.sum(dc*unit,axis=0,keepdims=True),jnp.sum(dc,axis=0,keepdims=True)],axis=0)
    @pl.when(i==0)
    def _(): small_o[...]=total
    @pl.when(i>0)
    def _(): small_o[...]+=total

def mlp(x,cot,live,attn,wo,bo,w1,b1,w2,b2,ng,ns,rb=256):
    t,d=x.shape; ff=w1.shape[1]; nf=ff//d
    rows=pl.BlockSpec((rb,d),lambda i:(i,0))
    wide=pl.BlockSpec((rb,ff),lambda i:(i,0))
    low=jax.ShapeDtypeStruct((t,d),BF)
    big=jax.ShapeDtypeStruct((t,ff),BF)
    return pl.pallas_call(functools.partial(mlp_kernel,nf),grid=(t//rb,),
        in_specs=[rows,rows,whole(live),rows]+[whole(a) for a in (wo,bo,w1,b1,w2,b2,ng,ns)],
        out_specs=[rows,rows,rows,wide,wide,rows,rows,rows,pl.BlockSpec((nf+4,d),lambda i:(0,0))],
        out_shape=[low,jax.ShapeDtypeStruct((t,d),F32),low,big,big,low,low,low,jax.ShapeDtypeStruct((nf+4,d),F32)],
        scratch_shapes=[pltpu.VMEM((rb,d),F32)]*2,
        compiler_params=pltpu.CompilerParams(vmem_limit_bytes=VM),name="mlp")(x,cot,live,attn,wo,bo,w1,b1,w2,b2,ng,ns)

MESH = pl.DeviceIdType.MESH
RATE=45e3
LATENCY=1.6
ENDS=(0.45,0.3)
CAP=99
ORDERS=(
    'cxyab', 'cyaxb', 'cayxb', 'cyxab', 'cxayb', 'caxyb', 'cxayb', 'cyabx',
    'cxayb', 'cyaxb', 'cxayb', 'cyaxb', 'cyaxb', 'cxyab', 'cxyab', 'cyxab',
    'cxyab', 'cyxab', 'cxayb', 'cxayb', 'cxyab', 'cyxab', 'cayxb', 'cyabx',
    'cxayb', 'cyaxb',
)

def halve(shape):
    rows, cols = shape
    if rows % 16 == 0: return 0
    if cols % 256 == 0: return 1
    return None

def bits_of(nb, nd):
    return ([("bucket",i) for i in range(int(math.log2(nb)))]
            + [("dp",i) for i in range(int(math.log2(nd)))])

def level_orders(nb, nd):
    bk=[("bucket",i) for i in range(int(math.log2(nb)))]
    dp=[("dp",i) for i in range(int(math.log2(nd)))]
    a=bk[:1]+dp[:2]+bk[1:]+dp[2:]
    b=bk[:1]+bk[1:]+dp[1:2]+dp[:1]+dp[2:]
    return a,b

class Job:
    def __init__(self, chunk, part, out, place, local, shape, order):
        self.chunk=chunk; self.part=part; self.out=out; self.place=place; self.local=local
        self.levels=[]
        for bit in order:
            d=halve(shape)
            after=list(shape)
            if d is not None: after[d]//=2
            self.levels.append((bit,d,tuple(shape),tuple(after)))
            shape=tuple(after)

def make_jobs(chunks, nb, nd):
    orders=level_orders(nb,nd)
    named=dict(c=("bucket",0),y=("bucket",1),x=("dp",0),a=("dp",1),b=("dp",2))
    chosen=[[named[n] for n in word] for word in ORDERS] if (nb,nd)==(4,8) else []
    jobs=[]
    for c,(out,r,k,rows,cols) in enumerate(chunks):
        for p in range(2):
            local=p*(rows//2)
            jobs.append(Job(c,p,out,(r+local,k),local,(rows//2,cols),chosen[2*c+p] if chosen else orders[p]))
    return jobs

class Links:
    def __init__(self): self.free={}
    def end(self, bit, size, t):
        if bit==("dp",2):
            mid,low=self.free.get(bit,0.0),self.free.get(("dp",1),0.0)
            start=max(t,mid,low)
            self.free[("dp",1)]=max(t,low)+size/RATE
            self.free[bit]=start+size/RATE*2
            return start+size/RATE*2+LATENCY
        rate=600e3 if bit==("bucket",0) else RATE
        start=max(t,self.free.get(bit,0.0))
        self.free[bit]=start+size/rate
        return self.free[bit]+LATENCY

def schedule(jobs, steps, ring, shares):
    links=Links(); heap=[]; items=[]; done=set(); now=0.0
    of_chunk={}
    for k,j in enumerate(jobs): of_chunk.setdefault(j.chunk,[]).append(k)
    def issue(k,s,t):
        L=len(jobs[k].levels)
        bit,d,before,after=jobs[k].levels[s if s<L else 2*L-1-s]
        end=t if (s>=L and d is None) else links.end(bit,4*after[0]*after[1],t)
        heapq.heappush(heap,(end,k,s))
    def one(t):
        end,k,s=heapq.heappop(heap)
        t=max(t,end)+ENDS[s>=len(jobs[k].levels)]
        items.append(("end",k,s)); done.add((k,s))
        if s+1<2*len(jobs[k].levels): issue(k,s+1,t)
        return t
    for i,(chunk,us) in enumerate(steps):
        n=0
        while heap and heap[0][0]<=now and n<CAP: now=one(now); n+=1
        if chunk is not None:
            need=[(k,0) for k in of_chunk.get(chunk-ring,[])] if us>0 and chunk+1<len(of_chunk) else []
            if chunk in shares:
                need+=[(k,2*len(jobs[k].levels)-1) for k in of_chunk[shares[chunk]]]
            while not all(n in done for n in need): now=one(now)
        items.append(("step",i)); now+=us
        if chunk is not None:
            for k in of_chunk[chunk]: issue(k,0,now)
    while heap: now=one(now)
    return items,now

class Place:
    def __init__(self, bits):
        me={n: lax.axis_index(n) for n in ("bucket","dp")}
        self.bit={(n,i): lax.rem(lax.div(me[n],1<<i),2) for n,i in bits}
        self.partner={(n,i): tuple(me[m]+(1-2*self.bit[n,i])*(1<<i) if m==n else me[m] for m in me) for n,i in bits}

def span(start,size,by):
    return pl.ds(start if isinstance(start,int) else pl.multiple_of(start,by),size)

def region(ref, off, shape):
    return ref.at[span(off[0],shape[0],8),span(off[1],shape[1],128)]

def add_rows(dst, a, b, shape):
    rows,cols=shape
    rb=8
    while rows%(rb*2)==0 and rb*2*cols<=32*1024: rb*=2
    def one(i,_):
        at=pl.ds(pl.multiple_of(i*rb,8),rb)
        dst[at,:]=a[at,:]+b[at,:]
        return 0
    lax.fori_loop(0,rows//rb,one,0)

class Run:
    def __init__(self, place, job, src, out, acc, recv, ss, rs, ls, credit=None, give=False, take=False):
        self.at=place; self.j=job; self.src=src; self.out=out; self.acc=acc; self.recv=recv
        self.ss=ss; self.rs=rs; self.ls=ls
        self.credit=credit; self.give=give; self.take=take
        self.n=len(job.levels)
        split=[s for s in range(2*self.n) if self.level(s)[1] is not None]
        self.store_at=min(s for s in split if s>=self.n)+1
        self.out_rows=sum(self.level(s)[3][0]*self.level(s)[3][1] for s in split[1:])//job.levels[0][2][1]
    def level(self, s):
        return self.j.levels[s if s<self.n else 2*self.n-1-s]
    def slot(self, s):
        return s if s==0 or self.level(s)[1] is None else 2*self.n-1
    def offset(self, first, last):
        off=[0,0]
        for bit,d,before,after in self.j.levels[first:last+1]:
            if d is not None: off[d]=off[d]+self.at.bit[bit]*after[d]
        return off
    def given(self, s, off):
        bit,d,before,after=self.j.levels[s]
        off=list(off); off[d]=off[d]+(1-self.at.bit[bit])*after[d]
        return off
    def piece(self, lv):
        off=self.offset(0,lv)
        return [self.j.place[0]+off[0],self.j.place[1]+off[1]]
    def local(self):
        after=self.level(self.n)[3]
        return pltpu.make_async_copy(region(self.acc,self.offset(1,self.n-1),after),
                                     region(self.out,self.piece(self.n-1),after),self.ls.at[0])
    def remote(self, s):
        bit,d,before,after=self.level(s)
        if s==0:
            src,dst=region(self.src,self.given(0,[self.j.local,0]),after),self.recv[0]
        elif s<self.n:
            off=self.offset(1,s-1)
            src,dst=region(self.acc,off if d is None else self.given(s,off),after),self.recv[s]
        else:
            dst=region(self.out,self.piece(2*self.n-1-s),after)
            first=all(self.level(i)[1] is None for i in range(self.n,s))
            src=region(self.acc,self.offset(1,self.n-1),after) if first else dst
        return pltpu.make_async_remote_copy(src_ref=src,dst_ref=dst,send_sem=self.ss.at[self.slot(s)],recv_sem=self.rs.at[s],
                                            device_id=self.at.partner[bit],device_id_type=MESH)
    def start(self, s):
        bit,d,before,after=self.level(s)
        if s==self.n: self.local().start()
        if s>=self.n and d is None: return
        if s==self.store_at: self.local().wait()
        if s==0 and self.take: pl.semaphore_wait(self.credit,1)
        self.remote(s).start()
    def finish(self, s):
        bit,d,before,after=self.level(s)
        if s>=self.n:
            if d is not None: self.remote(s).wait_recv()
        else:
            if d is None: self.remote(s).wait()
            else: self.remote(s).wait_recv()
            to=region(self.acc,self.offset(1,s),after)
            own=region(self.src,[self.j.local+self.offset(0,0)[0],0],after) if s==0 else to
            add_rows(to,own,self.recv[s],after)
            if s==0 and self.give:
                pl.semaphore_signal(self.credit,inc=1,device_id=self.at.partner[bit],device_id_type=MESH)
        if s+1<2*self.n: self.start(s+1)
        else: self.close()
    def sent(self):
        self.remote(0).wait_send()
    def close(self):
        if self.store_at==2*self.n: self.local().wait()
        if not self.give: self.sent()
        sent=region(self.out,(0,0),(self.out_rows,self.j.levels[0][2][1]))
        pltpu.make_async_remote_copy(src_ref=sent,dst_ref=sent,send_sem=self.ss.at[2*self.n-1],recv_sem=self.rs.at[0],
                                     device_id=self.at.partner[self.j.levels[0][0]],device_id_type=MESH).wait_send()

RING=2

def back_kernel(plan,*refs):
    (jobs,items,nchunk,nf,nhead,nblk,nrow,shares,bits,norm)=plan
    refs=list(refs)
    def take(n):
        out=refs[:n]; del refs[:n]; return out
    (wt,g,du,dm,c,at_h,db,a,w)=take(9)
    (q,k,v,do,at,lse,qu,ku,qr,kr)=take(10)
    (seg,qg,mid,x,dh,ng)=take(6)
    outs=take(5)
    (tg_o,)=take(1)
    (pool,stage,l0,dqkv,dq_s,dk_s,dv_s,kt_s,small,kc,qc,s_s,dp_s,p_s,ds_s)=take(15)
    (pool_sem,credit)=take(2)
    t,d=at_h.shape
    ob=t//nblk; tb=32
    own=nchunk-len(shares)-1
    bufs=[]
    for n in range(own+1):
        pair=[]
        for p in range(2):
            L=len(jobs[2*(n if n<own else nchunk-1)+p].levels)
            pair.append((take(1)[0],take(L-1 if n<own else L)))
        bufs.append(pair)
    place=Place(bits)
    runs=[]
    for n,j in enumerate(jobs):
        ss,rs,ls=take(3)
        if j.chunk==nchunk-1:
            acc,recv=bufs[own][j.part]
            runs.append(Run(place,j,small,outs[j.out],acc,recv,ss,rs,ls))
        else:
            acc,recv=bufs[shares.get(j.chunk,j.chunk)][j.part]
            runs.append(Run(place,j,stage.at[j.chunk%RING],outs[j.out],acc,[l0.at[2*(j.chunk%RING)+j.part]]+list(recv),ss,rs,ls,
                            credit.at[j.part],give=j.chunk+RING<nchunk-1,take=j.chunk>=RING))
    pid=pl.program_id(0)
    def col(ref,f): return ref.at[:,pl.ds(f*d,d)]
    names={"g":g,"du":du,"dm":dm,"c":c,"at":at_h,"db":db,"a":a,"w":w}
    plan_l=[]
    for f in range(nf): plan_l.append((("g",f),0 if f%2==0 else 2,1,True))
    for f in range(nf): plan_l.append((("du",f),0 if (nf+f)%2==0 else 2,3,False))
    load={i:[] for i in range(-1,2*nf+2)}
    load[-1]+= [(("dm",0),1),(("c",0),3)]
    for i,(what,s,other,_) in enumerate(plan_l):
        load[max(i-2,-1)].append((what,s))
    n0=2*nf+1
    s_at=0 if (2*nf)%2==0 else 2
    load[2*nf-2].append((("at",0),s_at))
    load[nf].append((("db",0),1))
    load[2*nf-1].append((("a",0),3))
    load[2*nf]+= [(("w",0),0),(("w",1),1),(("w",2),2)]
    def copy_of(what,s):
        name,f=what
        if name=="w": return pltpu.make_async_copy(col(w,f),pool.at[s,pl.ds(0,d),:],pool_sem.at[s])
        if name in ("g","du"): return pltpu.make_async_copy(col(names[name],f),pool.at[s],pool_sem.at[s])
        return pltpu.make_async_copy(names[name],pool.at[s],pool_sem.at[s])
    waiting={}
    def fetch_after(i):
        for what,s in load.get(i,[]):
            copy_of(what,s).start(); waiting[s]=what
    def ready(s):
        if s in waiting: copy_of(waiting.pop(s),s).wait()
    total=wt[0]
    for n in range(1,wt.shape[0]): total=total+wt[n]
    scale=wt[lax.axis_index("bucket")].astype(F32)/(total.astype(F32)*norm)
    products=[(s,other) if first else (other,s) for what,s,other,first in plan_l]+[(s_at,1)]
    n_h=1; n_x=n_h+nhead; n_r=n_x; n_end=n_r+nrow

    def weight_step(chunk,lhs,rhs,gate=None):
        if chunk>=RING:
            for p in range(2): runs[2*(chunk-RING)+p].sent()
        stage[chunk%RING]=scale*mm(lhs,rhs,0,0)
        if gate is not None: gate()
        for p in range(2): runs[2*chunk+p].start(0)

    segments=[[]]
    for it in items:
        if it[0]=="step": segments.append([])
        else: segments[-1].append(it)
    def before(i):
        for it in segments[i]: runs[it[1]].finish(it[2])
    heads=n0+nhead*nblk
    inner={h: [n0+h*nblk+ib for ib in range(nblk)] for h in range(nhead)}
    @pl.when(pid==0)
    def _():
        sem=pltpu.get_barrier_semaphore()
        for bit in bits:
            pl.semaphore_signal(sem,inc=1,device_id=place.partner[bit],device_id_type=MESH)
        fetch_after(-1)
        kc[...],qc[...]=segment_codes(column(seg[...].astype(F32),2*HD),t)
        small[...]=jnp.zeros_like(small)
        small[3:3+nf+2,:]=scale*mid[0:nf+2,:]
        small[nf+6:nf+7,:]=scale*mid[nf+2:nf+3,:]
        small[nf+8:nf+9,:]=scale*mid[nf+3:nf+4,:]
        for n,(lhs,rhs) in enumerate(products):
            before(n)
            ready(lhs); ready(rhs)
            weight_step(n,pool[lhs],pool[rhs],(lambda: pl.semaphore_wait(sem,len(bits))) if n==0 else None)
            fetch_after(n)
    for h in range(nhead):
        if segments[inner[h][0]]:
            @pl.when(pid==n_h+h)
            def _(h=h): before(inner[h][0])
    @pl.when(pid==n_r)
    def _():
        for s in range(4): ready(s)
        for n in range(3):
            before(heads+n)
            weight_step(n0+n,pool[3],dqkv[:,n*d:(n+1)*d])
        before(heads+3)
    for r in range(1,nrow):
        if segments[heads+3+r]:
            @pl.when(pid==n_r+r)
            def _(r=r): before(heads+3+r)
    @pl.when((pid>=n_h)&(pid<n_x))
    def _():
        hp=pid-n_h
        lanes=pl.ds(pl.multiple_of(hp*2*HD,2*HD),2*HD)
        kt_s[...]=k[...].T
        lane=lax.broadcasted_iota(jnp.int32,(1,2*HD),1)//HD
        half=lax.broadcasted_iota(jnp.int32,(8,2*HD),1)//HD
        pick=jnp.where(half==lax.broadcasted_iota(jnp.int32,(8,2*HD),0),1.0,0.0).astype(BF)
        for ib in range(nblk):
            for h in range(nhead):
                if ib>0 and segments[inner[h][ib]]:
                    @pl.when(hp==h)
                    def _(h=h):
                        before(inner[h][ib])
            rows=slice(ib*ob,(ib+1)*ob)
            dd=do[rows,:].astype(F32)*at[rows,:].astype(F32)
            hi=dd.astype(BF); rest=dd-hi.astype(F32); mid_=rest.astype(BF); low=(rest-mid_.astype(F32)).astype(BF)
            delta=mm(pick,hi,1,1)+(mm(pick,mid_,1,1)+mm(pick,low,1,1))
            dqs=[]
            for h in range(2):
                s_s[h]=mm(jnp.where(lane==h,k[...],kc[...]),jnp.where(lane==h,q[rows,:],qc[rows,:]),1,1)
                dp_s[h]=mm(v[...],jnp.where(lane==h,do[rows,:],0),1,1)
            for h in range(2):
                top,dl=lse[0,h:h+1,rows],delta[h:h+1,:]
                for n in range(t//tb):
                    at_n=slice(n*tb,(n+1)*tb)
                    p=jnp.exp(s_s[h,at_n,:]-top)
                    p_s[h,at_n,:]=p.astype(BF)
                    ds_s[h,at_n,:]=(p*(dp_s[h,at_n,:]-dl)).astype(BF)
                dvp=mm(p_s[h],jnp.where(lane==h,do[rows,:],0))
                dkp=mm(ds_s[h],jnp.where(lane==h,q[rows,:],0))
                if ib==0 and h==0: dv_s[...]=dvp; dk_s[...]=dkp
                else: dv_s[...]+=dvp; dk_s[...]+=dkp
                dqs.append(mm(kt_s[h*HD:(h+1)*HD,:],ds_s[h]))
            dq_s[rows,:]=jnp.concatenate(dqs,axis=0).T*(1.0/math.sqrt(HD))
        m=avg_matrix()[:2*HD,:2*HD]
        def avg(y):
            yh=y.astype(BF)
            return mm(yh,m)+mm((y-yh.astype(F32)).astype(BF),m)
        gains=per_head(qg,2)
        for n,(gr,un,rr) in enumerate(((dq_s,qu,qr),(dk_s,ku,kr))):
            gg=gr[...]; u=un[...].astype(F32)
            e=gg*gains[n:n+1,:]
            back=(rr[...]*(e-avg(e)-u*avg(e*u))).astype(BF)
            dqkv[:,pl.ds(pl.multiple_of(n*d+hp*2*HD,2*HD),2*HD)]=back
            small[n:n+1,lanes]=scale*jnp.sum(back.astype(F32),axis=0,keepdims=True)
            small[nf+9+n:nf+10+n,lanes]=scale*jnp.sum(gg*u,axis=0,keepdims=True)
            small[nf+11+n:nf+12+n,lanes]=scale*jnp.sum(gg,axis=0,keepdims=True)
        back=dv_s[...].astype(BF)
        dqkv[:,pl.ds(pl.multiple_of(2*d+hp*2*HD,2*HD),2*HD)]=back
        small[2:3,lanes]=scale*jnp.sum(back.astype(F32),axis=0,keepdims=True)
    @pl.when((pid>=n_r)&(pid<n_end))
    def _():
        rb=x.shape[0]
        rows=pl.ds(pl.multiple_of((pid-n_r)*rb,rb),rb)
        da=mm(dqkv[rows,0:d],pool[0,:d,:],1,1)+mm(dqkv[rows,d:2*d],pool[1,:d,:],1,1)+mm(dqkv[rows,2*d:],pool[2,:d,:],1,1)
        unit,r=row_norm(x[...].astype(F32))
        e=da*ng[0:1,:]
        tg_o[...]=dh[...]+r*(e-jnp.mean(e,axis=-1,keepdims=True)-unit*jnp.mean(e*unit,axis=-1,keepdims=True))
        small[nf+5:nf+6,:]+=scale*jnp.sum(da*unit,axis=0,keepdims=True)
        small[nf+7:nf+8,:]+=scale*jnp.sum(da,axis=0,keepdims=True)
    @pl.when(pid==n_end-1)
    def _():
        for p in range(2): runs[2*(nchunk-1)+p].start(0)
        before(heads+3+nrow)

def backward(wt,g,du,dm,c,at,db,a,w,q,k,v,do,lse,qu,ku,qr,kr,seg,qg,mid,x,dh,ng,nb,nd,ob=256,rb=256):
    t,d=x.shape; ff=g.shape[1]; nf=ff//d
    nhead=d//(2*HD); nblk=t//ob; nrow=t//rb
    n0=2*nf+1
    chunks=[(0,f*d,0,d,d) for f in range(nf)]+[(1,0,f*d,d,d) for f in range(nf)]+[(2,0,0,d,d)]
    chunks+=[(3,0,n*d,d,d) for n in range(3)]+[(4,0,0,32,d)]
    nchunk=len(chunks)
    shares={} if (nb,nd)==(4,8) else {n0+n:n for n in range(3)}
    jobs=make_jobs(chunks,nb,nd)
    steps=[(n,2.2) for n in range(n0)]+[(None,2.1)]*(nhead*nblk)+[(n0+n,2.2) for n in range(3)]+[(None,2.6)]*(nrow-1)+[(nchunk-1,2.6)]
    items,_=schedule(jobs,steps,RING,shares)
    bits=bits_of(nb,nd)
    n_h=1; n_r=n_h+nhead; n_end=n_r+nrow
    def head(i): return jnp.clip(i-n_h,0,nhead-1)
    def block(i): return jnp.clip(i-n_r,0,nrow-1)
    any_=pl.BlockSpec(memory_space=pltpu.HBM)
    colspec=pl.BlockSpec((t,2*HD),lambda i:(0,head(i)))
    rows=pl.BlockSpec((rb,d),lambda i:(block(i),0))
    in_specs=[pl.BlockSpec(memory_space=pltpu.SMEM)]+[any_]*8+[colspec]*5+[pl.BlockSpec((1,2,t),lambda i:(head(i),0,0))]+[colspec]*4
    in_specs+=[whole(seg),whole(qg),whole(mid),rows,rows,whole(ng)]
    out_specs=[any_]*5+[rows]
    S=jax.ShapeDtypeStruct
    out_shape=[S((ff,d),F32),S((d,ff),F32),S((d,d),F32),S((d,3*d),F32),S((32,d),F32),S((t,d),F32)]
    half=(d//2)//2
    scratch=[pltpu.VMEM((4,t,d),BF),pltpu.VMEM((RING,d,d),F32),pltpu.VMEM((2*RING,half,d),F32),pltpu.VMEM((t,3*d),BF)]
    scratch+=[pltpu.VMEM((t,2*HD),F32)]*3+[pltpu.VMEM((2*HD,t),BF),pltpu.VMEM((32,d),F32),pltpu.VMEM((t,2*HD),BF),pltpu.VMEM((t,2*HD),BF),pltpu.VMEM((2,t,ob),F32),pltpu.VMEM((2,t,ob),F32),pltpu.VMEM((2,t,ob),BF),pltpu.VMEM((2,t,ob),BF),pltpu.SemaphoreType.DMA((4,)),pltpu.SemaphoreType.REGULAR((2,))]
    own=nchunk-len(shares)-1
    for n in range(own+1):
        small=n==own
        for p in range(2):
            j=jobs[2*(nchunk-1 if small else n)+p]
            scratch.append(pltpu.VMEM(j.levels[0][3],F32))
            for lv in j.levels[0 if small else 1:]: scratch.append(pltpu.VMEM(lv[3],F32))
    for j in jobs:
        L=len(j.levels)
        scratch+=[pltpu.SemaphoreType.DMA((2*L,)),pltpu.SemaphoreType.DMA((2*L,)),pltpu.SemaphoreType.DMA((1,))]
    plan=(jobs,items,nchunk,nf,nhead,nblk,nrow,shares,bits,math.sqrt(t*nd))
    return pl.pallas_call(functools.partial(back_kernel,plan),grid=(n_end,),in_specs=in_specs,out_specs=out_specs,out_shape=out_shape,
        scratch_shapes=scratch,
        compiler_params=pltpu.CompilerParams(collective_id=7,has_side_effects=True,vmem_limit_bytes=63<<20),name="backward")(
        wt,g,du,dm,c,at,db,a,w,q,k,v,do,at,lse,qu,ku,qr,kr,seg,qg,mid,x,dh,ng)

def finish_kernel(nf,f2,f1,fo,fq,tg,small,f2_o,f1_o,fo_o,fq_o,tg_o,bq_o,bo_o,b1_o,b2_o,gain_o,shift_o,hg_o,hs_o):
    for src,dst in ((f2,f2_o),(f1,f1_o),(fo,fo_o),(fq,fq_o),(tg,tg_o)): dst[...]=src[...]
    d=small.shape[1]
    @pl.when(pl.program_id(0)==0)
    def _():
        for i in range(3): bq_o[i*d:(i+1)*d]=small[i,:]
        bo_o[...]=small[3,:]
        for i in range(nf): b1_o[i*d:(i+1)*d]=small[4+i,:]
        b2_o[...]=small[4+nf,:]
        gain_o[...]=small[5+nf:7+nf,:]
        shift_o[...]=small[7+nf:9+nf,:]
        for n,o in enumerate((hg_o,hs_o)):
            wide=small[9+nf+2*n:11+nf+2*n,:]
            pair=wide[:,:2*HD]
            for i in range(1,d//(2*HD)): pair=pair+wide[:,2*HD*i:2*HD*(i+1)]
            o[...]=pair[:,:HD]+pair[:,HD:]

def finish(f2,f1,fo,fq,tg,small,n=4):
    ff,d=f2.shape; nf=ff//d
    S=jax.ShapeDtypeStruct
    wide=[pl.BlockSpec((a.shape[0]//n,a.shape[1]),lambda i:(i,0)) for a in (f2,f1,fo,fq,tg)]
    big=[S(a.shape,F32) for a in (f2,f1,fo,fq,tg)]
    rest=[S((3*d,),F32),S((d,),F32),S((ff,),F32),S((d,),F32),S((2,d),F32),S((2,d),F32),S((2,HD),F32),S((2,HD),F32)]
    return pl.pallas_call(functools.partial(finish_kernel,nf),grid=(n,),
        in_specs=wide+[whole(small)],
        out_specs=wide+[whole(a) for a in rest],
        out_shape=big+rest,compiler_params=pltpu.CompilerParams(vmem_limit_bytes=VM),name="finish")(f2,f1,fo,fq,tg,small)


def body(
    tokens,
    segment,
    live,
    group_patches,
    qkv_weight,
    qkv_bias,
    out_weight,
    out_bias,
    fc1_weight,
    fc1_bias,
    fc2_weight,
    fc2_bias,
    norm_gain,
    norm_shift,
    qk_gain,
    qk_shift,
    cotangent,
):
    a_low, q_low, k_low, v_low, q_unit, k_unit, q_inv, k_inv = qkv_forward(
        tokens, qkv_weight, qkv_bias, norm_gain, norm_shift, qk_gain, qk_shift
    )
    attn_low, lse = attend_forward(q_low, k_low, v_low, segment)
    out, dhid, dattn, g_low, du_low, dm_low, c_low, db_low, mid_sums = mlp(
        tokens,
        cotangent,
        live[None],
        attn_low,
        out_weight,
        out_bias,
        fc1_weight,
        fc1_bias,
        fc2_weight,
        fc2_bias,
        norm_gain,
        norm_shift,
    )
    fc2_grad, fc1_grad, out_grad, qkv_grad, small, tokens_grad = backward(
        group_patches, g_low, du_low, dm_low, c_low, attn_low, db_low, a_low, qkv_weight,
        q_low, k_low, v_low, dattn, lse, q_unit, k_unit, q_inv, k_inv,
        segment[None], qk_gain, mid_sums, tokens, dhid, norm_gain,
        lax.axis_size("bucket"), lax.axis_size("dp"),
    )
    (fc2_grad, fc1_grad, out_grad, qkv_grad, tokens_grad, qkv_b, out_b, fc1_b, fc2_b, n_gain, n_shift, h_gain, h_shift) = finish(
        fc2_grad, fc1_grad, out_grad, qkv_grad, tokens_grad, small
    )
    return (
        out, tokens_grad, qkv_grad, qkv_b, out_grad, out_b, fc1_grad, fc1_b, fc2_grad, fc2_b,
        n_gain, n_shift, h_gain, h_shift,
    )


def solution(mesh):
    return jax.shard_map(
        body,
        mesh=mesh,
        in_specs=(
            P(("bucket", "dp"), None),
            P(("bucket", "dp")),
            P(("bucket", "dp")),
            *((P(),) * 13),
            P(("bucket", "dp"), None),
        ),
        out_specs=(P(("bucket", "dp"), None), P(("bucket", "dp"), None), *((P(),) * 12)),
        check_vma=False,
    )
```

```python
import functools
import heapq
import math

import jax
import jax.numpy as jnp
from jax import lax
from jax.experimental import pallas as pl
from jax.experimental.pallas import tpu as pltpu
from jax.sharding import PartitionSpec as P

F32=jnp.float32; BF=jnp.bfloat16
EPSILON=1e-6
NEG=-1e30
HD=64
VM=58<<20

def mm(a,b,ca=1,cb=0):
    return lax.dot_general(a,b,(((ca,),(cb,)),((),())),preferred_element_type=F32)

def row_norm(x):
    c=x-jnp.mean(x,axis=-1,keepdims=True)
    r=lax.rsqrt(jnp.mean(c*c,axis=-1,keepdims=True)+EPSILON)
    return c*r,r

def head_avg(x,m,twice):
    out=[]
    for i in range(x.shape[1]//256):
        part=x[:,256*i:256*(i+1)]
        hi=part.astype(BF)
        s=mm(hi,m)
        if twice: s=s+mm((part-hi.astype(F32)).astype(BF),m)
        out.append(s)
    return jnp.concatenate(out,axis=1)

def avg_matrix():
    i=lax.broadcasted_iota(jnp.int32,(256,256),0)//HD
    j=lax.broadcasted_iota(jnp.int32,(256,256),1)//HD
    return jnp.where(i==j,1.0/HD,0.0).astype(BF)

def row(ref):
    return ref[...][None,:]

def column(values, lanes):
    return jnp.broadcast_to(values,(lanes,values.shape[1])).T

def per_head(ref, times):
    return jnp.concatenate([ref[...]]*times,axis=1)

def whole(a):
    nd=len(a.shape)
    return pl.BlockSpec(a.shape,lambda *_:(0,)*nd,pipeline_mode=pl.Buffered(1))

def qkv_kernel(x,w,b,ng,ns,qg,qs,a_o,q_o,k_o,v_o,qu_o,ku_o,qr_o,kr_o):
    d=x.shape[1]
    gains=per_head(qg,d//HD); shifts=per_head(qs,d//HD)
    bias=row(b)
    u,_=row_norm(x[...].astype(F32))
    a=(u*ng[0:1,:]+ns[0:1,:]).astype(BF)
    a_o[...]=a
    m=avg_matrix()
    for i,(lo,un,rr) in enumerate(((q_o,qu_o,qr_o),(k_o,ku_o,kr_o))):
        raw=mm(a,w[:,i*d:(i+1)*d])+bias[:,i*d:(i+1)*d]
        c=raw-head_avg(raw,m,True)
        r=lax.rsqrt(head_avg(c*c,m,False)+EPSILON)
        unit=c*r
        un[...]=unit.astype(BF)
        rr[...]=r.astype(BF)
        n=unit*gains[i:i+1,:]+shifts[i:i+1,:]
        if i==0: n=n*(1.0/math.sqrt(HD))
        lo[...]=n.astype(BF)
    v_o[...]=(mm(a,w[:,2*d:])+bias[:,2*d:]).astype(BF)

def qkv_forward(x,w,b,ng,ns,qg,qs,rb=256):
    t,d=x.shape
    rows=pl.BlockSpec((rb,d),lambda i:(i,0))
    sh=lambda dt: jax.ShapeDtypeStruct((t,d),dt)
    return pl.pallas_call(qkv_kernel,grid=(t//rb,),
        in_specs=[rows,whole(w),whole(b),whole(ng),whole(ns),whole(qg),whole(qs)],
        out_specs=[rows]*8,
        out_shape=[sh(BF)]*8,
        compiler_params=pltpu.CompilerParams(vmem_limit_bytes=VM),name="norm_qkv")(x,w,b,ng,ns,qg,qs)

BIG=384.0

def segment_codes(col, count):
    bits=(count-1).bit_length()
    at=lax.rem(lax.broadcasted_iota(jnp.int32,col.shape,1),HD)
    bit=lax.shift_right_logical(col.astype(jnp.int32),jnp.minimum(at,bits))&1
    sign=jnp.where(at<bits,(2*bit-1).astype(F32),0.0)
    key=jnp.where(at==bits,1.0,sign)
    query=jnp.where(at==bits,-BIG*bits,BIG*sign)
    return key.astype(BF),query.astype(BF)

def attend_kernel(q,k,v,seg,o,lse,kc,qc,s_s,p_s,ob=1024,tb=16):
    t=q.shape[0]
    @pl.when(pl.program_id(0)==0)
    def _(): kc[...],qc[...]=segment_codes(column(row(seg).astype(F32),2*HD),t)
    vt=v[...].T
    lane=lax.broadcasted_iota(jnp.int32,(1,2*HD),1)//HD
    keys=[jnp.where(lane==h,k[...],kc[...]) for h in range(2)]
    for i in range(t//ob):
        rows=slice(i*ob,(i+1)*ob)
        parts=[]
        for h in range(2):
            s_s[h]=mm(keys[h],jnp.where(lane==h,q[rows,:],qc[rows,:]),1,1)
        for h in range(2):
            top=s_s[h,:tb,:]
            for n in range(1,t//tb): top=jnp.maximum(top,s_s[h,n*tb:(n+1)*tb,:])
            m=jnp.max(top,axis=0,keepdims=True)
            total=jnp.zeros((tb,ob),F32)
            for n in range(t//tb):
                p=jnp.exp(s_s[h,n*tb:(n+1)*tb,:]-m)
                total=total+p
                p_s[h,n*tb:(n+1)*tb,:]=p.astype(BF)
            l=jnp.sum(total,axis=0,keepdims=True)
            lse[0,h:h+1,rows]=m+jnp.log(l)
            parts.append(mm(vt[h*HD:(h+1)*HD,:],p_s[h])*(1.0/l))
        o[rows,:]=jnp.concatenate(parts,axis=0).T.astype(BF)

def attend_forward(q,k,v,seg):
    t,d=q.shape
    hp=d//(2*HD)
    col=pl.BlockSpec((t,2*HD),lambda h:(0,h))
    return pl.pallas_call(attend_kernel,grid=(hp,),
        in_specs=[col,col,col,whole(seg)],
        out_specs=[col,pl.BlockSpec((1,2,t),lambda h:(h,0,0))],
        out_shape=[jax.ShapeDtypeStruct((t,d),BF),jax.ShapeDtypeStruct((hp,2,t),F32)],
        scratch_shapes=[pltpu.VMEM((t,2*HD),BF)]*2+[pltpu.VMEM((2,t,1024),F32),pltpu.VMEM((2,t,1024),BF)],
        compiler_params=pltpu.CompilerParams(vmem_limit_bytes=VM),name="attend")(q,k,v,seg)

def mlp_kernel(nf,x,cot,live,attn,wo,bo,w1,b1,w2,b2,ng,ns,
               out_o,dhid_o,dattn_o,g_o,du_o,dm_o,c_o,db_o,small_o,pre_s,dg_s,tb=16):
    i=pl.program_id(0)
    rb,d=x.shape
    hid=x[...].astype(F32)+mm(attn[...],wo[...])+row(bo)
    unit,r=row_norm(hid)
    c=(unit*ng[1:2,:]+ns[1:2,:]).astype(BF)
    c_o[...]=c
    lv=column(live[:,pl.ds(pl.multiple_of(i*rb,rb),rb)].astype(F32),8)[:,:1]
    fc1_bias=row(b1)
    dm=cot[...].astype(F32)*lv
    dml=dm.astype(BF)
    dm_o[...]=dml
    out=jnp.zeros((rb,d),F32); dc=jnp.zeros((rb,d),F32)
    sums=[]
    for f in range(nf):
        cols=slice(f*d,(f+1)*d)
        pre_s[...]=mm(c,w1[:,cols])
        dg_s[...]=mm(dml,w2[cols,:],1,1)
        total=jnp.zeros((tb,d),F32)
        for n in range(rb//tb):
            at=slice(n*tb,(n+1)*tb)
            pre=pre_s[at,:]+fc1_bias[:,cols]
            phi=0.5*(1.0+lax.erf(pre*(1.0/math.sqrt(2.0))))
            slope=phi+pre*jnp.exp(-0.5*pre*pre)*(1.0/math.sqrt(2.0*math.pi))
            du=(dg_s[at,:]*slope).astype(BF)
            g_o[at,cols]=(pre*phi).astype(BF)
            du_o[at,cols]=du
            total=total+du.astype(F32)
        g,du=g_o[:,cols],du_o[:,cols]
        out=out+mm(g,w2[cols,:])
        dc=dc+mm(du,w1[:,cols],1,1)
        sums.append(jnp.sum(total,axis=0,keepdims=True))
    out_o[...]=(lv*(hid+out+row(b2))).astype(BF)
    e=dc*ng[1:2,:]
    dh=dm+r*(e-jnp.mean(e,axis=-1,keepdims=True)-unit*jnp.mean(e*unit,axis=-1,keepdims=True))
    dhid_o[...]=dh
    db=dh.astype(BF)
    db_o[...]=db
    dattn_o[...]=mm(db,wo[...],1,1).astype(BF)
    total=jnp.concatenate([jnp.sum(db.astype(F32),axis=0,keepdims=True)]+sums+[jnp.sum(dm,axis=0,keepdims=True),
        jnp.sum(dc*unit,axis=0,keepdims=True),jnp.sum(dc,axis=0,keepdims=True)],axis=0)
    @pl.when(i==0)
    def _(): small_o[...]=total
    @pl.when(i>0)
    def _(): small_o[...]+=total

def mlp(x,cot,live,attn,wo,bo,w1,b1,w2,b2,ng,ns,rb=256):
    t,d=x.shape; ff=w1.shape[1]; nf=ff//d
    rows=pl.BlockSpec((rb,d),lambda i:(i,0))
    wide=pl.BlockSpec((rb,ff),lambda i:(i,0))
    low=jax.ShapeDtypeStruct((t,d),BF)
    big=jax.ShapeDtypeStruct((t,ff),BF)
    return pl.pallas_call(functools.partial(mlp_kernel,nf),grid=(t//rb,),
        in_specs=[rows,rows,whole(live),rows]+[whole(a) for a in (wo,bo,w1,b1,w2,b2,ng,ns)],
        out_specs=[rows,rows,rows,wide,wide,rows,rows,rows,pl.BlockSpec((nf+4,d),lambda i:(0,0))],
        out_shape=[low,jax.ShapeDtypeStruct((t,d),F32),low,big,big,low,low,low,jax.ShapeDtypeStruct((nf+4,d),F32)],
        scratch_shapes=[pltpu.VMEM((rb,d),F32)]*2,
        compiler_params=pltpu.CompilerParams(vmem_limit_bytes=VM),name="mlp")(x,cot,live,attn,wo,bo,w1,b1,w2,b2,ng,ns)

MESH = pl.DeviceIdType.MESH
RATE=45e3
LATENCY=1.6
ENDS=(0.45,0.3)
CAP=99
ORDERS=(
    'cxyab', 'cyaxb', 'cayxb', 'cyxab', 'cxayb', 'caxyb', 'cxayb', 'cyabx',
    'cxayb', 'cyaxb', 'cxayb', 'cyaxb', 'cyaxb', 'cxyab', 'cxyab', 'cyxab',
    'cxyab', 'cyxab', 'cxayb', 'cxayb', 'cxyab', 'cyxab', 'cayxb', 'cyabx',
    'cxayb', 'cyaxb',
)

def halve(shape):
    rows, cols = shape
    if rows % 16 == 0: return 0
    if cols % 256 == 0: return 1
    return None

def bits_of(nb, nd):
    return ([("bucket",i) for i in range(int(math.log2(nb)))]
            + [("dp",i) for i in range(int(math.log2(nd)))])

def level_orders(nb, nd):
    bk=[("bucket",i) for i in range(int(math.log2(nb)))]
    dp=[("dp",i) for i in range(int(math.log2(nd)))]
    a=bk[:1]+dp[:2]+bk[1:]+dp[2:]
    b=bk[:1]+bk[1:]+dp[1:2]+dp[:1]+dp[2:]
    return a,b

class Job:
    def __init__(self, chunk, part, out, place, local, shape, order):
        self.chunk=chunk; self.part=part; self.out=out; self.place=place; self.local=local
        self.levels=[]
        for bit in order:
            d=halve(shape)
            after=list(shape)
            if d is not None: after[d]//=2
            self.levels.append((bit,d,tuple(shape),tuple(after)))
            shape=tuple(after)

def make_jobs(chunks, nb, nd):
    orders=level_orders(nb,nd)
    named=dict(c=("bucket",0),y=("bucket",1),x=("dp",0),a=("dp",1),b=("dp",2))
    chosen=[[named[n] for n in word] for word in ORDERS] if (nb,nd)==(4,8) else []
    jobs=[]
    for c,(out,r,k,rows,cols) in enumerate(chunks):
        for p in range(2):
            local=p*(rows//2)
            jobs.append(Job(c,p,out,(r+local,k),local,(rows//2,cols),chosen[2*c+p] if chosen else orders[p]))
    return jobs

class Links:
    def __init__(self): self.free={}
    def end(self, bit, size, t):
        if bit==("dp",2):
            mid,low=self.free.get(bit,0.0),self.free.get(("dp",1),0.0)
            start=max(t,mid,low)
            self.free[("dp",1)]=max(t,low)+size/RATE
            self.free[bit]=start+size/RATE*2
            return start+size/RATE*2+LATENCY
        rate=600e3 if bit==("bucket",0) else RATE
        start=max(t,self.free.get(bit,0.0))
        self.free[bit]=start+size/rate
        return self.free[bit]+LATENCY

def schedule(jobs, steps, ring, shares):
    links=Links(); heap=[]; items=[]; done=set(); now=0.0
    of_chunk={}
    for k,j in enumerate(jobs): of_chunk.setdefault(j.chunk,[]).append(k)
    def issue(k,s,t):
        L=len(jobs[k].levels)
        bit,d,before,after=jobs[k].levels[s if s<L else 2*L-1-s]
        end=t if (s>=L and d is None) else links.end(bit,4*after[0]*after[1],t)
        heapq.heappush(heap,(end,k,s))
    def one(t):
        end,k,s=heapq.heappop(heap)
        t=max(t,end)+ENDS[s>=len(jobs[k].levels)]
        items.append(("end",k,s)); done.add((k,s))
        if s+1<2*len(jobs[k].levels): issue(k,s+1,t)
        return t
    for i,(chunk,us) in enumerate(steps):
        n=0
        while heap and heap[0][0]<=now and n<CAP: now=one(now); n+=1
        if chunk is not None:
            need=[(k,0) for k in of_chunk.get(chunk-ring,[])] if us>0 and chunk+1<len(of_chunk) else []
            if chunk in shares:
                need+=[(k,2*len(jobs[k].levels)-1) for k in of_chunk[shares[chunk]]]
            while not all(n in done for n in need): now=one(now)
        items.append(("step",i)); now+=us
        if chunk is not None:
            for k in of_chunk[chunk]: issue(k,0,now)
    while heap: now=one(now)
    return items,now

class Place:
    def __init__(self, bits):
        me={n: lax.axis_index(n) for n in ("bucket","dp")}
        self.bit={(n,i): lax.rem(lax.div(me[n],1<<i),2) for n,i in bits}
        self.partner={(n,i): tuple(me[m]+(1-2*self.bit[n,i])*(1<<i) if m==n else me[m] for m in me) for n,i in bits}

def span(start,size,by):
    return pl.ds(start if isinstance(start,int) else pl.multiple_of(start,by),size)

def region(ref, off, shape):
    return ref.at[span(off[0],shape[0],8),span(off[1],shape[1],128)]

def add_rows(dst, a, b, shape):
    rows,cols=shape
    rb=8
    while rows%(rb*2)==0 and rb*2*cols<=32*1024: rb*=2
    def one(i,_):
        at=pl.ds(pl.multiple_of(i*rb,8),rb)
        dst[at,:]=a[at,:]+b[at,:]
        return 0
    lax.fori_loop(0,rows//rb,one,0)

class Run:
    def __init__(self, place, job, src, out, acc, recv, ss, rs, ls, credit=None, give=False, take=False):
        self.at=place; self.j=job; self.src=src; self.out=out; self.acc=acc; self.recv=recv
        self.ss=ss; self.rs=rs; self.ls=ls
        self.credit=credit; self.give=give; self.take=take
        self.n=len(job.levels)
        split=[s for s in range(2*self.n) if self.level(s)[1] is not None]
        self.store_at=min(s for s in split if s>=self.n)+1
        self.out_rows=sum(self.level(s)[3][0]*self.level(s)[3][1] for s in split[1:])//job.levels[0][2][1]
    def level(self, s):
        return self.j.levels[s if s<self.n else 2*self.n-1-s]
    def slot(self, s):
        return s if s==0 or self.level(s)[1] is None else 2*self.n-1
    def offset(self, first, last):
        off=[0,0]
        for bit,d,before,after in self.j.levels[first:last+1]:
            if d is not None: off[d]=off[d]+self.at.bit[bit]*after[d]
        return off
    def given(self, s, off):
        bit,d,before,after=self.j.levels[s]
        off=list(off); off[d]=off[d]+(1-self.at.bit[bit])*after[d]
        return off
    def piece(self, lv):
        off=self.offset(0,lv)
        return [self.j.place[0]+off[0],self.j.place[1]+off[1]]
    def local(self):
        after=self.level(self.n)[3]
        return pltpu.make_async_copy(region(self.acc,self.offset(1,self.n-1),after),
                                     region(self.out,self.piece(self.n-1),after),self.ls.at[0])
    def remote(self, s):
        bit,d,before,after=self.level(s)
        if s==0:
            src,dst=region(self.src,self.given(0,[self.j.local,0]),after),self.recv[0]
        elif s<self.n:
            off=self.offset(1,s-1)
            src,dst=region(self.acc,off if d is None else self.given(s,off),after),self.recv[s]
        else:
            dst=region(self.out,self.piece(2*self.n-1-s),after)
            first=all(self.level(i)[1] is None for i in range(self.n,s))
            src=region(self.acc,self.offset(1,self.n-1),after) if first else dst
        return pltpu.make_async_remote_copy(src_ref=src,dst_ref=dst,send_sem=self.ss.at[self.slot(s)],recv_sem=self.rs.at[s],
                                            device_id=self.at.partner[bit],device_id_type=MESH)
    def start(self, s):
        bit,d,before,after=self.level(s)
        if s==self.n: self.local().start()
        if s>=self.n and d is None: return
        if s==self.store_at: self.local().wait()
        if s==0 and self.take: pl.semaphore_wait(self.credit,1)
        self.remote(s).start()
    def finish(self, s):
        bit,d,before,after=self.level(s)
        if s>=self.n:
            if d is not None: self.remote(s).wait_recv()
        else:
            if d is None: self.remote(s).wait()
            else: self.remote(s).wait_recv()
            to=region(self.acc,self.offset(1,s),after)
            own=region(self.src,[self.j.local+self.offset(0,0)[0],0],after) if s==0 else to
            add_rows(to,own,self.recv[s],after)
            if s==0 and self.give:
                pl.semaphore_signal(self.credit,inc=1,device_id=self.at.partner[bit],device_id_type=MESH)
        if s+1<2*self.n: self.start(s+1)
        else: self.close()
    def sent(self):
        self.remote(0).wait_send()
    def close(self):
        if self.store_at==2*self.n: self.local().wait()
        if not self.give: self.sent()
        sent=region(self.out,(0,0),(self.out_rows,self.j.levels[0][2][1]))
        pltpu.make_async_remote_copy(src_ref=sent,dst_ref=sent,send_sem=self.ss.at[2*self.n-1],recv_sem=self.rs.at[0],
                                     device_id=self.at.partner[self.j.levels[0][0]],device_id_type=MESH).wait_send()

RING=2

def back_kernel(plan,*refs):
    (jobs,items,nchunk,nf,nhead,nblk,nrow,shares,bits,norm)=plan
    refs=list(refs)
    def take(n):
        out=refs[:n]; del refs[:n]; return out
    (wt,g,du,dm,c,at_h,db,a,w)=take(9)
    (q,k,v,do,at,lse,qu,ku,qr,kr)=take(10)
    (seg,qg,mid,x,dh,ng)=take(6)
    outs=take(5)
    (tg_o,)=take(1)
    (pool,stage,l0,dqkv,dq_s,dk_s,dv_s,kt_s,small,kc,qc,s_s,dp_s,p_s,ds_s)=take(15)
    (pool_sem,credit)=take(2)
    t,d=at_h.shape
    ob=t//nblk; tb=32
    own=nchunk-len(shares)-1
    bufs=[]
    for n in range(own+1):
        pair=[]
        for p in range(2):
            L=len(jobs[2*(n if n<own else nchunk-1)+p].levels)
            pair.append((take(1)[0],take(L-1 if n<own else L)))
        bufs.append(pair)
    place=Place(bits)
    runs=[]
    for n,j in enumerate(jobs):
        ss,rs,ls=take(3)
        if j.chunk==nchunk-1:
            acc,recv=bufs[own][j.part]
            runs.append(Run(place,j,small,outs[j.out],acc,recv,ss,rs,ls))
        else:
            acc,recv=bufs[shares.get(j.chunk,j.chunk)][j.part]
            runs.append(Run(place,j,stage.at[j.chunk%RING],outs[j.out],acc,[l0.at[2*(j.chunk%RING)+j.part]]+list(recv),ss,rs,ls,
                            credit.at[j.part],give=j.chunk+RING<nchunk-1,take=j.chunk>=RING))
    pid=pl.program_id(0)
    def col(ref,f): return ref.at[:,pl.ds(f*d,d)]
    names={"g":g,"du":du,"dm":dm,"c":c,"at":at_h,"db":db,"a":a,"w":w}
    plan_l=[]
    for f in range(nf): plan_l.append((("g",f),0 if f%2==0 else 2,1,True))
    for f in range(nf): plan_l.append((("du",f),0 if (nf+f)%2==0 else 2,3,False))
    load={i:[] for i in range(-1,2*nf+2)}
    load[-1]+= [(("dm",0),1),(("c",0),3)]
    for i,(what,s,other,_) in enumerate(plan_l):
        load[max(i-2,-1)].append((what,s))
    n0=2*nf+1
    s_at=0 if (2*nf)%2==0 else 2
    load[2*nf-2].append((("at",0),s_at))
    load[nf].append((("db",0),1))
    load[2*nf-1].append((("a",0),3))
    load[2*nf]+= [(("w",0),0),(("w",1),1),(("w",2),2)]
    def copy_of(what,s):
        name,f=what
        if name=="w": return pltpu.make_async_copy(col(w,f),pool.at[s,pl.ds(0,d),:],pool_sem.at[s])
        if name in ("g","du"): return pltpu.make_async_copy(col(names[name],f),pool.at[s],pool_sem.at[s])
        return pltpu.make_async_copy(names[name],pool.at[s],pool_sem.at[s])
    waiting={}
    def fetch_after(i):
        for what,s in load.get(i,[]):
            copy_of(what,s).start(); waiting[s]=what
    def ready(s):
        if s in waiting: copy_of(waiting.pop(s),s).wait()
    total=wt[0]
    for n in range(1,wt.shape[0]): total=total+wt[n]
    scale=wt[lax.axis_index("bucket")].astype(F32)/(total.astype(F32)*norm)
    products=[(s,other) if first else (other,s) for what,s,other,first in plan_l]+[(s_at,1)]
    n_h=1; n_x=n_h+nhead; n_r=n_x; n_end=n_r+nrow

    def weight_step(chunk,lhs,rhs,gate=None):
        if chunk>=RING:
            for p in range(2): runs[2*(chunk-RING)+p].sent()
        stage[chunk%RING]=scale*mm(lhs,rhs,0,0)
        if gate is not None: gate()
        for p in range(2): runs[2*chunk+p].start(0)

    segments=[[]]
    for it in items:
        if it[0]=="step": segments.append([])
        else: segments[-1].append(it)
    def before(i):
        for it in segments[i]: runs[it[1]].finish(it[2])
    heads=n0+nhead*nblk
    inner={h: [n0+h*nblk+ib for ib in range(nblk)] for h in range(nhead)}
    @pl.when(pid==0)
    def _():
        sem=pltpu.get_barrier_semaphore()
        for bit in bits:
            pl.semaphore_signal(sem,inc=1,device_id=place.partner[bit],device_id_type=MESH)
        fetch_after(-1)
        kc[...],qc[...]=segment_codes(column(seg[...].astype(F32),2*HD),t)
        small[...]=jnp.zeros_like(small)
        small[3:3+nf+2,:]=scale*mid[0:nf+2,:]
        small[nf+6:nf+7,:]=scale*mid[nf+2:nf+3,:]
        small[nf+8:nf+9,:]=scale*mid[nf+3:nf+4,:]
        for n,(lhs,rhs) in enumerate(products):
            before(n)
            ready(lhs); ready(rhs)
            weight_step(n,pool[lhs],pool[rhs],(lambda: pl.semaphore_wait(sem,len(bits))) if n==0 else None)
            fetch_after(n)
    for h in range(nhead):
        if segments[inner[h][0]]:
            @pl.when(pid==n_h+h)
            def _(h=h): before(inner[h][0])
    @pl.when(pid==n_r)
    def _():
        for s in range(4): ready(s)
        for n in range(3):
            before(heads+n)
            weight_step(n0+n,pool[3],dqkv[:,n*d:(n+1)*d])
        before(heads+3)
    for r in range(1,nrow):
        if segments[heads+3+r]:
            @pl.when(pid==n_r+r)
            def _(r=r): before(heads+3+r)
    @pl.when((pid>=n_h)&(pid<n_x))
    def _():
        hp=pid-n_h
        lanes=pl.ds(pl.multiple_of(hp*2*HD,2*HD),2*HD)
        kt_s[...]=k[...].T
        lane=lax.broadcasted_iota(jnp.int32,(1,2*HD),1)//HD
        half=lax.broadcasted_iota(jnp.int32,(8,2*HD),1)//HD
        pick=jnp.where(half==lax.broadcasted_iota(jnp.int32,(8,2*HD),0),1.0,0.0).astype(BF)
        for ib in range(nblk):
            for h in range(nhead):
                if ib>0 and segments[inner[h][ib]]:
                    @pl.when(hp==h)
                    def _(h=h):
                        before(inner[h][ib])
            rows=slice(ib*ob,(ib+1)*ob)
            dd=do[rows,:].astype(F32)*at[rows,:].astype(F32)
            hi=dd.astype(BF); rest=dd-hi.astype(F32); mid_=rest.astype(BF); low=(rest-mid_.astype(F32)).astype(BF)
            delta=mm(pick,hi,1,1)+(mm(pick,mid_,1,1)+mm(pick,low,1,1))
            dqs=[]
            for h in range(2):
                s_s[h]=mm(jnp.where(lane==h,k[...],kc[...]),jnp.where(lane==h,q[rows,:],qc[rows,:]),1,1)
                dp_s[h]=mm(v[...],jnp.where(lane==h,do[rows,:],0),1,1)
            for h in range(2):
                top,dl=lse[0,h:h+1,rows],delta[h:h+1,:]
                for n in range(t//tb):
                    at_n=slice(n*tb,(n+1)*tb)
                    p=jnp.exp(s_s[h,at_n,:]-top)
                    p_s[h,at_n,:]=p.astype(BF)
                    ds_s[h,at_n,:]=(p*(dp_s[h,at_n,:]-dl)).astype(BF)
                dvp=mm(p_s[h],jnp.where(lane==h,do[rows,:],0))
                dkp=mm(ds_s[h],jnp.where(lane==h,q[rows,:],0))
                if ib==0 and h==0: dv_s[...]=dvp; dk_s[...]=dkp
                else: dv_s[...]+=dvp; dk_s[...]+=dkp
                dqs.append(mm(kt_s[h*HD:(h+1)*HD,:],ds_s[h]))
            dq_s[rows,:]=jnp.concatenate(dqs,axis=0).T*(1.0/math.sqrt(HD))
        m=avg_matrix()[:2*HD,:2*HD]
        def avg(y):
            yh=y.astype(BF)
            return mm(yh,m)+mm((y-yh.astype(F32)).astype(BF),m)
        gains=per_head(qg,2)
        for n,(gr,un,rr) in enumerate(((dq_s,qu,qr),(dk_s,ku,kr))):
            gg=gr[...]; u=un[...].astype(F32)
            e=gg*gains[n:n+1,:]
            back=(rr[...]*(e-avg(e)-u*avg(e*u))).astype(BF)
            dqkv[:,pl.ds(pl.multiple_of(n*d+hp*2*HD,2*HD),2*HD)]=back
            small[n:n+1,lanes]=scale*jnp.sum(back.astype(F32),axis=0,keepdims=True)
            small[nf+9+n:nf+10+n,lanes]=scale*jnp.sum(gg*u,axis=0,keepdims=True)
            small[nf+11+n:nf+12+n,lanes]=scale*jnp.sum(gg,axis=0,keepdims=True)
        back=dv_s[...].astype(BF)
        dqkv[:,pl.ds(pl.multiple_of(2*d+hp*2*HD,2*HD),2*HD)]=back
        small[2:3,lanes]=scale*jnp.sum(back.astype(F32),axis=0,keepdims=True)
    @pl.when((pid>=n_r)&(pid<n_end))
    def _():
        rb=x.shape[0]
        rows=pl.ds(pl.multiple_of((pid-n_r)*rb,rb),rb)
        da=mm(dqkv[rows,0:d],pool[0,:d,:],1,1)+mm(dqkv[rows,d:2*d],pool[1,:d,:],1,1)+mm(dqkv[rows,2*d:],pool[2,:d,:],1,1)
        unit,r=row_norm(x[...].astype(F32))
        e=da*ng[0:1,:]
        tg_o[...]=dh[...]+r*(e-jnp.mean(e,axis=-1,keepdims=True)-unit*jnp.mean(e*unit,axis=-1,keepdims=True))
        small[nf+5:nf+6,:]+=scale*jnp.sum(da*unit,axis=0,keepdims=True)
        small[nf+7:nf+8,:]+=scale*jnp.sum(da,axis=0,keepdims=True)
    @pl.when(pid==n_end-1)
    def _():
        for p in range(2): runs[2*(nchunk-1)+p].start(0)
        before(heads+3+nrow)

def backward(wt,g,du,dm,c,at,db,a,w,q,k,v,do,lse,qu,ku,qr,kr,seg,qg,mid,x,dh,ng,nb,nd,ob=256,rb=256):
    t,d=x.shape; ff=g.shape[1]; nf=ff//d
    nhead=d//(2*HD); nblk=t//ob; nrow=t//rb
    n0=2*nf+1
    chunks=[(0,f*d,0,d,d) for f in range(nf)]+[(1,0,f*d,d,d) for f in range(nf)]+[(2,0,0,d,d)]
    chunks+=[(3,0,n*d,d,d) for n in range(3)]+[(4,0,0,32,d)]
    nchunk=len(chunks)
    shares={} if (nb,nd)==(4,8) else {n0+n:n for n in range(3)}
    jobs=make_jobs(chunks,nb,nd)
    steps=[(n,2.2) for n in range(n0)]+[(None,2.1)]*(nhead*nblk)+[(n0+n,2.2) for n in range(3)]+[(None,2.6)]*(nrow-1)+[(nchunk-1,2.6)]
    items,_=schedule(jobs,steps,RING,shares)
    bits=bits_of(nb,nd)
    n_h=1; n_r=n_h+nhead; n_end=n_r+nrow
    def head(i): return jnp.clip(i-n_h,0,nhead-1)
    def block(i): return jnp.clip(i-n_r,0,nrow-1)
    any_=pl.BlockSpec(memory_space=pltpu.HBM)
    colspec=pl.BlockSpec((t,2*HD),lambda i:(0,head(i)))
    rows=pl.BlockSpec((rb,d),lambda i:(block(i),0))
    in_specs=[pl.BlockSpec(memory_space=pltpu.SMEM)]+[any_]*8+[colspec]*5+[pl.BlockSpec((1,2,t),lambda i:(head(i),0,0))]+[colspec]*4
    in_specs+=[whole(seg),whole(qg),whole(mid),rows,rows,whole(ng)]
    out_specs=[any_]*5+[rows]
    S=jax.ShapeDtypeStruct
    out_shape=[S((ff,d),F32),S((d,ff),F32),S((d,d),F32),S((d,3*d),F32),S((32,d),F32),S((t,d),F32)]
    half=(d//2)//2
    scratch=[pltpu.VMEM((4,t,d),BF),pltpu.VMEM((RING,d,d),F32),pltpu.VMEM((2*RING,half,d),F32),pltpu.VMEM((t,3*d),BF)]
    scratch+=[pltpu.VMEM((t,2*HD),F32)]*3+[pltpu.VMEM((2*HD,t),BF),pltpu.VMEM((32,d),F32),pltpu.VMEM((t,2*HD),BF),pltpu.VMEM((t,2*HD),BF),pltpu.VMEM((2,t,ob),F32),pltpu.VMEM((2,t,ob),F32),pltpu.VMEM((2,t,ob),BF),pltpu.VMEM((2,t,ob),BF),pltpu.SemaphoreType.DMA((4,)),pltpu.SemaphoreType.REGULAR((2,))]
    own=nchunk-len(shares)-1
    for n in range(own+1):
        small=n==own
        for p in range(2):
            j=jobs[2*(nchunk-1 if small else n)+p]
            scratch.append(pltpu.VMEM(j.levels[0][3],F32))
            for lv in j.levels[0 if small else 1:]: scratch.append(pltpu.VMEM(lv[3],F32))
    for j in jobs:
        L=len(j.levels)
        scratch+=[pltpu.SemaphoreType.DMA((2*L,)),pltpu.SemaphoreType.DMA((2*L,)),pltpu.SemaphoreType.DMA((1,))]
    plan=(jobs,items,nchunk,nf,nhead,nblk,nrow,shares,bits,math.sqrt(t*nd))
    return pl.pallas_call(functools.partial(back_kernel,plan),grid=(n_end,),in_specs=in_specs,out_specs=out_specs,out_shape=out_shape,
        scratch_shapes=scratch,
        compiler_params=pltpu.CompilerParams(collective_id=7,has_side_effects=True,vmem_limit_bytes=63<<20),name="backward")(
        wt,g,du,dm,c,at,db,a,w,q,k,v,do,at,lse,qu,ku,qr,kr,seg,qg,mid,x,dh,ng)

def finish_kernel(nf,f2,f1,fo,fq,tg,small,f2_o,f1_o,fo_o,fq_o,tg_o,bq_o,bo_o,b1_o,b2_o,gain_o,shift_o,hg_o,hs_o):
    for src,dst in ((f2,f2_o),(f1,f1_o),(fo,fo_o),(fq,fq_o),(tg,tg_o)): dst[...]=src[...]
    d=small.shape[1]
    @pl.when(pl.program_id(0)==0)
    def _():
        for i in range(3): bq_o[i*d:(i+1)*d]=small[i,:]
        bo_o[...]=small[3,:]
        for i in range(nf): b1_o[i*d:(i+1)*d]=small[4+i,:]
        b2_o[...]=small[4+nf,:]
        gain_o[...]=small[5+nf:7+nf,:]
        shift_o[...]=small[7+nf:9+nf,:]
        for n,o in enumerate((hg_o,hs_o)):
            wide=small[9+nf+2*n:11+nf+2*n,:]
            pair=wide[:,:2*HD]
            for i in range(1,d//(2*HD)): pair=pair+wide[:,2*HD*i:2*HD*(i+1)]
            o[...]=pair[:,:HD]+pair[:,HD:]

def finish(f2,f1,fo,fq,tg,small,n=4):
    ff,d=f2.shape; nf=ff//d
    S=jax.ShapeDtypeStruct
    wide=[pl.BlockSpec((a.shape[0]//n,a.shape[1]),lambda i:(i,0)) for a in (f2,f1,fo,fq,tg)]
    big=[S(a.shape,F32) for a in (f2,f1,fo,fq,tg)]
    rest=[S((3*d,),F32),S((d,),F32),S((ff,),F32),S((d,),F32),S((2,d),F32),S((2,d),F32),S((2,HD),F32),S((2,HD),F32)]
    return pl.pallas_call(functools.partial(finish_kernel,nf),grid=(n,),
        in_specs=wide+[whole(small)],
        out_specs=wide+[whole(a) for a in rest],
        out_shape=big+rest,compiler_params=pltpu.CompilerParams(vmem_limit_bytes=VM),name="finish")(f2,f1,fo,fq,tg,small)


def body(
    tokens,
    segment,
    live,
    group_patches,
    qkv_weight,
    qkv_bias,
    out_weight,
    out_bias,
    fc1_weight,
    fc1_bias,
    fc2_weight,
    fc2_bias,
    norm_gain,
    norm_shift,
    qk_gain,
    qk_shift,
    cotangent,
):
    a_low, q_low, k_low, v_low, q_unit, k_unit, q_inv, k_inv = qkv_forward(
        tokens, qkv_weight, qkv_bias, norm_gain, norm_shift, qk_gain, qk_shift
    )
    attn_low, lse = attend_forward(q_low, k_low, v_low, segment)
    out, dhid, dattn, g_low, du_low, dm_low, c_low, db_low, mid_sums = mlp(
        tokens,
        cotangent,
        live[None],
        attn_low,
        out_weight,
        out_bias,
        fc1_weight,
        fc1_bias,
        fc2_weight,
        fc2_bias,
        norm_gain,
        norm_shift,
    )
    fc2_grad, fc1_grad, out_grad, qkv_grad, small, tokens_grad = backward(
        group_patches, g_low, du_low, dm_low, c_low, attn_low, db_low, a_low, qkv_weight,
        q_low, k_low, v_low, dattn, lse, q_unit, k_unit, q_inv, k_inv,
        segment[None], qk_gain, mid_sums, tokens, dhid, norm_gain,
        lax.axis_size("bucket"), lax.axis_size("dp"),
    )
    (fc2_grad, fc1_grad, out_grad, qkv_grad, tokens_grad, qkv_b, out_b, fc1_b, fc2_b, n_gain, n_shift, h_gain, h_shift) = finish(
        fc2_grad, fc1_grad, out_grad, qkv_grad, tokens_grad, small
    )
    return (
        out, tokens_grad, qkv_grad, qkv_b, out_grad, out_b, fc1_grad, fc1_b, fc2_grad, fc2_b,
        n_gain, n_shift, h_gain, h_shift,
    )


def solution(mesh):
    return jax.shard_map(
        body,
        mesh=mesh,
        in_specs=(
            P(("bucket", "dp"), None),
            P(("bucket", "dp")),
            P(("bucket", "dp")),
            *((P(),) * 13),
            P(("bucket", "dp"), None),
        ),
        out_specs=(P(("bucket", "dp"), None), P(("bucket", "dp"), None), *((P(),) * 12)),
        check_vma=False,
    )
```
